128 devices in a mesh: gx: 4 (over x), gy: 4 (over z_lo, core), gz: 8 (over z_hi, y).
Axes of the slice: x: 4, y: 4, z: 4 (z_hi: 2, z_lo: 2; z = z_hi * 2 + z_lo), core: 2. Of those that a mesh axis runs over, the one named last changes fastest.
Arguments:
- orbitals: float32 [16, 32, 64, 512], P(None, 'gz', 'gy', 'gx'), may hold values from -6 to 6
- potential: float32 [32, 64, 512], P('gz', 'gy', 'gx'), may hold values from -1 to 0.5
- tile_proj: float32 [32768, 4, 128], P(('gx', 'gy', 'gz')), may hold values from -1 to 1
- tile_atom: int32 [32768], P(('gx', 'gy', 'gz')), may hold values from 0 to 8191, as said below
- tile_column: int32 [32768], P(('gx', 'gy', 'gz')), may hold values from 0 to 63
- tile_count: int32 [128], P(('gx', 'gy', 'gz')), may hold values from 64 to 256, as said below
- atom_home: int32 [8192], replicated, may hold values from 0 to 8191, each once
- coupling: float32 [8192, 4], P(('gx', 'gy', 'gz')), may hold values from 0.5 to 3
Outputs:
- filtered: float32 [16, 32, 64, 512], P(None, 'gz', 'gy', 'gx')
The draws below stay inside these ranges and needn't reach their ends.
Inputs may be any that keep to these rules, and one draw needn't show every extreme that they name: `tile_atom`: each live or dead slot names an atom numbered d * 64 to d * 64 + 63 for a device d whose gx, gy and gz indices each differ from the slot's own device's by at most one. `tile_count`: some device has all 256 slots live. `atom_home`: each coupling row once.
All inputs are finite; a program needn't handle non-finite values.
Results may differ from the reference program's by a relative error of at most 0.00018.
Values sent between devices are 32-bit elements; how exact they have to be, the bound alone decides.
A program may use at most 128 MiB of HBM per device.

```python
import math
import jax
import jax.numpy as jnp
from jax import lax

NORB = 16
NPROJ = 4
DEGREE = 4
CX = 128
CY = 16
CZ = 4
TILES_DEV = 256
ATOM_DEV = 64
NX = 512
NY = 64
NZ = 32
ATOMS = 8192
N_GX = 4
N_GY = 4
N_GZ = 8
DEVICES = 128


def draw_tile_atom(key, part):
    tile_total = DEVICES * TILES_DEV
    subkeys = jax.random.split(key, 4)
    device = jnp.arange(tile_total, dtype=jnp.int32) // TILES_DEV
    home_x = device // (N_GY * N_GZ)
    home_y = device // N_GZ % N_GY
    home_z = device % N_GZ
    near_x = jnp.clip(home_x + jax.random.randint(subkeys[0], (tile_total,), -1, 2), 0, N_GX - 1)
    near_y = jnp.clip(home_y + jax.random.randint(subkeys[1], (tile_total,), -1, 2), 0, N_GY - 1)
    near_z = jnp.clip(home_z + jax.random.randint(subkeys[2], (tile_total,), -1, 2), 0, N_GZ - 1)
    neighbour = (near_x * N_GY + near_y) * N_GZ + near_z
    within = jax.random.randint(subkeys[3], (tile_total,), 0, ATOM_DEV)
    return (neighbour * ATOM_DEV + within).astype(jnp.int32)


def draw_tile_count(key, part):
    counts = jax.random.randint(key, (DEVICES,), TILES_DEV // 4, TILES_DEV + 1)
    return counts.at[0].set(TILES_DEV).astype(jnp.int32)


def touch_ends(entries, own_key, low, top_value):
    index_at = [jax.random.randint(jax.random.fold_in(own_key, axis), (), 0, length) for axis, length in enumerate(entries.shape)]
    main_axis = entries.shape.index(max(entries.shape))
    beside = index_at[:main_axis] + [(index_at[main_axis] + 1) % entries.shape[main_axis]] + index_at[main_axis + 1:]
    return entries.at[tuple(index_at)].set(low).at[tuple(beside)].set(top_value)


def block_levels(rng, extent, pieces, low, top_value):
    def one(dim, shards_of):
        draws = jax.random.uniform(jax.random.fold_in(jax.random.fold_in(rng, 6), dim), (shards_of,), jnp.float32, low / len(pieces), top_value / len(pieces))
        return jnp.repeat(jnp.exp(draws), extent[dim] // shards_of).reshape((-1,) + (1,) * (len(extent) - dim - 1))

    factor_of = one(*pieces[0])
    for cut in pieces[1:]:
        factor_of = factor_of * one(*cut)
    return factor_of


def centred(rng, extent, deviation, reach, cuts=(), kind=jnp.bfloat16):
    array = jax.random.normal(rng, extent, jnp.float32) * deviation
    if len(cuts) > 0:
        array = block_levels(rng, extent, cuts, -0.22, 0.18) * array
    return jnp.clip(array, min=-reach, max=reach).astype(kind)


def setup_inputs(seed: int = 0) -> dict:
    streams_of = jax.random.split(jax.random.key(seed), 9)
    orbitals = centred(streams_of[0], (NORB, NZ, NY, NX), 1.0, 6.0, ((1, 8), (2, 4), (3, 4)), jnp.float32)
    potential = jnp.clip(-1.0 + 1.5 * jax.random.uniform(streams_of[1], (NZ, NY, NX), jnp.float32) ** block_levels(streams_of[1], (NZ, NY, NX), ((0, 8), (1, 4), (2, 4)), -0.2, 0.2), -1.0, 0.5)
    tile_proj = centred(streams_of[2], (DEVICES * TILES_DEV, NPROJ, CX), ((CX * TILES_DEV // ATOM_DEV // 3) ** -0.5), 1.0, ((0, 128),), jnp.float32)
    tile_atom = draw_tile_atom(jax.random.fold_in(streams_of[8], 71), 0)
    tile_column = touch_ends(jax.random.randint(streams_of[4], (DEVICES * TILES_DEV,), 0, CZ * CY), jax.random.fold_in(streams_of[4], 1), 0, (CZ * CY) - 1).astype(jnp.int32)
    tile_count = draw_tile_count(jax.random.fold_in(streams_of[8], 71), 0)
    atom_home = jax.random.permutation(streams_of[6], ATOMS).astype(jnp.int32)
    coupling = jnp.clip(jnp.exp(math.log(3.0) - 1.7917595 * jax.random.uniform(streams_of[7], (ATOMS, NPROJ), jnp.float32) ** block_levels(streams_of[7], (ATOMS, NPROJ), ((0, 128),), -0.2, 0.2)), 0.5, 3.0)
    return {"orbitals": orbitals, "potential": potential, "tile_proj": tile_proj, "tile_atom": tile_atom, "tile_column": tile_column, "tile_count": tile_count, "atom_home": atom_home, "coupling": coupling}


stencil_weights = (-205.0 / 72.0, 8.0 / 5.0, -1.0 / 5.0, 8.0 / 315.0, -1.0 / 560.0)
lower_edge = 4.0
upper_edge = 24.0


def laplacian(values):
    result = 3.0 * stencil_weights[0] * values
    for dimension in range(3):
        widths = tuple((4, 4) if position == dimension else (0, 0) for position in range(3))
        padded = jnp.pad(values, widths)
        length = values.shape[dimension]
        for offset in range(1, 5):
            upper = lax.slice_in_dim(padded, 4 + offset, 4 + offset + length, axis=dimension)
            lower = lax.slice_in_dim(padded, 4 - offset, 4 - offset + length, axis=dimension)
            result = result + stencil_weights[offset] * (upper + lower)
    return result


def reference(orbitals, potential, tile_proj, tile_atom, tile_column, tile_count, atom_home, coupling):
    tile_total = tile_atom.shape[0]
    slots = jnp.arange(tile_total, dtype=jnp.int32)
    device = slots // TILES_DEV
    live = ((slots % TILES_DEV) < tile_count[device]).astype(tile_proj.dtype)
    proj_live = tile_proj * live[:, None, None]
    grid_x = device // (N_GY * N_GZ)
    grid_y = (device // N_GZ) % N_GY
    grid_z = device % N_GZ
    local_z = tile_column // CY
    local_y = tile_column % CY
    plane = ((grid_z * CZ + local_z) * NY + grid_y * CY + local_y).astype(jnp.int32)
    atom_scale = coupling[atom_home]
    center = 0.5 * (upper_edge + lower_edge)
    half_width = 0.5 * (upper_edge - lower_edge)

    def hamiltonian(values):
        lines = values.reshape(NZ * NY, N_GX, CX)
        tile_rows = lines[plane, grid_x]
        partial_value = jnp.einsum('tpx,tx->tp', proj_live, tile_rows, precision=lax.Precision.HIGHEST)
        coefficient = jax.ops.segment_sum(partial_value, tile_atom, num_segments=ATOMS)
        scaled = coefficient * atom_scale
        returned = jnp.einsum('tpx,tp->tx', proj_live, scaled[tile_atom], precision=lax.Precision.HIGHEST)
        projected = jnp.zeros_like(lines).at[plane, grid_x].add(returned).reshape(values.shape)
        return -0.5 * laplacian(values) + potential * values + projected

    def one_orbital(values):
        previous = values
        current = (hamiltonian(values) - center * values) / half_width
        for repeat in range(DEGREE - 1):
            following = 2.0 * (hamiltonian(current) - center * current) / half_width - previous
            previous = current
            current = following
        return current

    return lax.map(one_orbital, orbitals)
```

```python
import jax
import jax.numpy as jnp
import numpy as np
from jax import lax
from jax.experimental import pallas as pl
from jax.experimental.pallas import tpu as pltpu
from jax.sharding import PartitionSpec as P

F32, BF16, I32 = jnp.float32, jnp.bfloat16, jnp.int32
STENCIL = (-205.0 / 72.0, 8.0 / 5.0, -1.0 / 5.0, 8.0 / 315.0, -1.0 / 560.0)
CENTER, HALF = 14.0, 10.0
STEPS = 4
DIRS = [(dx, dy) for dx in (-1, 0, 1) for dy in (-1, 0, 1)]
SELF = 4
XP, XM, YL, YH, ZH, RS0, RO0, BS0, BO0, NSEM = 0, 1, 2, 3, 4, 5, 14, 23, 32, 41
V0, PF0, PT0, ME0, CP0, OU0, NSET = 0, 3, 9, 12, 15, 25, 28


def stencil_constants():
    table = np.zeros((144, 128), np.float32)
    for x in range(128):
        for k in range(1, 5):
            if x + k < 128:
                table[x, x + k] = -0.5 * STENCIL[k]
            if x - k >= 0:
                table[x, x - k] = -0.5 * STENCIL[k]
    for j in range(4):
        table[128 + j, 124 + j] = 1.0
        table[132 + j, j] = 1.0
        for x in range(128):
            k = x + 4 - j
            if 1 <= k <= 4:
                table[136 + j, x] = -0.5 * STENCIL[k]
            k = 128 + j - x
            if 1 <= k <= 4:
                table[140 + j, x] = -0.5 * STENCIL[k]
    return table


def split(value):
    high = value.astype(BF16)
    return high, (value - high.astype(F32)).astype(BF16)


def dot_nt(a, b):
    return lax.dot_general(a, b, (((1,), (1,)), ((), ())), preferred_element_type=F32)


def dot_nn(a, b):
    return lax.dot_general(a, b, (((1,), (0,)), ((), ())), preferred_element_type=F32)


def dot_tn(a, b):
    return lax.dot_general(a, b, (((0,), (0,)), ((), ())), preferred_element_type=F32)


def kernel(
    orb, pot_in, tp, meta_in, cpl_in, table, out,
    X, Z, VH, VL, PF, PN, POT, META, MKF, MKB, NIDX, NMB, WT, LH, LS, RS, RO, CS, SS, SC, XS, XR, CB, CONST,
    PART, set_s, set_r, sem_s, sem_r,
):
    ix, iy, iz = lax.axis_index("gx"), lax.axis_index("gy"), lax.axis_index("gz")
    zh, q = iz // 4, iz % 4
    oz = 1 - zh

    def dev(gx, gy, gz):
        return {"gx": gx, "gy": gy, "gz": gz}

    def ring(j):
        return dev(ix, iy, zh * 4 + (q + j) % 4)

    def near(dx, dy, half):
        return dev((ix + dx + 4) % 4, (iy + dy + 4) % 4, half * 4 + q)

    def copy(src, dst, s, r, to):
        return pltpu.make_async_remote_copy(
            src_ref=src, dst_ref=dst, send_sem=s, recv_sem=r, device_id=to, device_id_type=pl.DeviceIdType.MESH
        )

    def clear(i, _):
        X[i, :, 0:4] = jnp.zeros((4, 4, 32, 128), F32)
        X[i, :, 20:24] = jnp.zeros((4, 4, 32, 128), F32)
        X[i, :, 4:20, 0:8] = jnp.zeros((4, 16, 8, 128), F32)
        X[i, :, 4:20, 24:32] = jnp.zeros((4, 16, 8, 128), F32)
        return 0

    lax.fori_loop(1, 5, clear, 0)
    X[0, :, 4:20, 8:24] = jnp.zeros((4, 16, 16, 128), F32)

    barrier = pltpu.get_barrier_semaphore()
    peers = [near(dx, dy, half) for dx, dy in DIRS for half in (zh, oz)]
    peers = [p for i, p in enumerate(peers) if i != 2 * SELF]
    peers += [ring(j) for j in (1, 2, 3)]
    peers += [dev((ix + 2) % 4, iy, iz), dev(ix, (iy + 2) % 4, iz)]
    for peer in peers:
        pl.semaphore_signal(barrier, inc=1, device_id=peer, device_id_type=pl.DeviceIdType.MESH)
    pl.semaphore_wait(barrier, len(peers))

    def field_block(index, block):
        return X.at[index, :, pl.ds(4 + 4 * block, 4), pl.ds(8, 16), :]

    sends = []

    def start(c):
        c.start()
        sends.append(c)
        return c

    def set_copy(src, dst, index, to):
        return copy(src, dst, set_s.at[index], set_r.at[index], to)

    values = []
    for j in (1, 3, 2):
        values.append(
            start(set_copy(orb.at[pl.ds(4 * ((q + j) % 4), 4)], field_block(1, q), V0 + j - 1, ring(j)))
        )
    metas = [start(set_copy(meta_in, META.at[q], ME0 + j - 1, ring(j))) for j in (1, 3, 2)]

    def rows(first, count):
        return CB.at[pl.ds(first, count)]

    CB[pl.ds(2 * ((ix * 4 + iy) * 8 + iz), 2), :] = cpl_in[...]
    mine = 2 * ((ix * 4 + iy) * 8 + iz)
    ring_cpl = [start(set_copy(cpl_in, rows(mine, 2), CP0 + j - 1, ring(j))) for j in (1, 3, 2)]
    up = [start(set_copy(tp.at[pl.ds(2 * h, 2)], PF.at[q, pl.ds(2 * h, 2)], PF0 + h, ring(1))) for h in (0, 1)]
    down = [start(set_copy(tp.at[pl.ds(2 * h, 2)], PF.at[q, pl.ds(2 * h, 2)], PF0 + 3 - h, ring(3))) for h in (1, 0)]
    pots = [start(set_copy(pot_in, POT.at[pl.ds(4 * q, 4)], PT0 + j - 1, ring(j))) for j in (1, 3, 2)]

    X[1, :, pl.ds(4 + 4 * q, 4), 8:24, :] = orb[pl.ds(4 * q, 4)]
    PF[pl.ds(q, 1)] = tp[...][None]
    POT[pl.ds(4 * q, 4)] = pot_in[...]
    META[pl.ds(q, 1)] = meta_in[...][None]

    wx_h, wx_l = split(table[0:128, :])
    CONST[0:128, 0:128] = wx_h
    CONST[0:128, 128:256] = wx_l
    e2 = table[128:136, :].astype(BF16)
    edge_row = lax.broadcasted_iota(I32, (8, 128), 0)
    inside = jnp.where(
        edge_row < 4, jnp.where(ix > 0, 1.0, 0.0).astype(F32), jnp.where(ix < 3, 1.0, 0.0).astype(F32)
    )
    edge = table[136:144, :] * inside
    edge_h = edge.astype(BF16).astype(F32)
    edge_1 = jnp.concatenate([edge_h, edge_h], axis=0).astype(BF16)
    edge_2 = jnp.concatenate([edge - edge_h, edge - edge_h], axis=0).astype(BF16)

    for c in metas:
        c.wait_recv()
    row64 = lax.broadcasted_iota(I32, (64, 256), 0)
    row128 = lax.broadcasted_iota(I32, (128, 256), 0)
    for b in range(4):
        index = META[b]
        mask = jnp.where(row64 == index[2:3, :], 1.0, 0.0).astype(F32)
        MKF[b] = mask
        MKB[b] = mask.astype(BF16)
        hot = jnp.where(row128 == index[1:2, :], 1.0, 0.0).astype(BF16)
        WT[b, 0:128] = hot
        WT[b, 128:256] = hot
        number = jnp.broadcast_to(index[0:1, :], (16, 256))
        NIDX[b] = number
        for n in range(27):
            NMB[n, :, b * 256 : (b + 1) * 256] = jnp.where(number == n, 1.0, 0.0).astype(BF16)

    for c in ring_cpl:
        c.wait_recv()
    group = 2 * ((ix * 4 + iy) * 8 + zh * 4)
    flip = start(set_copy(rows(group, 8), rows(group, 8), CP0 + 3, dev(ix, iy, oz * 4 + q)))
    flip.wait_recv()
    group = 2 * ((ix * 4 + iy) * 8)
    cpl_y = [
        start(set_copy(rows(group, 16), rows(group, 16), CP0 + 3 + j, dev(ix, (iy + j) % 4, iz))) for j in (1, 3, 2)
    ]
    for c in cpl_y:
        c.wait_recv()
    group = 2 * (ix * 32)
    cpl_x = [
        start(set_copy(rows(group, 64), rows(group, 64), CP0 + 6 + j, dev((ix + j) % 4, iy, iz))) for j in (1, 3, 2)
    ]
    for c in cpl_x:
        c.wait_recv()
    home = meta_in[3:4, :]
    home_row = 2 * lax.shift_right_logical(home, 6)
    home_lane = jnp.bitwise_and(home, 63)
    rows256 = lax.broadcasted_iota(I32, (256, 256), 0)
    lane_hot = jnp.where(lax.broadcasted_iota(I32, (64, 256), 0) == home_lane, 1.0, 0.0).astype(F32)
    cb = CB[...]
    cb_1 = cb.astype(BF16)
    rest = cb - cb_1.astype(F32)
    cb_2 = rest.astype(BF16)
    cb_3 = (rest - cb_2.astype(F32)).astype(BF16)
    for r in range(2):
        pick = jnp.where(rows256 == home_row + r, 1.0, 0.0).astype(BF16)
        found = dot_tn(cb_1, pick) + dot_tn(cb_2, pick) + dot_tn(cb_3, pick)
        for p2 in range(2):
            line = jnp.sum(found[p2 * 64 : (p2 + 1) * 64] * lane_hot, axis=0, keepdims=True)
            p = 2 * r + p2
            for pair in range(2):
                SC[pair, p * 4 : (p + 1) * 4, :] = jnp.broadcast_to(line[:, pair * 128 : (pair + 1) * 128], (4, 128))

    for c in values:
        c.wait_recv()
    v = X[1, :, 4:20, 8:24, :]
    high, low = split(v)
    VH[...] = high
    VL[...] = low

    up[0].wait_recv()
    below = (q + 3) % 4
    above = (q + 1) % 4
    on_up = start(set_copy(PF.at[below, pl.ds(0, 2)], PF.at[below, pl.ds(0, 2)], PF0 + 4, ring(1)))
    down[0].wait_recv()
    on_down = start(set_copy(PF.at[above, pl.ds(2, 2)], PF.at[above, pl.ds(2, 2)], PF0 + 5, ring(3)))
    for c in pots:
        c.wait_recv()
    up[1].wait_recv()
    down[1].wait_recv()
    on_up.wait_recv()
    on_down.wait_recv()

    def split_proj(b, _):
        ph, pl_ = split(PF[b].reshape(1024, 128))
        PN[b, :, 0:128] = ph
        PN[b, :, 128:256] = pl_
        return 0

    lax.fori_loop(0, 4, split_proj, 0)

    def step_copies(s):
        cur = s + 1

        def sc(src, dst, index, to):
            return copy(src, dst, sem_s.at[s, index], sem_r.at[s, index], to)

        c = {}
        c["xp"] = sc(XS.at[s, pl.ds(0, 4)], XR.at[s, pl.ds(0, 4)], XP, dev((ix + 1) % 4, iy, iz))
        c["xm"] = sc(XS.at[s, pl.ds(4, 4)], XR.at[s, pl.ds(4, 4)], XM, dev((ix + 3) % 4, iy, iz))
        inner = pl.ds(4, 16)
        c["yl"] = sc(
            X.at[cur, :, inner, pl.ds(8, 4), :], X.at[cur, :, inner, pl.ds(24, 4), :], YL, dev(ix, (iy + 3) % 4, iz)
        )
        c["yh"] = sc(
            X.at[cur, :, inner, pl.ds(20, 4), :], X.at[cur, :, inner, pl.ds(4, 4), :], YH, dev(ix, (iy + 1) % 4, iz)
        )
        c["z"] = sc(
            X.at[cur, :, pl.ds(4 + 12 * oz, 4), pl.ds(8, 16), :],
            X.at[cur, :, pl.ds(20 * zh, 4), pl.ds(8, 16), :],
            ZH,
            dev(ix, iy, oz * 4 + q),
        )
        for i, (dx, dy) in enumerate(DIRS):
            slot = 8 - i
            if i != SELF:
                c["rs", i] = sc(LS.at[s, pl.ds(3 * i, 2)], RS.at[s, slot], RS0 + slot, near(dx, dy, zh))
                c["bs", i] = sc(CS.at[s], SS.at[s, pl.ds(3 * slot, 2)], BS0 + slot, near(dx, dy, zh))
            c["ro", i] = sc(LS.at[s, 3 * i + 2], RO.at[s, slot], RO0 + slot, near(dx, dy, oz))
            c["bo", i] = sc(CS.at[s, oz], SS.at[s, 3 * slot + 2], BO0 + slot, near(dx, dy, oz))
        return c

    def step(s, _):
        cur = s + 1
        c = step_copies(s)
        alpha = jnp.where(s == 0, 1.0 / HALF, 2.0 / HALF).astype(F32)
        c["z"].start()

        @pl.when(iy > 0)
        def _():
            c["yl"].start()

        @pl.when(iy < 3)
        def _():
            c["yh"].start()

        vh_all = VH[...].reshape(1024, 128)
        vl_all = VL[...].reshape(1024, 128)
        XS[s] = dot_nt(e2, vh_all) + dot_nt(e2, vl_all)

        def partials(b, _):
            vh = VH[:, pl.ds(4 * b, 4)].reshape(256, 128)
            vl = VL[:, pl.ds(4 * b, 4)].reshape(256, 128)
            vhh = jnp.concatenate([vh, vh], axis=1)
            t = dot_nt(vhh, PN[b]) + dot_nt(vl, PN[b, :, 0:128])
            mask = MKF[b]
            for p in range(4):
                for o in range(4):
                    tile = t[o * 64 : (o + 1) * 64, p * 256 : (p + 1) * 256]
                    PART[b, pl.ds(p * 4 + o, 1), :] = jnp.sum(tile * mask, axis=0, keepdims=True)
            xp = dot_nt(vhh, CONST[...]) + dot_nt(vl, CONST[:, 0:128])
            Z[:, pl.ds(4 * b, 4)] = xp.reshape(4, 4, 16, 128)
            return 0

        lax.fori_loop(0, 4, partials, 0)
        c["xp"].start()
        c["xm"].start()

        for b in range(4):
            ph, pl_ = split(PART[b])
            for n in range(27):
                m = NMB[n, :, b * 256 : (b + 1) * 256]
                LH[n, 0:16, b * 256 : (b + 1) * 256] = ph * m
                LH[n, 16:32, b * 256 : (b + 1) * 256] = pl_ * m
        sums = None
        for b in range(4):
            lhs = LH[:, :, b * 256 : (b + 1) * 256].reshape(864, 256)
            term = dot_nt(lhs, WT[b, 0:128])
            sums = term if sums is None else sums + term
        sums = sums.reshape(27, 32, 128)
        LS[s] = sums[:, 0:16] + sums[:, 16:32]
        for i in range(9):
            if i != SELF:
                c["rs", i].start()
            c["ro", i].start()

        c["xp"].wait_recv()
        c["xm"].wait_recv()
        xr = XR[s]
        xr_h = xr.astype(BF16).astype(F32)
        faces = jnp.concatenate([xr_h, xr - xr_h], axis=0).astype(BF16)
        Z[...] = Z[...] + (dot_tn(faces, edge_1) + dot_tn(faces, edge_2)).reshape(4, 16, 16, 128)
        c["z"].wait_recv()

        @pl.when(iy > 0)
        def _():
            c["yh"].wait_recv()

        @pl.when(iy < 3)
        def _():
            c["yl"].wait_recv()

        def line(i, _):
            o = i // 16
            z = i % 16
            v0 = X[cur, o, z + 4, 8:24, :]
            acc = Z[o, z] + v0 * (POT[z] + (-1.5 * STENCIL[0] - CENTER))
            for k in range(1, 5):
                around = (X[cur, o, z + 4 - k, 8:24, :] + X[cur, o, z + 4 + k, 8:24, :]) + (
                    X[cur, o, z + 4, 8 - k : 24 - k, :] + X[cur, o, z + 4, 8 + k : 24 + k, :]
                )
                acc = acc + (-0.5 * STENCIL[k]) * around
            Z[o, z] = alpha * acc - X[s, o, z + 4, 8:24, :]
            return 0

        lax.fori_loop(0, 64, line, 0, unroll=4)

        total = LS[s, 3 * SELF : 3 * SELF + 2]
        for slot in range(9):
            if slot != SELF:
                c["rs", 8 - slot].wait_recv()
                total = total + RS[s, slot]
        other = None
        for slot in range(9):
            c["ro", 8 - slot].wait_recv()
            other = RO[s, slot] if other is None else other + RO[s, slot]
        at_0 = jnp.where(zh == 1, 1.0, 0.0).astype(F32)
        scaled = alpha * SC[...] * jnp.stack([total[0] + at_0 * other, total[1] + (1.0 - at_0) * other])
        CS[s] = scaled
        SS[s, 3 * SELF : 3 * SELF + 2] = scaled
        for i in range(9):
            if i != SELF:
                c["bs", i].start()
            c["bo", i].start()
        for i in range(9):
            if i != SELF:
                c["bs", i].wait_recv()
            c["bo", i].wait_recv()

        sh, sl = split(SS[s].reshape(432, 128))
        shl = jnp.concatenate([sh, sl], axis=1)

        def apply(b, _):
            r = dot_nn(shl, WT[b])
            number = NIDX[b]
            pt = jnp.zeros((16, 256), F32)
            for n in range(27):
                pt = pt + jnp.where(number == n, r[n * 16 : (n + 1) * 16], 0.0)
            pth, ptl = split(pt)
            mask = MKB[b]
            a_h = jnp.concatenate(
                [
                    jnp.concatenate([mask * pth[p * 4 + o : p * 4 + o + 1] for p in range(4)], axis=1)
                    for o in range(4)
                ],
                axis=0,
            )
            a_l = jnp.concatenate(
                [
                    jnp.concatenate([mask * ptl[p * 4 + o : p * 4 + o + 1] for p in range(4)], axis=1)
                    for o in range(4)
                ],
                axis=0,
            )
            wide = dot_nn(a_h, PN[b])
            projected = wide[:, 0:128] + wide[:, 128:256] + dot_nn(a_l, PN[b, :, 0:128])
            y = Z[:, pl.ds(4 * b, 4)] + projected.reshape(4, 4, 16, 128)
            X[cur + 1, :, pl.ds(4 + 4 * b, 4), 8:24, :] = y
            yh, yl = split(y)
            VH[:, pl.ds(4 * b, 4)] = yh
            VL[:, pl.ds(4 * b, 4)] = yl
            return 0

        lax.fori_loop(0, 4, apply, 0)
        return 0

    lax.fori_loop(0, STEPS, step, 0)

    final = STEPS + 1
    outs = []
    for j in (1, 3, 2):
        outs.append(
            start(set_copy(field_block(final, (q + j) % 4), out.at[pl.ds(4 * q, 4)], OU0 + j - 1, ring(j)))
        )
    out[pl.ds(4 * q, 4)] = X[final, :, pl.ds(4 + 4 * q, 4), 8:24, :]
    for c in outs:
        c.wait_recv()
    for c in sends:
        c.wait_send()

    def drain(s, _):
        c = step_copies(s)
        for name, item in c.items():
            if name not in ("yl", "yh"):
                item.wait_send()

        @pl.when(iy > 0)
        def _():
            c["yl"].wait_send()

        @pl.when(iy < 3)
        def _():
            c["yh"].wait_send()

        return 0

    lax.fori_loop(0, STEPS, drain, 0)


def per_device(orbitals, potential, tile_proj, tile_atom, tile_column, tile_count, atom_home, coupling):
    ix, iy, iz = lax.axis_index("gx"), lax.axis_index("gy"), lax.axis_index("gz")
    zh = iz // 4
    owner = tile_atom >> 6
    dx = (owner >> 5) - ix + 1
    dy = ((owner >> 3) & 3) - iy + 1
    zb = (owner & 7) - 4 * zh
    pair = jnp.where((zb >= 0) & (zb < 4), zb >> 1, 2)
    number = (dx * 3 + dy) * 3 + pair
    lane = (zb & 1) * 64 + (tile_atom & 63)
    column = jnp.where(jnp.arange(256, dtype=I32) < tile_count[0], tile_column, -1)
    home = lax.dynamic_slice(atom_home, (((ix * 4 + iy) * 2 + zh) * 256,), (256,))
    meta = jnp.stack([number, lane, column, home, home, home, home, home]).astype(I32)
    vmem = pl.BlockSpec(memory_space=pltpu.VMEM)
    return pl.pallas_call(
        kernel,
        out_shape=jax.ShapeDtypeStruct((16, 4, 16, 128), F32),
        in_specs=[vmem] * 6,
        out_specs=vmem,
        scratch_shapes=[
            pltpu.VMEM((6, 4, 24, 32, 128), F32),
            pltpu.VMEM((4, 16, 16, 128), F32),
            pltpu.VMEM((4, 16, 16, 128), BF16),
            pltpu.VMEM((4, 16, 16, 128), BF16),
            pltpu.VMEM((4, 4, 256, 128), F32),
            pltpu.VMEM((4, 1024, 256), BF16),
            pltpu.VMEM((16, 16, 128), F32),
            pltpu.VMEM((4, 8, 256), I32),
            pltpu.VMEM((4, 64, 256), F32),
            pltpu.VMEM((4, 64, 256), BF16),
            pltpu.VMEM((4, 16, 256), I32),
            pltpu.VMEM((27, 16, 1024), BF16),
            pltpu.VMEM((4, 256, 256), BF16),
            pltpu.VMEM((27, 32, 1024), BF16),
            pltpu.VMEM((4, 27, 16, 128), F32),
            pltpu.VMEM((4, 9, 2, 16, 128), F32),
            pltpu.VMEM((4, 9, 16, 128), F32),
            pltpu.VMEM((4, 2, 16, 128), F32),
            pltpu.VMEM((4, 27, 16, 128), F32),
            pltpu.VMEM((2, 16, 128), F32),
            pltpu.VMEM((4, 8, 1024), F32),
            pltpu.VMEM((4, 8, 1024), F32),
            pltpu.VMEM((256, 128), F32),
            pltpu.VMEM((128, 256), BF16),
            pltpu.VMEM((4, 16, 256), F32),
            pltpu.SemaphoreType.DMA((NSET,)),
            pltpu.SemaphoreType.DMA((NSET,)),
            pltpu.SemaphoreType.DMA((STEPS, NSEM)),
            pltpu.SemaphoreType.DMA((STEPS, NSEM)),
        ],
        compiler_params=pltpu.CompilerParams(
            collective_id=0, has_side_effects=True, vmem_limit_bytes=60000 * 1024
        ),
        name="chebyshev",
    )(
        orbitals,
        potential,
        tile_proj.transpose(1, 0, 2),
        meta,
        coupling.T.reshape(2, 128),
        jnp.asarray(stencil_constants()),
    )


def solution(mesh):
    return jax.shard_map(
        per_device,
        mesh=mesh,
        in_specs=(
            P(None, "gz", "gy", "gx"),
            P("gz", "gy", "gx"),
            P(("gx", "gy", "gz"), None, None),
            P(("gx", "gy", "gz")),
            P(("gx", "gy", "gz")),
            P(("gx", "gy", "gz")),
            P(),
            P(("gx", "gy", "gz"), None),
        ),
        out_specs=P(None, "gz", "gy", "gx"),
        check_vma=False,
    )
```

```python
import jax
import jax.numpy as jnp
import numpy as np
from jax import lax
from jax.experimental import pallas as pl
from jax.experimental.pallas import tpu as pltpu
from jax.sharding import PartitionSpec as P

F32, BF16, I32 = jnp.float32, jnp.bfloat16, jnp.int32
STENCIL = (-205.0 / 72.0, 8.0 / 5.0, -1.0 / 5.0, 8.0 / 315.0, -1.0 / 560.0)
CENTER, HALF = 14.0, 10.0
STEPS = 4
DIRS = [(dx, dy) for dx in (-1, 0, 1) for dy in (-1, 0, 1)]
SELF = 4
XP, XM, YL, YH, ZH, RS0, RO0, BS0, BO0, NSEM = 0, 1, 2, 3, 4, 5, 14, 23, 32, 41
V0, PF0, PT0, ME0, CP0, PA0, OU0, FT0, NSET = 0, 3, 9, 12, 15, 25, 28, 31, 34


def stencil_constants():
    table = np.zeros((144, 128), np.float32)
    for x in range(128):
        for k in range(1, 5):
            if x + k < 128:
                table[x, x + k] = -0.5 * STENCIL[k]
            if x - k >= 0:
                table[x, x - k] = -0.5 * STENCIL[k]
    for j in range(4):
        table[128 + j, 124 + j] = 1.0
        table[132 + j, j] = 1.0
        for x in range(128):
            k = x + 4 - j
            if 1 <= k <= 4:
                table[136 + j, x] = -0.5 * STENCIL[k]
            k = 128 + j - x
            if 1 <= k <= 4:
                table[140 + j, x] = -0.5 * STENCIL[k]
    return table


def split(value):
    high = value.astype(BF16)
    return high, (value - high.astype(F32)).astype(BF16)


def dot_nt(a, b):
    return lax.dot_general(a, b, (((1,), (1,)), ((), ())), preferred_element_type=F32)


def dot_nn(a, b):
    return lax.dot_general(a, b, (((1,), (0,)), ((), ())), preferred_element_type=F32)


def dot_tn(a, b):
    return lax.dot_general(a, b, (((0,), (0,)), ((), ())), preferred_element_type=F32)


def kernel(
    orb, pot_in, tp, atom_hbm, column_hbm, count_in, home_hbm, cpl_hbm, table_hbm, out,
    X, Z, VH, VL, PF, PN, POT, META, MKF, MKB, NIDX, NMB, WT, LH, LS, RS, RO, CS, SS, SC, XS, XR, CB, CONST,
    PART, PART0, PTS, PTR, ZO, ORB, atom_in, column_in, home_in, cpl_in, table,
    set_s, set_r, sem_s, sem_r, local_sem,
):
    ix, iy, iz = lax.axis_index("gx"), lax.axis_index("gy"), lax.axis_index("gz")
    zh, q = iz // 4, iz % 4
    oz = 1 - zh
    below, above, across = (q + 3) % 4, (q + 1) % 4, (q + 2) % 4

    def dev(gx, gy, gz):
        return {"gx": gx, "gy": gy, "gz": gz}

    def ring(j):
        return dev(ix, iy, zh * 4 + (q + j) % 4)

    def near(dx, dy, half):
        return dev((ix + dx + 4) % 4, (iy + dy + 4) % 4, half * 4 + q)

    def exists(i):
        dx, dy = DIRS[i]
        return jnp.logical_and(
            jnp.logical_and(ix + dx >= 0, ix + dx <= 3), jnp.logical_and(iy + dy >= 0, iy + dy <= 3)
        )

    def copy(src, dst, s, r, to):
        return pltpu.make_async_remote_copy(
            src_ref=src, dst_ref=dst, send_sem=s, recv_sem=r, device_id=to, device_id_type=pl.DeviceIdType.MESH
        )

    barrier = pltpu.get_barrier_semaphore()
    peers = [near(dx, dy, half) for dx, dy in DIRS for half in (zh, oz)]
    peers = [p for i, p in enumerate(peers) if i != 2 * SELF]
    peers += [ring(j) for j in (1, 2, 3)]
    peers += [dev((ix + 2) % 4, iy, iz), dev(ix, (iy + 2) % 4, iz)]
    for peer in peers:
        pl.semaphore_signal(barrier, inc=1, device_id=peer, device_id_type=pl.DeviceIdType.MESH)
    take_proj = pltpu.make_async_copy(tp, PF.at[q], local_sem.at[0])
    take_orb = pltpu.make_async_copy(orb, ORB, local_sem.at[1])
    take_pot = pltpu.make_async_copy(pot_in, POT.at[pl.ds(4 * q, 4)], local_sem.at[2])
    take_own = pltpu.make_async_copy(
        orb.at[pl.ds(4 * q, 4)], X.at[1, :, pl.ds(4 + 4 * q, 4), pl.ds(8, 16), :], local_sem.at[3]
    )
    smalls = [
        pltpu.make_async_copy(src, dst, local_sem.at[4 + i])
        for i, (src, dst) in enumerate(
            (
                (atom_hbm, atom_in),
                (column_hbm, column_in),
                (cpl_hbm, cpl_in),
                (table_hbm, table),
                (home_hbm.at[pl.ds(2 * ((ix * 4 + iy) * 2 + zh), 2)], home_in),
            )
        )
    ]
    for c in smalls + [take_proj, take_orb, take_own, take_pot]:
        c.start()
    for c in smalls:
        c.wait()

    atom = atom_in[...]
    owner = lax.shift_right_logical(atom, 6)
    dx = lax.shift_right_logical(owner, 5) - ix + 1
    dy = jnp.bitwise_and(lax.shift_right_logical(owner, 3), 3) - iy + 1
    zb = jnp.bitwise_and(owner, 7) - 4 * zh
    pair = jnp.where(jnp.logical_and(zb >= 0, zb < 4), lax.shift_right_arithmetic(zb, 1), 2)
    number = (dx * 3 + dy) * 3 + pair
    lane = jnp.bitwise_and(zb, 1) * 64 + jnp.bitwise_and(atom, 63)
    column = jnp.where(lax.broadcasted_iota(I32, (1, 256), 1) < count_in[0], column_in[...], -1)
    META[pl.ds(q, 1)] = jnp.concatenate([number, lane, column] + [column] * 5, axis=0)[None]
    cpl = cpl_in[...]
    mine = 2 * ((ix * 4 + iy) * 8 + iz)
    CB[pl.ds(mine, 2), :] = jnp.concatenate(
        [jnp.concatenate([cpl[0:1], cpl[1:2]], axis=1), jnp.concatenate([cpl[2:3], cpl[3:4]], axis=1)], axis=0
    )

    row64 = lax.broadcasted_iota(I32, (64, 256), 0)
    row128 = lax.broadcasted_iota(I32, (128, 256), 0)

    def masks(b):
        mask = jnp.where(row64 == META[b, 2:3, :], 1.0, 0.0).astype(F32)
        MKF[b] = mask
        MKB[b] = mask.astype(BF16)

    masks(q)

    def clear(i, _):
        X[i, :, pl.ds(20 * zh, 4)] = jnp.zeros((4, 4, 32, 128), F32)

        @pl.when(iy == 0)
        def _():
            X[i, :, 4:20, 0:8] = jnp.zeros((4, 16, 8, 128), F32)

        @pl.when(iy == 3)
        def _():
            X[i, :, 4:20, 24:32] = jnp.zeros((4, 16, 8, 128), F32)

        return 0

    lax.fori_loop(1, 5, clear, 0)

    def clear_sums(i, _):
        for slot in range(9):
            if slot != SELF:

                @pl.when(jnp.logical_not(exists(slot)))
                def _():
                    RS[i, slot] = jnp.zeros((2, 16, 128), F32)
                    RO[i, slot] = jnp.zeros((16, 128), F32)

        return 0

    lax.fori_loop(0, 4, clear_sums, 0)

    wx_h, wx_l = split(table[0:128, :])
    CONST[0:128, 0:128] = wx_h
    CONST[0:128, 128:256] = wx_l
    e2 = table[128:136, :].astype(BF16)
    edge_row = lax.broadcasted_iota(I32, (8, 128), 0)
    inside = jnp.where(
        edge_row < 4, jnp.where(ix > 0, 1.0, 0.0).astype(F32), jnp.where(ix < 3, 1.0, 0.0).astype(F32)
    )
    edge = table[136:144, :] * inside
    edge_h = edge.astype(BF16).astype(F32)
    edge_1 = jnp.concatenate([edge_h, edge_h], axis=0).astype(BF16)
    edge_2 = jnp.concatenate([edge - edge_h, edge - edge_h], axis=0).astype(BF16)

    pl.semaphore_wait(barrier, len(peers))

    def field_block(index, block):
        return X.at[index, :, pl.ds(4 + 4 * block, 4), pl.ds(8, 16), :]

    sends = []

    def start(c):
        c.start()
        sends.append(c)
        return c

    def set_copy(src, dst, index, to):
        return copy(src, dst, set_s.at[index], set_r.at[index], to)

    def rows(first, count):
        return CB.at[pl.ds(first, count)]

    values = [
        start(set_copy(orb.at[pl.ds(4 * ((q + j) % 4), 4)], field_block(1, q), V0 + j - 1, ring(j))) for j in (2, 1, 3)
    ]
    metas = [start(set_copy(META.at[q], META.at[q], ME0 + j - 1, ring(j))) for j in (1, 3, 2)]
    ring_cpl = [start(set_copy(rows(mine, 2), rows(mine, 2), CP0 + j - 1, ring(j))) for j in (1, 3, 2)]

    def split_proj(b):
        for p in range(4):
            ph, pl_ = split(PF[b, pl.ds(p, 256, stride=4), :])
            PN[b, p * 256 : (p + 1) * 256, 0:128] = ph
            PN[b, p * 256 : (p + 1) * 256, 128:256] = pl_

    def tile_sums(vh, vl, b, result, at):
        t = dot_nt(jnp.concatenate([vh, vh], axis=1), PN[b]) + dot_nt(vl, PN[b, :, 0:128])
        mask = MKF[b]
        for p in range(4):
            for o in range(4):
                tile = t[o * 64 : (o + 1) * 64, p * 256 : (p + 1) * 256]
                result[at, pl.ds(p * 4 + o, 1), :] = jnp.sum(tile * mask, axis=0, keepdims=True)

    take_proj.wait()
    split_proj(q)
    take_orb.wait()

    def own_sums(g, _):
        vh, vl = split(ORB[pl.ds(4 * g, 4)].reshape(256, 128))
        tile_sums(vh, vl, q, PART0, g)
        return 0

    lax.fori_loop(0, 4, own_sums, 0)
    parts = [start(set_copy(PART0.at[(q + j) % 4], PART.at[q], PA0 + j - 1, ring(j))) for j in (2, 1, 3)]
    half = [pl.ds(0, 512), pl.ds(512, 512)]
    up = [start(set_copy(tp.at[half[h]], PF.at[q, half[h]], PF0 + h, ring(1))) for h in (0, 1)]
    down = [start(set_copy(tp.at[half[h]], PF.at[q, half[h]], PF0 + 3 - h, ring(3))) for h in (1, 0)]
    pots = [start(set_copy(pot_in, POT.at[pl.ds(4 * q, 4)], PT0 + j - 1, ring(j))) for j in (1, 3, 2)]
    PART[pl.ds(q, 1)] = PART0[pl.ds(q, 1)]

    for c in ring_cpl:
        c.wait_recv()
    group = 2 * ((ix * 4 + iy) * 8 + zh * 4)
    flip = start(set_copy(rows(group, 8), rows(group, 8), CP0 + 3, dev(ix, iy, oz * 4 + q)))

    for c in metas:
        c.wait_recv()
    masks(below)
    masks(above)
    masks(across)
    for b in range(4):
        index = META[b]
        hot = jnp.where(row128 == index[1:2, :], 1.0, 0.0).astype(BF16)
        WT[b, 0:128] = hot
        WT[b, 128:256] = hot
        number = jnp.broadcast_to(index[0:1, :], (16, 256))
        NIDX[b] = number
        for n in range(27):
            NMB[n, :, b * 256 : (b + 1) * 256] = jnp.where(number == n, 1.0, 0.0).astype(BF16)

    flip.wait_recv()
    group = 2 * ((ix * 4 + iy) * 8)
    cpl_y = [
        start(set_copy(rows(group, 16), rows(group, 16), CP0 + 3 + j, dev(ix, (iy + j) % 4, iz))) for j in (1, 3, 2)
    ]

    def step_copies(s):
        cur = s + 1

        def sc(src, dst, index, to):
            return copy(src, dst, sem_s.at[s, index], sem_r.at[s, index], to)

        c = {}
        c["xp"] = sc(XS.at[s, pl.ds(0, 4)], XR.at[s, pl.ds(0, 4)], XP, dev((ix + 1) % 4, iy, iz))
        c["xm"] = sc(XS.at[s, pl.ds(4, 4)], XR.at[s, pl.ds(4, 4)], XM, dev((ix + 3) % 4, iy, iz))
        inner = pl.ds(4, 16)
        c["yl"] = sc(
            X.at[cur, :, inner, pl.ds(8, 4), :], X.at[cur, :, inner, pl.ds(24, 4), :], YL, dev(ix, (iy + 3) % 4, iz)
        )
        c["yh"] = sc(
            X.at[cur, :, inner, pl.ds(20, 4), :], X.at[cur, :, inner, pl.ds(4, 4), :], YH, dev(ix, (iy + 1) % 4, iz)
        )
        c["z"] = sc(
            X.at[cur, :, pl.ds(4 + 12 * oz, 4), pl.ds(8, 16), :],
            X.at[cur, :, pl.ds(20 * zh, 4), pl.ds(8, 16), :],
            ZH,
            dev(ix, iy, oz * 4 + q),
        )
        for i, (dx, dy) in enumerate(DIRS):
            slot = 8 - i
            if i != SELF:
                c["rs", i] = sc(LS.at[s, pl.ds(3 * i, 2)], RS.at[s, slot], RS0 + slot, near(dx, dy, zh))
                c["bs", i] = sc(CS.at[s], SS.at[s, pl.ds(3 * slot, 2)], BS0 + slot, near(dx, dy, zh))
            c["ro", i] = sc(LS.at[s, 3 * i + 2], RO.at[s, slot], RO0 + slot, near(dx, dy, oz))
            c["bo", i] = sc(CS.at[s, oz], SS.at[s, 3 * slot + 2], BO0 + slot, near(dx, dy, oz))
        return c

    def when(condition, action):
        @pl.when(condition)
        def _():
            action()

    def neighbours(c, names, action, mirrored):
        for i in range(9):
            def both(i=i):
                for name in names:
                    if (name, i) in c:
                        getattr(c[name, i], action)()

            if i == SELF:
                both()
            else:
                when(exists(8 - i if mirrored else i), both)

    def send_halos(c):
        c["z"].start()
        when(iy > 0, c["yl"].start)
        when(iy < 3, c["yh"].start)

    def pack_x(s, c):
        vh_all = VH[...].reshape(1024, 128)
        vl_all = VL[...].reshape(1024, 128)
        XS[s] = dot_nt(e2, vh_all) + dot_nt(e2, vl_all)
        xp = dot_nt(jnp.concatenate([vh_all, vh_all], axis=1), CONST[...]) + dot_nt(vl_all, CONST[:, 0:128])
        Z[...] = xp.reshape(4, 16, 16, 128)
        c["xp"].start()
        c["xm"].start()

    def atom_sums(s, c):
        for b in range(4):
            ph, pl_ = split(PART[b])
            for n in range(27):
                m = NMB[n, :, b * 256 : (b + 1) * 256]
                LH[n, 0:16, b * 256 : (b + 1) * 256] = ph * m
                LH[n, 16:32, b * 256 : (b + 1) * 256] = pl_ * m
        sums = None
        for b in range(4):
            lhs = LH[:, :, b * 256 : (b + 1) * 256].reshape(864, 256)
            term = dot_nt(lhs, WT[b, 0:128])
            sums = term if sums is None else sums + term
        sums = sums.reshape(27, 32, 128)
        LS[s] = sums[:, 0:16] + sums[:, 16:32]
        neighbours(c, ("ro", "rs"), "start", False)

    def stencil(s, c, first):
        c["xp"].wait_recv()
        c["xm"].wait_recv()
        xr = XR[s]
        xr_h = xr.astype(BF16).astype(F32)
        faces = jnp.concatenate([xr_h, xr - xr_h], axis=0).astype(BF16)
        Z[...] = Z[...] + (dot_tn(faces, edge_1) + dot_tn(faces, edge_2)).reshape(4, 16, 16, 128)
        c["z"].wait_recv()
        when(iy > 0, c["yh"].wait_recv)
        when(iy < 3, c["yl"].wait_recv)
        cur = s + 1
        scale = (1.0 if first else 2.0) / HALF

        def line(i, _):
            o = i // 16
            z = i % 16
            v0 = X[cur, o, z + 4, 8:24, :]
            acc = Z[o, z] + v0 * (POT[z] + (-1.5 * STENCIL[0] - CENTER))
            for k in range(1, 5):
                around = (X[cur, o, z + 4 - k, 8:24, :] + X[cur, o, z + 4 + k, 8:24, :]) + (
                    X[cur, o, z + 4, 8 - k : 24 - k, :] + X[cur, o, z + 4, 8 + k : 24 + k, :]
                )
                acc = acc + (-0.5 * STENCIL[k]) * around
            acc = scale * acc
            Z[o, z] = acc if first else acc - X[s, o, z + 4, 8:24, :]
            return 0

        lax.fori_loop(0, 64, line, 0, unroll=4)

    def scale_totals(s, c, first):
        neighbours(c, ("rs", "ro"), "wait_recv", True)
        total = LS[s, 3 * SELF : 3 * SELF + 2]
        other = None
        for slot in range(9):
            if slot != SELF:
                total = total + RS[s, slot]
            other = RO[s, slot] if other is None else other + RO[s, slot]
        at_0 = jnp.where(zh == 1, 1.0, 0.0).astype(F32)
        scale = (1.0 if first else 2.0) / HALF
        scaled = scale * SC[...] * jnp.stack([total[0] + at_0 * other, total[1] + (1.0 - at_0) * other])
        CS[s] = scaled
        SS[s, 3 * SELF : 3 * SELF + 2] = scaled
        neighbours(c, ("bo", "bs"), "start", False)

    def per_tile(s, b):
        sh, sl = split(SS[s].reshape(432, 128))
        r = dot_nn(jnp.concatenate([sh, sl], axis=1), WT[b])
        number = NIDX[b]
        pt = jnp.zeros((16, 256), F32)
        for n in range(27):
            pt = pt + jnp.where(number == n, r[n * 16 : (n + 1) * 16], 0.0)
        return pt

    def project(pt, b):
        pth, ptl = split(pt)
        mask = MKB[b]

        def spread(part):
            return jnp.concatenate(
                [
                    jnp.concatenate([mask * part[p * 4 + o : p * 4 + o + 1] for p in range(4)], axis=1)
                    for o in range(4)
                ],
                axis=0,
            )

        wide = dot_nn(spread(pth), PN[b])
        return wide[:, 0:128] + wide[:, 128:256] + dot_nn(spread(ptl), PN[b, :, 0:128])

    def apply(s, b):
        y = Z[:, pl.ds(4 * b, 4)] + project(per_tile(s, b), b).reshape(4, 4, 16, 128)
        X[s + 2, :, pl.ds(4 + 4 * b, 4), 8:24, :] = y
        yh, yl = split(y)
        VH[:, pl.ds(4 * b, 4)] = yh
        VL[:, pl.ds(4 * b, 4)] = yl

    c = step_copies(0)
    take_own.wait()
    for v in values:
        v.wait_recv()
    send_halos(c)
    for v in parts:
        v.wait_recv()
    atom_sums(0, c)
    high, low = split(X[1, :, 4:20, 8:24, :])
    VH[...] = high
    VL[...] = low
    pack_x(0, c)

    for v in cpl_y:
        v.wait_recv()
    group = 2 * (ix * 32)
    cpl_x = [
        start(set_copy(rows(group, 64), rows(group, 64), CP0 + 6 + j, dev((ix + j) % 4, iy, iz))) for j in (1, 3, 2)
    ]
    take_pot.wait()
    for v in pots:
        v.wait_recv()
    stencil(0, c, True)

    for v in cpl_x:
        v.wait_recv()
    home2 = home_in[...]
    home = jnp.concatenate([home2[0:1], home2[1:2]], axis=1)
    home_row = 2 * lax.shift_right_logical(home, 6)
    rows256 = lax.broadcasted_iota(I32, (256, 256), 0)
    lane_hot = jnp.where(row64 == jnp.bitwise_and(home, 63), 1.0, 0.0).astype(F32)
    cb = CB[...]
    cb_1 = cb.astype(BF16)
    rest = cb - cb_1.astype(F32)
    cb_2 = rest.astype(BF16)
    cb_3 = (rest - cb_2.astype(F32)).astype(BF16)
    for r in range(2):
        pick = jnp.where(rows256 == home_row + r, 1.0, 0.0).astype(BF16)
        found = dot_tn(cb_1, pick) + dot_tn(cb_2, pick) + dot_tn(cb_3, pick)
        for p2 in range(2):
            line = jnp.sum(found[p2 * 64 : (p2 + 1) * 64] * lane_hot, axis=0, keepdims=True)
            p = 2 * r + p2
            for pair in range(2):
                SC[pair, p * 4 : (p + 1) * 4, :] = jnp.broadcast_to(line[:, pair * 128 : (pair + 1) * 128], (4, 128))

    scale_totals(0, c, True)

    up[0].wait_recv()
    on_up = start(set_copy(PF.at[below, half[0]], PF.at[below, half[0]], PF0 + 4, ring(1)))
    down[0].wait_recv()
    on_down = start(set_copy(PF.at[above, half[1]], PF.at[above, half[1]], PF0 + 5, ring(3)))
    neighbours(c, ("bs", "bo"), "wait_recv", True)
    apply(0, q)
    up[1].wait_recv()
    split_proj(below)
    apply(0, below)
    down[1].wait_recv()
    split_proj(above)
    apply(0, above)
    on_up.wait_recv()
    on_down.wait_recv()
    split_proj(across)
    apply(0, across)

    def head(s):
        c = step_copies(s)
        send_halos(c)
        pack_x(s, c)

        def sums(b, _):
            vh = VH[:, pl.ds(4 * b, 4)].reshape(256, 128)
            vl = VL[:, pl.ds(4 * b, 4)].reshape(256, 128)
            tile_sums(vh, vl, b, PART, b)
            return 0

        lax.fori_loop(0, 4, sums, 0)
        atom_sums(s, c)
        stencil(s, c, False)
        return c

    def step(s, _):
        c = head(s)
        scale_totals(s, c, False)
        neighbours(c, ("bs", "bo"), "wait_recv", True)

        def one(b, _):
            apply(s, b)
            return 0

        lax.fori_loop(0, 4, one, 0)
        return 0

    lax.fori_loop(1, STEPS - 1, step, 0)

    last = STEPS - 1
    c = head(last)
    scale_totals(last, c, False)
    outs = [
        start(set_copy(Z.at[:, pl.ds(4 * ((q + j) % 4), 4)], ZO.at[pl.ds(4 * q, 4)], OU0 + j - 1, ring(j)))
        for j in (2, 1, 3)
    ]
    neighbours(c, ("bs", "bo"), "wait_recv", True)
    finals = []
    for j in (2, 1, 3):
        b = (q + j) % 4
        PTS[pl.ds(b, 1)] = per_tile(last, b)[None]
        finals.append(start(set_copy(PTS.at[b], PTR.at[q], FT0 + j - 1, ring(j))))
    result = Z[:, pl.ds(4 * q, 4)] + project(per_tile(last, q), q).reshape(4, 4, 16, 128)
    out[pl.ds(4 * q, 4)] = result
    for v in outs:
        v.wait_recv()
    for index, j in ((1, 1), (2, 3), (0, 2)):
        finals[index].wait_recv()
        g = (q - j + 4) % 4
        out[pl.ds(4 * g, 4)] = ZO[pl.ds(4 * g, 4)] + project(PTR[g], q).reshape(4, 4, 16, 128)
    for v in sends:
        v.wait_send()

    def drain(s, _):
        c = step_copies(s)
        for name in ("xp", "xm", "z"):
            c[name].wait_send()
        when(iy > 0, c["yl"].wait_send)
        when(iy < 3, c["yh"].wait_send)
        neighbours(c, ("rs", "ro", "bs", "bo"), "wait_send", False)
        return 0

    lax.fori_loop(0, STEPS, drain, 0)


def per_device(orbitals, potential, tile_proj, tile_atom, tile_column, tile_count, atom_home, coupling):
    vmem = pl.BlockSpec(memory_space=pltpu.VMEM)
    hbm = pl.BlockSpec(memory_space=pltpu.HBM)
    smem = pl.BlockSpec(memory_space=pltpu.SMEM)
    return pl.pallas_call(
        kernel,
        out_shape=jax.ShapeDtypeStruct((16, 4, 16, 128), F32),
        in_specs=[hbm] * 5 + [smem] + [hbm] * 3,
        out_specs=vmem,
        scratch_shapes=[
            pltpu.VMEM((6, 4, 24, 32, 128), F32),
            pltpu.VMEM((4, 16, 16, 128), F32),
            pltpu.VMEM((4, 16, 16, 128), BF16),
            pltpu.VMEM((4, 16, 16, 128), BF16),
            pltpu.VMEM((4, 1024, 128), F32),
            pltpu.VMEM((4, 1024, 256), BF16),
            pltpu.VMEM((16, 16, 128), F32),
            pltpu.VMEM((4, 8, 256), I32),
            pltpu.VMEM((4, 64, 256), F32),
            pltpu.VMEM((4, 64, 256), BF16),
            pltpu.VMEM((4, 16, 256), I32),
            pltpu.VMEM((27, 16, 1024), BF16),
            pltpu.VMEM((4, 256, 256), BF16),
            pltpu.VMEM((27, 32, 1024), BF16),
            pltpu.VMEM((4, 27, 16, 128), F32),
            pltpu.VMEM((4, 9, 2, 16, 128), F32),
            pltpu.VMEM((4, 9, 16, 128), F32),
            pltpu.VMEM((4, 2, 16, 128), F32),
            pltpu.VMEM((4, 27, 16, 128), F32),
            pltpu.VMEM((2, 16, 128), F32),
            pltpu.VMEM((4, 8, 1024), F32),
            pltpu.VMEM((4, 8, 1024), F32),
            pltpu.VMEM((256, 128), F32),
            pltpu.VMEM((128, 256), BF16),
            pltpu.VMEM((4, 16, 256), F32),
            pltpu.VMEM((4, 16, 256), F32),
            pltpu.VMEM((4, 16, 256), F32),
            pltpu.VMEM((4, 16, 256), F32),
            pltpu.VMEM((16, 4, 16, 128), F32),
            pltpu.VMEM((16, 4, 16, 128), F32),
            pltpu.VMEM((1, 256), I32),
            pltpu.VMEM((1, 256), I32),
            pltpu.VMEM((2, 128), I32),
            pltpu.VMEM((4, 64), F32),
            pltpu.VMEM((144, 128), F32),
            pltpu.SemaphoreType.DMA((NSET,)),
            pltpu.SemaphoreType.DMA((NSET,)),
            pltpu.SemaphoreType.DMA((STEPS, NSEM)),
            pltpu.SemaphoreType.DMA((STEPS, NSEM)),
            pltpu.SemaphoreType.DMA((9,)),
        ],
        compiler_params=pltpu.CompilerParams(
            collective_id=0, has_side_effects=True, vmem_limit_bytes=60000 * 1024
        ),
        name="chebyshev",
    )(
        orbitals,
        potential,
        tile_proj.reshape(1024, 128),
        tile_atom.reshape(1, 256),
        tile_column.reshape(1, 256),
        tile_count,
        atom_home.reshape(64, 128),
        coupling.T,
        jnp.asarray(stencil_constants()),
    )


def solution(mesh):
    return jax.shard_map(
        per_device,
        mesh=mesh,
        in_specs=(
            P(None, "gz", "gy", "gx"),
            P("gz", "gy", "gx"),
            P(("gx", "gy", "gz"), None, None),
            P(("gx", "gy", "gz")),
            P(("gx", "gy", "gz")),
            P(("gx", "gy", "gz")),
            P(),
            P(("gx", "gy", "gz"), None),
        ),
        out_specs=P(None, "gz", "gy", "gx"),
        check_vma=False,
    )
```

```python
import jax
import jax.numpy as jnp
import numpy as np
from jax import lax
from jax.experimental import pallas as pl
from jax.experimental.pallas import tpu as pltpu
from jax.sharding import PartitionSpec as P

F32, BF16, I32 = jnp.float32, jnp.bfloat16, jnp.int32
STENCIL = (-205.0 / 72.0, 8.0 / 5.0, -1.0 / 5.0, 8.0 / 315.0, -1.0 / 560.0)
CENTER, HALF = 14.0, 10.0
STEPS = 4
DIRS = [(dx, dy) for dx in (-1, 0, 1) for dy in (-1, 0, 1)]
SELF = 4
XP, XM, YL, YH, ZH, RS0, RO0, BS0, BO0, NSEM = 0, 1, 2, 3, 4, 5, 14, 23, 32, 41
V0, PF0, PT0, ME0, CP0, PA0, OU0, FT0, NSET = 0, 6, 12, 15, 18, 28, 31, 37, 40


def stencil_constants():
    table = np.zeros((144, 128), np.float32)
    for x in range(128):
        for k in range(1, 5):
            if x + k < 128:
                table[x, x + k] = -0.5 * STENCIL[k]
            if x - k >= 0:
                table[x, x - k] = -0.5 * STENCIL[k]
    for j in range(4):
        table[128 + j, 124 + j] = 1.0
        table[132 + j, j] = 1.0
        for x in range(128):
            k = x + 4 - j
            if 1 <= k <= 4:
                table[136 + j, x] = -0.5 * STENCIL[k]
            k = 128 + j - x
            if 1 <= k <= 4:
                table[140 + j, x] = -0.5 * STENCIL[k]
    return table


def split(value):
    high = value.astype(BF16)
    return high, (value - high.astype(F32)).astype(BF16)


def dot_nt(a, b):
    return lax.dot_general(a, b, (((1,), (1,)), ((), ())), preferred_element_type=F32)


def dot_nn(a, b):
    return lax.dot_general(a, b, (((1,), (0,)), ((), ())), preferred_element_type=F32)


def dot_tn(a, b):
    return lax.dot_general(a, b, (((0,), (0,)), ((), ())), preferred_element_type=F32)


def kernel(
    orb, pot_in, tp, atom_hbm, column_hbm, count_in, home_hbm, cpl_hbm, table_hbm, out,
    X, Z, VH, VL, PF, PN, POT, META, MKF, MKB, NIDX, NMB, WT, LH, LHO, LSA, LSO, RS, RO, CS, SSA, SSO, SHA, SHO, SC, XS, XR, CB, CONST,
    PART, PART0, PTS, PTR, ZO, ORB, RL, RLO, atom_in, column_in, home_in, cpl_in, table,
    set_s, set_r, sem_s, sem_r, local_sem,
):
    ix, iy, iz = lax.axis_index("gx"), lax.axis_index("gy"), lax.axis_index("gz")
    zh, q = iz // 4, iz % 4
    oz = 1 - zh
    edge_block = 3 * oz
    below, above, across = (q + 3) % 4, (q + 1) % 4, (q + 2) % 4

    def dev(gx, gy, gz):
        return {"gx": gx, "gy": gy, "gz": gz}

    def ring(j):
        return dev(ix, iy, zh * 4 + (q + j) % 4)

    def near(dx, dy, half):
        return dev((ix + dx + 4) % 4, (iy + dy + 4) % 4, half * 4 + q)

    def exists(i):
        dx, dy = DIRS[i]
        return jnp.logical_and(
            jnp.logical_and(ix + dx >= 0, ix + dx <= 3), jnp.logical_and(iy + dy >= 0, iy + dy <= 3)
        )

    def copy(src, dst, s, r, to):
        return pltpu.make_async_remote_copy(
            src_ref=src, dst_ref=dst, send_sem=s, recv_sem=r, device_id=to, device_id_type=pl.DeviceIdType.MESH
        )

    barrier = pltpu.get_barrier_semaphore()
    peers = [near(dx, dy, half) for dx, dy in DIRS for half in (zh, oz)]
    peers = [p for i, p in enumerate(peers) if i != 2 * SELF]
    peers += [ring(j) for j in (1, 2, 3)]
    peers += [dev((ix + 2) % 4, iy, iz), dev(ix, (iy + 2) % 4, iz)]
    for peer in peers:
        pl.semaphore_signal(barrier, inc=1, device_id=peer, device_id_type=pl.DeviceIdType.MESH)
    take_proj = pltpu.make_async_copy(tp, PF.at[q], local_sem.at[0])
    take_orb = pltpu.make_async_copy(orb, ORB, local_sem.at[1])
    take_pot = pltpu.make_async_copy(pot_in, POT.at[pl.ds(4 * q, 4)], local_sem.at[2])
    take_own = pltpu.make_async_copy(
        orb.at[pl.ds(4 * q, 4)], X.at[1, :, pl.ds(4 + 4 * q, 4), pl.ds(8, 16), :], local_sem.at[3]
    )
    smalls = [
        pltpu.make_async_copy(src, dst, local_sem.at[4 + i])
        for i, (src, dst) in enumerate(
            (
                (atom_hbm, atom_in),
                (column_hbm, column_in),
                (cpl_hbm, cpl_in),
                (table_hbm, table),
                (home_hbm.at[pl.ds(2 * ((ix * 4 + iy) * 2 + zh), 2)], home_in),
            )
        )
    ]
    for c in smalls + [take_proj, take_orb, take_own, take_pot]:
        c.start()
    for c in smalls:
        c.wait()

    atom = atom_in[...]
    owner = lax.shift_right_logical(atom, 6)
    dx = lax.shift_right_logical(owner, 5) - ix + 1
    dy = jnp.bitwise_and(lax.shift_right_logical(owner, 3), 3) - iy + 1
    zb = jnp.bitwise_and(owner, 7) - 4 * zh
    pair = jnp.where(jnp.logical_and(zb >= 0, zb < 4), lax.shift_right_arithmetic(zb, 1), 2)
    number = (dx * 3 + dy) * 3 + pair
    lane = jnp.bitwise_and(zb, 1) * 64 + jnp.bitwise_and(atom, 63)
    column = jnp.where(lax.broadcasted_iota(I32, (1, 256), 1) < count_in[0], column_in[...], -1)
    META[pl.ds(q, 1)] = jnp.concatenate([number, lane, column] + [column] * 5, axis=0)[None]
    cpl = cpl_in[...]
    mine = 2 * ((ix * 4 + iy) * 8 + iz)
    CB[pl.ds(mine, 2), :] = jnp.concatenate(
        [jnp.concatenate([cpl[0:1], cpl[1:2]], axis=1), jnp.concatenate([cpl[2:3], cpl[3:4]], axis=1)], axis=0
    )

    row64 = lax.broadcasted_iota(I32, (64, 256), 0)
    row128 = lax.broadcasted_iota(I32, (128, 256), 0)

    def masks(b):
        mask = jnp.where(row64 == META[b, 2:3, :], 1.0, 0.0).astype(F32)
        MKF[b] = mask
        MKB[b] = mask.astype(BF16)

    masks(q)

    def clear(i, _):
        X[i, :, pl.ds(20 * zh, 4)] = jnp.zeros((4, 4, 32, 128), F32)

        @pl.when(iy == 0)
        def _():
            X[i, :, 4:20, 0:8] = jnp.zeros((4, 16, 8, 128), F32)

        @pl.when(iy == 3)
        def _():
            X[i, :, 4:20, 24:32] = jnp.zeros((4, 16, 8, 128), F32)

        return 0

    lax.fori_loop(1, 5, clear, 0)

    def clear_sums(i, _):
        for slot in range(9):
            if slot != SELF:

                @pl.when(jnp.logical_not(exists(slot)))
                def _():
                    RS[i, slot] = jnp.zeros((2, 16, 128), F32)
                    RO[i, slot] = jnp.zeros((16, 128), F32)

        return 0

    lax.fori_loop(0, 4, clear_sums, 0)

    wx_h, wx_l = split(table[0:128, :])
    CONST[0:128, 0:128] = wx_h
    CONST[0:128, 128:256] = wx_l
    e2 = table[128:136, :].astype(BF16)
    edge_row = lax.broadcasted_iota(I32, (8, 128), 0)
    inside = jnp.where(
        edge_row < 4, jnp.where(ix > 0, 1.0, 0.0).astype(F32), jnp.where(ix < 3, 1.0, 0.0).astype(F32)
    )
    edge = table[136:144, :] * inside
    edge_h = edge.astype(BF16).astype(F32)
    edge_1 = jnp.concatenate([edge_h, edge_h], axis=0).astype(BF16)
    edge_2 = jnp.concatenate([edge - edge_h, edge - edge_h], axis=0).astype(BF16)

    def split_proj(b):
        for p in range(4):
            ph, pl_ = split(PF[b, pl.ds(p, 256, stride=4), :])
            PN[b, p * 256 : (p + 1) * 256, 0:128] = ph
            PN[b, p * 256 : (p + 1) * 256, 128:256] = pl_

    take_proj.wait()
    split_proj(q)
    pl.semaphore_wait(barrier, len(peers))

    def field_block(index, block):
        return X.at[index, :, pl.ds(4 + 4 * block, 4), pl.ds(8, 16), :]

    sends = []

    def start(c):
        c.start()
        sends.append(c)
        return c

    def set_copy(src, dst, index, to):
        return copy(src, dst, set_s.at[index], set_r.at[index], to)

    def rows(first, count):
        return CB.at[pl.ds(first, count)]

    metas = [start(set_copy(META.at[q], META.at[q], ME0 + j - 1, ring(j))) for j in (1, 3, 2)]
    ring_cpl = [start(set_copy(rows(mine, 2), rows(mine, 2), CP0 + j - 1, ring(j))) for j in (1, 3, 2)]

    def around(source, target, relay, base):
        to_up = start(set_copy(source(across, 0, 2), relay.at[0], base, ring(1)))
        to_down = start(set_copy(source(across, 2, 2), relay.at[1], base + 1, ring(3)))
        near_up = start(set_copy(source(above, 0, 4), target(q, 0, 4), base + 2, ring(1)))
        near_down = start(set_copy(source(below, 0, 4), target(q, 0, 4), base + 3, ring(3)))

        def forward():
            to_up.wait_recv()
            far_up = start(set_copy(relay.at[0], target(below, 0, 2), base + 4, ring(1)))
            to_down.wait_recv()
            far_down = start(set_copy(relay.at[1], target(above, 2, 2), base + 5, ring(3)))
            return near_up, near_down, far_up, far_down

        return forward

    values_on = around(
        lambda block, o, n: orb.at[pl.ds(4 * block + o, n)],
        lambda block, o, n: X.at[1, pl.ds(o, n), pl.ds(4 + 4 * block, 4), pl.ds(8, 16), :],
        RL,
        V0,
    )

    def tile_sums(vh, vl, b, result, at):
        t = dot_nt(jnp.concatenate([vh, vh], axis=1), PN[b]) + dot_nt(vl, PN[b, :, 0:128])
        mask = MKF[b]
        for p in range(4):
            for o in range(4):
                tile = t[o * 64 : (o + 1) * 64, p * 256 : (p + 1) * 256]
                result[at, pl.ds(p * 4 + o, 1), :] = jnp.sum(tile * mask, axis=0, keepdims=True)

    take_orb.wait()

    def own_sums(g, _):
        vh, vl = split(ORB[pl.ds(4 * g, 4)].reshape(256, 128))
        tile_sums(vh, vl, q, PART0, g)
        return 0

    lax.fori_loop(0, 4, own_sums, 0)
    values = values_on()
    parts = [start(set_copy(PART0.at[(q + j) % 4], PART.at[q], PA0 + j - 1, ring(j))) for j in (2, 1, 3)]
    half = [pl.ds(0, 512), pl.ds(512, 512)]
    up = [start(set_copy(tp.at[half[h]], PF.at[q, half[h]], PF0 + h, ring(1))) for h in (0, 1)]
    down = [start(set_copy(tp.at[half[h]], PF.at[q, half[h]], PF0 + 3 - h, ring(3))) for h in (1, 0)]
    pots = [start(set_copy(pot_in, POT.at[pl.ds(4 * q, 4)], PT0 + j - 1, ring(j))) for j in (1, 3, 2)]
    PART[pl.ds(q, 1)] = PART0[pl.ds(q, 1)]

    for c in ring_cpl:
        c.wait_recv()
    group = 2 * ((ix * 4 + iy) * 8 + zh * 4)
    flip = start(set_copy(rows(group, 8), rows(group, 8), CP0 + 3, dev(ix, iy, oz * 4 + q)))

    for c in metas:
        c.wait_recv()
    masks(below)
    masks(above)
    masks(across)
    for b in range(4):
        index = META[b]
        hot = jnp.where(row128 == index[1:2, :], 1.0, 0.0).astype(BF16)
        WT[b, 0:128] = hot
        WT[b, 128:256] = hot
        number = jnp.broadcast_to(index[0:1, :], (16, 256))
        NIDX[b] = number
        for n in range(27):
            NMB[b, n] = jnp.where(number == n, 1.0, 0.0).astype(BF16)

    flip.wait_recv()
    group = 2 * ((ix * 4 + iy) * 8)
    cpl_y = [
        start(set_copy(rows(group, 16), rows(group, 16), CP0 + 3 + j, dev(ix, (iy + j) % 4, iz))) for j in (1, 3, 2)
    ]

    def step_copies(s):
        cur = s + 1

        def sc(src, dst, index, to):
            return copy(src, dst, sem_s.at[s, index], sem_r.at[s, index], to)

        c = {}
        c["xp"] = sc(XS.at[s, pl.ds(0, 4)], XR.at[s, pl.ds(0, 4)], XP, dev((ix + 1) % 4, iy, iz))
        c["xm"] = sc(XS.at[s, pl.ds(4, 4)], XR.at[s, pl.ds(4, 4)], XM, dev((ix + 3) % 4, iy, iz))
        inner = pl.ds(4, 16)
        c["yl"] = sc(
            X.at[cur, :, inner, pl.ds(8, 4), :], X.at[cur, :, inner, pl.ds(24, 4), :], YL, dev(ix, (iy + 3) % 4, iz)
        )
        c["yh"] = sc(
            X.at[cur, :, inner, pl.ds(20, 4), :], X.at[cur, :, inner, pl.ds(4, 4), :], YH, dev(ix, (iy + 1) % 4, iz)
        )
        c["z"] = sc(
            X.at[cur, :, pl.ds(4 + 12 * oz, 4), pl.ds(8, 16), :],
            X.at[cur, :, pl.ds(20 * zh, 4), pl.ds(8, 16), :],
            ZH,
            dev(ix, iy, oz * 4 + q),
        )
        for i, (dx, dy) in enumerate(DIRS):
            slot = 8 - i
            if i != SELF:
                c["rs", i] = sc(LSA.at[s, i], RS.at[s, slot], RS0 + slot, near(dx, dy, zh))
                c["bs", i] = sc(CS.at[s], SSA.at[s, slot], BS0 + slot, near(dx, dy, zh))
            c["ro", i] = sc(LSO.at[s, i], RO.at[s, slot], RO0 + slot, near(dx, dy, oz))
            c["bo", i] = sc(CS.at[s, oz], SSO.at[s, slot], BO0 + slot, near(dx, dy, oz))
        return c

    def when(condition, action):
        @pl.when(condition)
        def _():
            action()

    def neighbours(c, names, action, mirrored):
        for i in range(9):
            def both(i=i):
                for name in names:
                    if (name, i) in c:
                        getattr(c[name, i], action)()

            if i == SELF:
                both()
            else:
                when(exists(8 - i if mirrored else i), both)

    def send_halos(c):
        c["z"].start()
        when(iy > 0, c["yl"].start)
        when(iy < 3, c["yh"].start)

    def pack_x(s, c):
        vh_all = VH[...].reshape(1024, 128)
        vl_all = VL[...].reshape(1024, 128)
        XS[s] = dot_nt(e2, vh_all) + dot_nt(e2, vl_all)
        xp = dot_nt(jnp.concatenate([vh_all, vh_all], axis=1), CONST[...]) + dot_nt(vl_all, CONST[:, 0:128])
        Z[...] = xp.reshape(4, 16, 16, 128)
        c["xp"].start()
        c["xm"].start()

    def sums_for_other_half(s, c):
        ph, pl_ = split(PART[edge_block])
        for i in range(9):
            m = NMB[edge_block, 3 * i + 2]
            LHO[i, 0:16] = ph * m
            LHO[i, 16:32] = pl_ * m
        sums = dot_nt(LHO[...].reshape(288, 256), WT[edge_block, 0:128]).reshape(9, 32, 128)
        LSO[s] = sums[:, 0:16] + sums[:, 16:32]
        neighbours(c, ("ro",), "start", False)

    def sums_for_own_half(s, c):
        for b in range(4):
            ph, pl_ = split(PART[b])
            for i in range(9):
                for pair in range(2):
                    m = NMB[b, 3 * i + pair]
                    LH[2 * i + pair, 0:16, b * 256 : (b + 1) * 256] = ph * m
                    LH[2 * i + pair, 16:32, b * 256 : (b + 1) * 256] = pl_ * m
        sums = None
        for b in range(4):
            lhs = LH[:, :, b * 256 : (b + 1) * 256].reshape(576, 256)
            term = dot_nt(lhs, WT[b, 0:128])
            sums = term if sums is None else sums + term
        sums = sums.reshape(18, 32, 128)
        LSA[s] = (sums[:, 0:16] + sums[:, 16:32]).reshape(9, 2, 16, 128)
        neighbours(c, ("rs",), "start", False)

    def stencil(s, c, first):
        c["xp"].wait_recv()
        c["xm"].wait_recv()
        xr = XR[s]
        xr_h = xr.astype(BF16).astype(F32)
        faces = jnp.concatenate([xr_h, xr - xr_h], axis=0).astype(BF16)
        Z[...] = Z[...] + (dot_tn(faces, edge_1) + dot_tn(faces, edge_2)).reshape(4, 16, 16, 128)
        c["z"].wait_recv()
        when(iy > 0, c["yh"].wait_recv)
        when(iy < 3, c["yl"].wait_recv)
        cur = s + 1
        scale = (1.0 if first else 2.0) / HALF

        def line(i, _):
            o = i // 16
            z = i % 16
            v0 = X[cur, o, z + 4, 8:24, :]
            acc = Z[o, z] + v0 * (POT[z] + (-1.5 * STENCIL[0] - CENTER))
            for k in range(1, 5):
                around = (X[cur, o, z + 4 - k, 8:24, :] + X[cur, o, z + 4 + k, 8:24, :]) + (
                    X[cur, o, z + 4, 8 - k : 24 - k, :] + X[cur, o, z + 4, 8 + k : 24 + k, :]
                )
                acc = acc + (-0.5 * STENCIL[k]) * around
            acc = scale * acc
            Z[o, z] = acc if first else acc - X[s, o, z + 4, 8:24, :]
            return 0

        lax.fori_loop(0, 64, line, 0, unroll=4)

    def scale_totals(s, c, first):
        neighbours(c, ("rs", "ro"), "wait_recv", True)
        total = LSA[s, SELF]
        other = None
        for slot in range(9):
            if slot != SELF:
                total = total + RS[s, slot]
            other = RO[s, slot] if other is None else other + RO[s, slot]
        at_0 = jnp.where(zh == 1, 1.0, 0.0).astype(F32)
        scale = (1.0 if first else 2.0) / HALF
        scaled = scale * SC[...] * jnp.stack([total[0] + at_0 * other, total[1] + (1.0 - at_0) * other])
        CS[s] = scaled
        SSA[s, SELF] = scaled
        neighbours(c, ("bo", "bs"), "start", False)

    def take_same(s, c):
        neighbours(c, ("bs",), "wait_recv", True)
        sh, sl = split(SSA[s].reshape(288, 128))
        SHA[:, 0:128] = sh
        SHA[:, 128:256] = sl

    def take_other(s, c):
        neighbours(c, ("bo",), "wait_recv", True)
        sh, sl = split(SSO[s].reshape(144, 128))
        SHO[:, 0:128] = sh
        SHO[:, 128:256] = sl

    def per_tile(b, with_other):
        r = dot_nn(SHA[...], WT[b])
        number = NIDX[b]
        pt = jnp.zeros((16, 256), F32)
        for i in range(9):
            for pair in range(2):
                k = 2 * i + pair
                pt = pt + jnp.where(number == 3 * i + pair, r[k * 16 : (k + 1) * 16], 0.0)
        if with_other:
            r = dot_nn(SHO[...], WT[b])
            for i in range(9):
                pt = pt + jnp.where(number == 3 * i + 2, r[i * 16 : (i + 1) * 16], 0.0)
        return pt

    def project(pt, b):
        mask = MKB[b]
        high = pt.astype(BF16).astype(F32)

        def spread(part):
            def one(p, o):
                row = jnp.broadcast_to(part[p * 4 + o : p * 4 + o + 1], (16, 256)).astype(BF16)
                return mask * jnp.concatenate([row] * 4, axis=0)

            return jnp.concatenate(
                [jnp.concatenate([one(p, o) for p in range(4)], axis=1) for o in range(4)], axis=0
            )

        wide = dot_nn(spread(high), PN[b])
        return wide[:, 0:128] + wide[:, 128:256] + dot_nn(spread(pt - high), PN[b, :, 0:128])

    def apply(s, b, with_other):
        y = Z[:, pl.ds(4 * b, 4)] + project(per_tile(b, with_other), b).reshape(4, 4, 16, 128)
        X[s + 2, :, pl.ds(4 + 4 * b, 4), 8:24, :] = y
        yh, yl = split(y)
        VH[:, pl.ds(4 * b, 4)] = yh
        VL[:, pl.ds(4 * b, 4)] = yl

    c = step_copies(0)
    take_own.wait()
    for v in values:
        v.wait_recv()
    send_halos(c)
    for v in parts:
        v.wait_recv()
    sums_for_other_half(0, c)
    sums_for_own_half(0, c)
    for v in cpl_y:
        v.wait_recv()
    group = 2 * (ix * 32)
    cpl_x = [
        start(set_copy(rows(group, 64), rows(group, 64), CP0 + 6 + j, dev((ix + j) % 4, iy, iz))) for j in (1, 3, 2)
    ]
    high, low = split(X[1, :, 4:20, 8:24, :])
    VH[...] = high
    VL[...] = low
    pack_x(0, c)
    for v in cpl_x:
        v.wait_recv()
    home2 = home_in[...]
    home = jnp.concatenate([home2[0:1], home2[1:2]], axis=1)
    home_row = 2 * lax.shift_right_logical(home, 6)
    rows256 = lax.broadcasted_iota(I32, (256, 256), 0)
    lane_hot = jnp.where(row64 == jnp.bitwise_and(home, 63), 1.0, 0.0).astype(F32)
    cb = CB[...]
    cb_1 = cb.astype(BF16)
    rest = cb - cb_1.astype(F32)
    cb_2 = rest.astype(BF16)
    cb_3 = (rest - cb_2.astype(F32)).astype(BF16)
    for r in range(2):
        pick = jnp.where(rows256 == home_row + r, 1.0, 0.0).astype(BF16)
        found = dot_tn(cb_1, pick) + dot_tn(cb_2, pick) + dot_tn(cb_3, pick)
        for p2 in range(2):
            line = jnp.sum(found[p2 * 64 : (p2 + 1) * 64] * lane_hot, axis=0, keepdims=True)
            p = 2 * r + p2
            for pair in range(2):
                SC[pair, p * 4 : (p + 1) * 4, :] = jnp.broadcast_to(line[:, pair * 128 : (pair + 1) * 128], (4, 128))

    scale_totals(0, c, True)

    up[0].wait_recv()
    on_up = start(set_copy(PF.at[below, half[0]], PF.at[below, half[0]], PF0 + 4, ring(1)))
    down[0].wait_recv()
    on_down = start(set_copy(PF.at[above, half[1]], PF.at[above, half[1]], PF0 + 5, ring(3)))
    take_pot.wait()
    for v in pots:
        v.wait_recv()
    stencil(0, c, True)
    take_same(0, c)
    take_other(0, c)
    apply(0, q, True)
    up[1].wait_recv()
    split_proj(below)
    apply(0, below, True)
    down[1].wait_recv()
    split_proj(above)
    apply(0, above, True)
    on_up.wait_recv()
    on_down.wait_recv()
    split_proj(across)
    apply(0, across, True)

    def block_sums(b):
        vh = VH[:, pl.ds(4 * b, 4)].reshape(256, 128)
        vl = VL[:, pl.ds(4 * b, 4)].reshape(256, 128)
        tile_sums(vh, vl, b, PART, b)

    def head(s):
        c = step_copies(s)
        send_halos(c)
        block_sums(edge_block)
        sums_for_other_half(s, c)

        def sums(j, _):
            block_sums((edge_block + j) % 4)
            return 0

        lax.fori_loop(1, 4, sums, 0)
        sums_for_own_half(s, c)
        pack_x(s, c)
        scale_totals(s, c, False)
        stencil(s, c, False)
        return c

    def step(s, _):
        c = head(s)
        take_same(s, c)

        def one(j, _):
            apply(s, (edge_block + j) % 4, False)
            return 0

        lax.fori_loop(1, 4, one, 0)
        take_other(s, c)
        apply(s, edge_block, True)
        return 0

    lax.fori_loop(1, STEPS - 1, step, 0)

    last = STEPS - 1
    c = head(last)
    outs_on = around(
        lambda block, o, n: Z.at[pl.ds(o, n), pl.ds(4 * block, 4)],
        lambda block, o, n: ZO.at[pl.ds(4 * block + o, n)],
        RLO,
        OU0,
    )
    take_same(last, c)
    take_other(last, c)
    finals = []
    for j in (2, 1, 3):
        b = (q + j) % 4
        PTS[pl.ds(b, 1)] = per_tile(b, True)[None]
        finals.append(start(set_copy(PTS.at[b], PTR.at[q], FT0 + j - 1, ring(j))))
    outs = outs_on()
    result = Z[:, pl.ds(4 * q, 4)] + project(per_tile(q, True), q).reshape(4, 4, 16, 128)
    out[pl.ds(4 * q, 4)] = result
    for v in outs:
        v.wait_recv()
    for index, j in ((1, 1), (2, 3), (0, 2)):
        finals[index].wait_recv()
        g = (q - j + 4) % 4
        out[pl.ds(4 * g, 4)] = ZO[pl.ds(4 * g, 4)] + project(PTR[g], q).reshape(4, 4, 16, 128)
    for v in sends:
        v.wait_send()

    def drain(s, _):
        c = step_copies(s)
        for name in ("xp", "xm", "z"):
            c[name].wait_send()
        when(iy > 0, c["yl"].wait_send)
        when(iy < 3, c["yh"].wait_send)
        neighbours(c, ("rs", "ro", "bs", "bo"), "wait_send", False)
        return 0

    lax.fori_loop(0, STEPS, drain, 0)


def per_device(orbitals, potential, tile_proj, tile_atom, tile_column, tile_count, atom_home, coupling):
    vmem = pl.BlockSpec(memory_space=pltpu.VMEM)
    hbm = pl.BlockSpec(memory_space=pltpu.HBM)
    smem = pl.BlockSpec(memory_space=pltpu.SMEM)
    return pl.pallas_call(
        kernel,
        out_shape=jax.ShapeDtypeStruct((16, 4, 16, 128), F32),
        in_specs=[hbm] * 5 + [smem] + [hbm] * 3,
        out_specs=vmem,
        scratch_shapes=[
            pltpu.VMEM((6, 4, 24, 32, 128), F32),
            pltpu.VMEM((4, 16, 16, 128), F32),
            pltpu.VMEM((4, 16, 16, 128), BF16),
            pltpu.VMEM((4, 16, 16, 128), BF16),
            pltpu.VMEM((4, 1024, 128), F32),
            pltpu.VMEM((4, 1024, 256), BF16),
            pltpu.VMEM((16, 16, 128), F32),
            pltpu.VMEM((4, 8, 256), I32),
            pltpu.VMEM((4, 64, 256), F32),
            pltpu.VMEM((4, 64, 256), BF16),
            pltpu.VMEM((4, 16, 256), I32),
            pltpu.VMEM((4, 27, 16, 256), BF16),
            pltpu.VMEM((4, 256, 256), BF16),
            pltpu.VMEM((18, 32, 1024), BF16),
            pltpu.VMEM((9, 32, 256), BF16),
            pltpu.VMEM((4, 9, 2, 16, 128), F32),
            pltpu.VMEM((4, 9, 16, 128), F32),
            pltpu.VMEM((4, 9, 2, 16, 128), F32),
            pltpu.VMEM((4, 9, 16, 128), F32),
            pltpu.VMEM((4, 2, 16, 128), F32),
            pltpu.VMEM((4, 9, 2, 16, 128), F32),
            pltpu.VMEM((4, 9, 16, 128), F32),
            pltpu.VMEM((288, 256), BF16),
            pltpu.VMEM((144, 256), BF16),
            pltpu.VMEM((2, 16, 128), F32),
            pltpu.VMEM((4, 8, 1024), F32),
            pltpu.VMEM((4, 8, 1024), F32),
            pltpu.VMEM((256, 128), F32),
            pltpu.VMEM((128, 256), BF16),
            pltpu.VMEM((4, 16, 256), F32),
            pltpu.VMEM((4, 16, 256), F32),
            pltpu.VMEM((4, 16, 256), F32),
            pltpu.VMEM((4, 16, 256), F32),
            pltpu.VMEM((16, 4, 16, 128), F32),
            pltpu.VMEM((16, 4, 16, 128), F32),
            pltpu.VMEM((2, 2, 4, 16, 128), F32),
            pltpu.VMEM((2, 2, 4, 16, 128), F32),
            pltpu.VMEM((1, 256), I32),
            pltpu.VMEM((1, 256), I32),
            pltpu.VMEM((2, 128), I32),
            pltpu.VMEM((4, 64), F32),
            pltpu.VMEM((144, 128), F32),
            pltpu.SemaphoreType.DMA((NSET,)),
            pltpu.SemaphoreType.DMA((NSET,)),
            pltpu.SemaphoreType.DMA((STEPS, NSEM)),
            pltpu.SemaphoreType.DMA((STEPS, NSEM)),
            pltpu.SemaphoreType.DMA((9,)),
        ],
        compiler_params=pltpu.CompilerParams(
            collective_id=0, has_side_effects=True, vmem_limit_bytes=60000 * 1024
        ),
        name="chebyshev",
    )(
        orbitals,
        potential,
        tile_proj.reshape(1024, 128),
        tile_atom.reshape(1, 256),
        tile_column.reshape(1, 256),
        tile_count,
        atom_home.reshape(64, 128),
        coupling.T,
        jnp.asarray(stencil_constants()),
    )


def solution(mesh):
    return jax.shard_map(
        per_device,
        mesh=mesh,
        in_specs=(
            P(None, "gz", "gy", "gx"),
            P("gz", "gy", "gx"),
            P(("gx", "gy", "gz"), None, None),
            P(("gx", "gy", "gz")),
            P(("gx", "gy", "gz")),
            P(("gx", "gy", "gz")),
            P(),
            P(("gx", "gy", "gz"), None),
        ),
        out_specs=P(None, "gz", "gy", "gx"),
        check_vma=False,
    )
```

```python
import jax
import jax.numpy as jnp
import numpy as np
from jax import lax
from jax.experimental import pallas as pl
from jax.experimental.pallas import tpu as pltpu
from jax.sharding import PartitionSpec as P

F32, BF16, I32 = jnp.float32, jnp.bfloat16, jnp.int32
STENCIL = (-205.0 / 72.0, 8.0 / 5.0, -1.0 / 5.0, 8.0 / 315.0, -1.0 / 560.0)
CENTER, HALF = 14.0, 10.0
STEPS = 4
DIRS = [(dx, dy) for dx in (-1, 0, 1) for dy in (-1, 0, 1)]
SELF = 4
XP, XM, YL, YH, ZH, RS0, RO0, BS0, BO0, NSEM = 0, 1, 2, 3, 4, 5, 14, 23, 32, 41
V0, PF0, PT0, ME0, CP0, PA0, OU0, FT0, NSET = 0, 6, 12, 15, 18, 28, 31, 37, 40


def stencil_constants():
    table = np.zeros((144, 128), np.float32)
    for x in range(128):
        for k in range(1, 5):
            if x + k < 128:
                table[x, x + k] = -0.5 * STENCIL[k]
            if x - k >= 0:
                table[x, x - k] = -0.5 * STENCIL[k]
    for j in range(4):
        table[128 + j, 124 + j] = 1.0
        table[132 + j, j] = 1.0
        for x in range(128):
            k = x + 4 - j
            if 1 <= k <= 4:
                table[136 + j, x] = -0.5 * STENCIL[k]
            k = 128 + j - x
            if 1 <= k <= 4:
                table[140 + j, x] = -0.5 * STENCIL[k]
    return table


def split(value):
    high = value.astype(BF16)
    return high, (value - high.astype(F32)).astype(BF16)


def dot_nt(a, b):
    return lax.dot_general(a, b, (((1,), (1,)), ((), ())), preferred_element_type=F32)


def dot_nn(a, b):
    return lax.dot_general(a, b, (((1,), (0,)), ((), ())), preferred_element_type=F32)


def dot_tn(a, b):
    return lax.dot_general(a, b, (((0,), (0,)), ((), ())), preferred_element_type=F32)


def kernel(
    orb, pot_in, tp, atom_hbm, column_hbm, count_in, home_hbm, cpl_hbm, table_hbm, out,
    X, Z, VH, VL, PF, PT, POT, META, MKB, NIDX, NMB, WT, LH, LHO, LSA, LSO, RS, RO, CS, CSO, SSA, SSO, SHA, SHO, SC, XS, XR, CB, CONST,
    PART, PART0, PTS, PTR, ZO, ORB, RL, RLO, atom_in, column_in, home_in, cpl_in, table,
    set_s, set_r, sem_s, sem_r, local_sem,
):
    ix, iy, iz = lax.axis_index("gx"), lax.axis_index("gy"), lax.axis_index("gz")
    zh, q = iz // 4, iz % 4
    oz = 1 - zh
    edge_block = 3 * oz
    below, above, across = (q + 3) % 4, (q + 1) % 4, (q + 2) % 4

    def dev(gx, gy, gz):
        return {"gx": gx, "gy": gy, "gz": gz}

    def ring(j):
        return dev(ix, iy, zh * 4 + (q + j) % 4)

    def near(dx, dy, half):
        return dev((ix + dx + 4) % 4, (iy + dy + 4) % 4, half * 4 + q)

    def exists(i):
        dx, dy = DIRS[i]
        return jnp.logical_and(
            jnp.logical_and(ix + dx >= 0, ix + dx <= 3), jnp.logical_and(iy + dy >= 0, iy + dy <= 3)
        )

    def copy(src, dst, s, r, to):
        return pltpu.make_async_remote_copy(
            src_ref=src, dst_ref=dst, send_sem=s, recv_sem=r, device_id=to, device_id_type=pl.DeviceIdType.MESH
        )

    barrier = pltpu.get_barrier_semaphore()
    peers = [near(dx, dy, half) for dx, dy in DIRS for half in (zh, oz)]
    peers = [p for i, p in enumerate(peers) if i != 2 * SELF]
    peers += [ring(j) for j in (1, 2, 3)]
    peers += [dev((ix + 2) % 4, iy, iz), dev(ix, (iy + 2) % 4, iz)]
    for peer in peers:
        pl.semaphore_signal(barrier, inc=1, device_id=peer, device_id_type=pl.DeviceIdType.MESH)
    take_proj = pltpu.make_async_copy(tp, PF, local_sem.at[0])
    take_orb = pltpu.make_async_copy(orb, ORB, local_sem.at[1])
    take_pot = pltpu.make_async_copy(pot_in, POT.at[pl.ds(4 * q, 4)], local_sem.at[2])
    take_own = pltpu.make_async_copy(
        orb.at[pl.ds(4 * q, 4)], X.at[1, :, pl.ds(4 + 4 * q, 4), pl.ds(8, 16), :], local_sem.at[3]
    )
    smalls = [
        pltpu.make_async_copy(src, dst, local_sem.at[4 + i])
        for i, (src, dst) in enumerate(
            (
                (atom_hbm, atom_in),
                (column_hbm, column_in),
                (cpl_hbm, cpl_in),
                (table_hbm, table),
                (home_hbm.at[pl.ds(2 * ((ix * 4 + iy) * 2 + zh), 2)], home_in),
            )
        )
    ]
    for c in smalls + [take_proj, take_orb, take_own, take_pot]:
        c.start()
    for c in smalls:
        c.wait()

    atom = atom_in[...]
    owner = lax.shift_right_logical(atom, 6)
    dx = lax.shift_right_logical(owner, 5) - ix + 1
    dy = jnp.bitwise_and(lax.shift_right_logical(owner, 3), 3) - iy + 1
    zb = jnp.bitwise_and(owner, 7) - 4 * zh
    pair = jnp.where(jnp.logical_and(zb >= 0, zb < 4), lax.shift_right_arithmetic(zb, 1), 2)
    number = (dx * 3 + dy) * 3 + pair
    lane = jnp.bitwise_and(zb, 1) * 64 + jnp.bitwise_and(atom, 63)
    column = jnp.where(lax.broadcasted_iota(I32, (1, 256), 1) < count_in[0], column_in[...], -1)
    META[pl.ds(q, 1)] = jnp.concatenate([number, lane, column] + [column] * 5, axis=0)[None]
    cpl = cpl_in[...]
    mine = 2 * ((ix * 4 + iy) * 8 + iz)
    CB[pl.ds(mine, 2), :] = jnp.concatenate(
        [jnp.concatenate([cpl[0:1], cpl[1:2]], axis=1), jnp.concatenate([cpl[2:3], cpl[3:4]], axis=1)], axis=0
    )

    row64 = lax.broadcasted_iota(I32, (64, 256), 0)
    row128 = lax.broadcasted_iota(I32, (128, 256), 0)

    def masks(b):
        mask = jnp.where(row64 == META[b, 2:3, :], 1.0, 0.0).astype(BF16)
        MKB[b, 0:64] = mask
        MKB[b, 64:128] = mask

    masks(q)

    def clear(i, _):
        X[i, :, pl.ds(20 * zh, 4)] = jnp.zeros((4, 4, 32, 128), F32)

        @pl.when(iy == 0)
        def _():
            X[i, :, 4:20, 0:8] = jnp.zeros((4, 16, 8, 128), F32)

        @pl.when(iy == 3)
        def _():
            X[i, :, 4:20, 24:32] = jnp.zeros((4, 16, 8, 128), F32)

        return 0

    lax.fori_loop(1, 5, clear, 0)

    def clear_sums(i, _):
        for slot in range(9):
            if slot != SELF:

                @pl.when(jnp.logical_not(exists(slot)))
                def _():
                    RS[i, slot] = jnp.zeros((2, 16, 128), F32)
                    RO[i, slot] = jnp.zeros((8, 128), F32)

        return 0

    lax.fori_loop(0, 4, clear_sums, 0)

    wx_h, wx_l = split(table[0:128, :])
    CONST[0:128, 0:128] = wx_h
    CONST[0:128, 128:256] = wx_l
    e2 = table[128:136, :].astype(BF16)
    edge_row = lax.broadcasted_iota(I32, (8, 128), 0)
    inside = jnp.where(
        edge_row < 4, jnp.where(ix > 0, 1.0, 0.0).astype(F32), jnp.where(ix < 3, 1.0, 0.0).astype(F32)
    )
    edge = table[136:144, :] * inside
    edge_h = edge.astype(BF16).astype(F32)
    edge_1 = jnp.concatenate([edge_h, edge_h], axis=0).astype(BF16)
    edge_2 = jnp.concatenate([edge - edge_h, edge - edge_h], axis=0).astype(BF16)

    take_proj.wait()
    for p in range(4):
        PT[q, p] = PF[pl.ds(p, 256, stride=4), :].T
    pl.semaphore_wait(barrier, len(peers))

    def field_block(index, block):
        return X.at[index, :, pl.ds(4 + 4 * block, 4), pl.ds(8, 16), :]

    sends = []

    def start(c):
        c.start()
        sends.append(c)
        return c

    def set_copy(src, dst, index, to):
        return copy(src, dst, set_s.at[index], set_r.at[index], to)

    def rows(first, count):
        return CB.at[pl.ds(first, count)]

    metas = [start(set_copy(META.at[q], META.at[q], ME0 + j - 1, ring(j))) for j in (1, 3, 2)]
    ring_cpl = [start(set_copy(rows(mine, 2), rows(mine, 2), CP0 + j - 1, ring(j))) for j in (1, 3, 2)]

    def around(source, target, relay, base):
        to_up = start(set_copy(source(across, 0, 2), relay.at[0], base, ring(1)))
        to_down = start(set_copy(source(across, 2, 2), relay.at[1], base + 1, ring(3)))
        near_up = start(set_copy(source(above, 0, 4), target(q, 0, 4), base + 2, ring(1)))
        near_down = start(set_copy(source(below, 0, 4), target(q, 0, 4), base + 3, ring(3)))

        def forward():
            to_up.wait_recv()
            far_up = start(set_copy(relay.at[0], target(below, 0, 2), base + 4, ring(1)))
            to_down.wait_recv()
            far_down = start(set_copy(relay.at[1], target(above, 2, 2), base + 5, ring(3)))
            return near_up, near_down, far_up, far_down

        return forward

    values_on = around(
        lambda block, o, n: orb.at[pl.ds(4 * block + o, n)],
        lambda block, o, n: X.at[1, pl.ds(o, n), pl.ds(4 + 4 * block, 4), pl.ds(8, 16), :],
        RL,
        V0,
    )

    def tile_sums(vh, vl, b, result, at):
        for o in range(4):
            r = dot_tn(jnp.concatenate([vh[o], vl[o]], axis=0), MKB[b])
            for p in range(4):
                result[at, pl.ds(p * 4 + o, 1), :] = jnp.sum(r * PT[b, p], axis=0, keepdims=True)

    take_orb.wait()

    def own_sums(g, _):
        vh, vl = split(ORB[pl.ds(4 * g, 4)].reshape(4, 64, 128))
        tile_sums(vh, vl, q, PART0, g)
        return 0

    lax.fori_loop(0, 4, own_sums, 0)
    values = values_on()
    parts = [start(set_copy(PART0.at[(q + j) % 4], PART.at[q], PA0 + j - 1, ring(j))) for j in (2, 1, 3)]
    half = [pl.ds(0, 2), pl.ds(2, 2)]
    up = [start(set_copy(PT.at[q, half[h]], PT.at[q, half[h]], PF0 + h, ring(1))) for h in (0, 1)]
    down = [start(set_copy(PT.at[q, half[h]], PT.at[q, half[h]], PF0 + 3 - h, ring(3))) for h in (1, 0)]
    pots = [start(set_copy(pot_in, POT.at[pl.ds(4 * q, 4)], PT0 + j - 1, ring(j))) for j in (1, 3, 2)]
    PART[pl.ds(q, 1)] = PART0[pl.ds(q, 1)]

    for c in ring_cpl:
        c.wait_recv()
    group = 2 * ((ix * 4 + iy) * 8 + zh * 4)
    flip = start(set_copy(rows(group, 8), rows(group, 8), CP0 + 3, dev(ix, iy, oz * 4 + q)))

    for c in metas:
        c.wait_recv()
    masks(below)
    masks(above)
    masks(across)
    for b in range(4):
        index = META[b]
        hot = jnp.where(row128 == index[1:2, :], 1.0, 0.0).astype(BF16)
        WT[b, 0:128] = hot
        WT[b, 128:256] = hot
        number = jnp.broadcast_to(index[0:1, :], (16, 256))
        NIDX[b] = number
        for n in range(27):
            NMB[b, n] = jnp.where(number == n, 1.0, 0.0).astype(BF16)

    flip.wait_recv()
    group = 2 * ((ix * 4 + iy) * 8)
    cpl_y = [
        start(set_copy(rows(group, 16), rows(group, 16), CP0 + 3 + j, dev(ix, (iy + j) % 4, iz))) for j in (1, 3, 2)
    ]

    def step_copies(s):
        cur = s + 1

        def sc(src, dst, index, to):
            return copy(src, dst, sem_s.at[s, index], sem_r.at[s, index], to)

        c = {}
        c["xp"] = sc(XS.at[s, pl.ds(0, 4)], XR.at[s, pl.ds(0, 4)], XP, dev((ix + 1) % 4, iy, iz))
        c["xm"] = sc(XS.at[s, pl.ds(4, 4)], XR.at[s, pl.ds(4, 4)], XM, dev((ix + 3) % 4, iy, iz))
        inner = pl.ds(4, 16)
        c["yl"] = sc(
            X.at[cur, :, inner, pl.ds(8, 4), :], X.at[cur, :, inner, pl.ds(24, 4), :], YL, dev(ix, (iy + 3) % 4, iz)
        )
        c["yh"] = sc(
            X.at[cur, :, inner, pl.ds(20, 4), :], X.at[cur, :, inner, pl.ds(4, 4), :], YH, dev(ix, (iy + 1) % 4, iz)
        )
        c["z"] = sc(
            X.at[cur, :, pl.ds(4 + 12 * oz, 4), pl.ds(8, 16), :],
            X.at[cur, :, pl.ds(20 * zh, 4), pl.ds(8, 16), :],
            ZH,
            dev(ix, iy, oz * 4 + q),
        )
        for i, (dx, dy) in enumerate(DIRS):
            slot = 8 - i
            if i != SELF:
                c["rs", i] = sc(LSA.at[s, i], RS.at[s, slot], RS0 + slot, near(dx, dy, zh))
                c["bs", i] = sc(CS.at[s], SSA.at[s, slot], BS0 + slot, near(dx, dy, zh))
            c["ro", i] = sc(LSO.at[s, i], RO.at[s, slot], RO0 + slot, near(dx, dy, oz))
            c["bo", i] = sc(CSO.at[s], SSO.at[s, slot], BO0 + slot, near(dx, dy, oz))
        return c

    def when(condition, action):
        @pl.when(condition)
        def _():
            action()

    def neighbours(c, names, action, mirrored):
        for i in range(9):
            def both(i=i):
                for name in names:
                    if (name, i) in c:
                        getattr(c[name, i], action)()

            if i == SELF:
                both()
            else:
                when(exists(8 - i if mirrored else i), both)

    def send_y(c):
        when(iy > 0, c["yl"].start)
        when(iy < 3, c["yh"].start)

    def pack_x(s, c):
        vh_all = VH[...].reshape(1024, 128)
        vl_all = VL[...].reshape(1024, 128)
        XS[s] = dot_nt(e2, vh_all) + dot_nt(e2, vl_all)
        xp = dot_nt(jnp.concatenate([vh_all, vh_all], axis=1), CONST[...]) + dot_nt(vl_all, CONST[:, 0:128])
        Z[...] = xp.reshape(4, 16, 16, 128)
        c["xp"].start()
        c["xm"].start()

    def turn(value):
        return pltpu.roll(value.reshape(-1, 128), 64, 1).reshape(value.shape)

    def sums_for_other_half(s, c):
        ph, pl_ = split(PART[edge_block])
        for i in range(9):
            m = NMB[edge_block, 3 * i + 2]
            LHO[i, 0:16] = ph * m
            LHO[i, 16:32] = pl_ * m
        sums = dot_nt(LHO[...].reshape(288, 256), WT[edge_block, 0:128]).reshape(9, 32, 128)
        sums = sums[:, 0:16] + sums[:, 16:32]
        LSO[s] = sums[:, 0:8] + turn(sums[:, 8:16])
        neighbours(c, ("ro",), "start", False)

    def sums_for_own_half(s, c):
        for b in range(4):
            ph, pl_ = split(PART[b])
            for i in range(9):
                for pair in range(2):
                    m = NMB[b, 3 * i + pair]
                    LH[2 * i + pair, 0:16, b * 256 : (b + 1) * 256] = ph * m
                    LH[2 * i + pair, 16:32, b * 256 : (b + 1) * 256] = pl_ * m
        sums = None
        for b in range(4):
            lhs = LH[:, :, b * 256 : (b + 1) * 256].reshape(576, 256)
            term = dot_nt(lhs, WT[b, 0:128])
            sums = term if sums is None else sums + term
        sums = sums.reshape(18, 32, 128)
        LSA[s] = (sums[:, 0:16] + sums[:, 16:32]).reshape(9, 2, 16, 128)
        neighbours(c, ("rs",), "start", False)

    def stencil(s, c, first):
        c["xp"].wait_recv()
        c["xm"].wait_recv()
        xr = XR[s]
        xr_h = xr.astype(BF16).astype(F32)
        faces = jnp.concatenate([xr_h, xr - xr_h], axis=0).astype(BF16)
        Z[...] = Z[...] + (dot_tn(faces, edge_1) + dot_tn(faces, edge_2)).reshape(4, 16, 16, 128)
        c["z"].wait_recv()
        when(iy > 0, c["yh"].wait_recv)
        when(iy < 3, c["yl"].wait_recv)
        cur = s + 1
        scale = (1.0 if first else 2.0) / HALF

        def line(i, _):
            o = i // 16
            z = i % 16
            v0 = X[cur, o, z + 4, 8:24, :]
            acc = Z[o, z] + v0 * (POT[z] + (-1.5 * STENCIL[0] - CENTER))
            for k in range(1, 5):
                around = (X[cur, o, z + 4 - k, 8:24, :] + X[cur, o, z + 4 + k, 8:24, :]) + (
                    X[cur, o, z + 4, 8 - k : 24 - k, :] + X[cur, o, z + 4, 8 + k : 24 + k, :]
                )
                acc = acc + (-0.5 * STENCIL[k]) * around
            acc = scale * acc
            Z[o, z] = acc if first else acc - X[s, o, z + 4, 8:24, :]
            return 0

        lax.fori_loop(0, 64, line, 0, unroll=4)

    def scale_totals(s, c, first):
        neighbours(c, ("rs", "ro"), "wait_recv", True)
        total = LSA[s, SELF]
        other = None
        for slot in range(9):
            if slot != SELF:
                total = total + RS[s, slot]
            other = RO[s, slot] if other is None else other + RO[s, slot]
        theirs = lax.broadcasted_iota(I32, (8, 128), 1) // 64 == oz
        other = jnp.concatenate([jnp.where(theirs, other, 0.0), jnp.where(theirs, turn(other), 0.0)], axis=0)
        at_0 = jnp.where(zh == 1, 1.0, 0.0).astype(F32)
        scale = (1.0 if first else 2.0) / HALF
        scaled = scale * SC[...] * jnp.stack([total[0] + at_0 * other, total[1] + (1.0 - at_0) * other])
        CS[s] = scaled
        edge_pair = at_0 * scaled[0] + (1.0 - at_0) * scaled[1]
        CSO[s] = jnp.where(theirs, edge_pair[0:8], turn(edge_pair[8:16]))
        SSA[s, SELF] = scaled
        neighbours(c, ("bo", "bs"), "start", False)

    def take_same(s, c):
        neighbours(c, ("bs",), "wait_recv", True)
        sh, sl = split(SSA[s].reshape(288, 128))
        SHA[:, 0:128] = sh
        SHA[:, 128:256] = sl

    def take_other(s, c):
        neighbours(c, ("bo",), "wait_recv", True)
        packed = SSO[s]
        sh, sl = split(jnp.concatenate([packed, turn(packed)], axis=1).reshape(144, 128))
        SHO[:, 0:128] = sh
        SHO[:, 128:256] = sl

    def per_tile(b, with_other):
        r = dot_nn(SHA[...], WT[b])
        number = NIDX[b]
        pt = jnp.zeros((16, 256), F32)
        for i in range(9):
            for pair in range(2):
                k = 2 * i + pair
                pt = pt + jnp.where(number == 3 * i + pair, r[k * 16 : (k + 1) * 16], 0.0)
        if with_other:
            r = dot_nn(SHO[...], WT[b])
            for i in range(9):
                pt = pt + jnp.where(number == 3 * i + 2, r[i * 16 : (i + 1) * 16], 0.0)
        return pt

    def project(pt, b):
        mask = MKB[b, 0:64]
        results = []
        for o in range(4):
            r = PT[b, 0] * pt[o : o + 1]
            for p in range(1, 4):
                r = r + PT[b, p] * pt[p * 4 + o : p * 4 + o + 1]
            rh, rl = split(r)
            results.append(dot_nt(mask, rh) + dot_nt(mask, rl))
        return jnp.stack(results)

    def apply(s, b, with_other):
        y = Z[:, pl.ds(4 * b, 4)] + project(per_tile(b, with_other), b).reshape(4, 4, 16, 128)
        X[s + 2, :, pl.ds(4 + 4 * b, 4), 8:24, :] = y
        yh, yl = split(y)
        VH[:, pl.ds(4 * b, 4)] = yh
        VL[:, pl.ds(4 * b, 4)] = yl

    c = step_copies(0)
    take_own.wait()
    for v in values:
        v.wait_recv()
    c["z"].start()
    send_y(c)
    for v in parts:
        v.wait_recv()
    sums_for_other_half(0, c)
    sums_for_own_half(0, c)
    for v in cpl_y:
        v.wait_recv()
    group = 2 * (ix * 32)
    cpl_x = [
        start(set_copy(rows(group, 64), rows(group, 64), CP0 + 6 + j, dev((ix + j) % 4, iy, iz))) for j in (1, 3, 2)
    ]
    high, low = split(X[1, :, 4:20, 8:24, :])
    VH[...] = high
    VL[...] = low
    pack_x(0, c)
    for v in cpl_x:
        v.wait_recv()
    home2 = home_in[...]
    home = jnp.concatenate([home2[0:1], home2[1:2]], axis=1)
    home_row = 2 * lax.shift_right_logical(home, 6)
    rows256 = lax.broadcasted_iota(I32, (256, 256), 0)
    lane_hot = jnp.where(row64 == jnp.bitwise_and(home, 63), 1.0, 0.0).astype(F32)
    cb = CB[...]
    cb_1 = cb.astype(BF16)
    rest = cb - cb_1.astype(F32)
    cb_2 = rest.astype(BF16)
    cb_3 = (rest - cb_2.astype(F32)).astype(BF16)
    for r in range(2):
        pick = jnp.where(rows256 == home_row + r, 1.0, 0.0).astype(BF16)
        found = dot_tn(cb_1, pick) + dot_tn(cb_2, pick) + dot_tn(cb_3, pick)
        for p2 in range(2):
            line = jnp.sum(found[p2 * 64 : (p2 + 1) * 64] * lane_hot, axis=0, keepdims=True)
            p = 2 * r + p2
            for pair in range(2):
                SC[pair, p * 4 : (p + 1) * 4, :] = jnp.broadcast_to(line[:, pair * 128 : (pair + 1) * 128], (4, 128))

    scale_totals(0, c, True)

    up[0].wait_recv()
    on_up = start(set_copy(PT.at[below, half[0]], PT.at[below, half[0]], PF0 + 4, ring(1)))
    down[0].wait_recv()
    on_down = start(set_copy(PT.at[above, half[1]], PT.at[above, half[1]], PF0 + 5, ring(3)))
    take_pot.wait()
    for v in pots:
        v.wait_recv()
    stencil(0, c, True)
    def block_sums(b):
        vh = VH[:, pl.ds(4 * b, 4)].reshape(4, 64, 128)
        vl = VL[:, pl.ds(4 * b, 4)].reshape(4, 64, 128)
        tile_sums(vh, vl, b, PART, b)

    def rest_of_step(s, c):
        send_y(c)
        sums_for_own_half(s, c)
        pack_x(s, c)
        scale_totals(s, c, False)
        stencil(s, c, False)

    take_same(0, c)
    take_other(0, c)
    c = step_copies(1)
    for b, arrivals in ((q, ()), (below, (up[1],)), (above, (down[1],)), (across, (on_up, on_down))):
        for v in arrivals:
            v.wait_recv()
        apply(0, b, True)
        block_sums(b)
    c["z"].start()
    sums_for_other_half(1, c)
    rest_of_step(1, c)

    def step(s, _):
        before = step_copies(s - 1)
        c = step_copies(s)
        take_same(s - 1, before)
        take_other(s - 1, before)
        apply(s - 1, edge_block, True)
        c["z"].start()
        block_sums(edge_block)
        sums_for_other_half(s, c)

        def one(j, _):
            b = (edge_block + j) % 4
            apply(s - 1, b, False)
            block_sums(b)
            return 0

        lax.fori_loop(1, 4, one, 0)
        rest_of_step(s, c)
        return 0

    lax.fori_loop(2, STEPS, step, 0)

    last = STEPS - 1
    c = step_copies(last)
    outs_on = around(
        lambda block, o, n: Z.at[pl.ds(o, n), pl.ds(4 * block, 4)],
        lambda block, o, n: ZO.at[pl.ds(4 * block + o, n)],
        RLO,
        OU0,
    )
    take_same(last, c)
    take_other(last, c)
    finals = []
    for j in (2, 1, 3):
        b = (q + j) % 4
        PTS[pl.ds(b, 1)] = per_tile(b, True)[None]
        finals.append(start(set_copy(PTS.at[b], PTR.at[q], FT0 + j - 1, ring(j))))
    outs = outs_on()
    result = Z[:, pl.ds(4 * q, 4)] + project(per_tile(q, True), q).reshape(4, 4, 16, 128)
    out[pl.ds(4 * q, 4)] = result
    for v in outs:
        v.wait_recv()
    for index, j in ((1, 1), (2, 3), (0, 2)):
        finals[index].wait_recv()
        g = (q - j + 4) % 4
        out[pl.ds(4 * g, 4)] = ZO[pl.ds(4 * g, 4)] + project(PTR[g], q).reshape(4, 4, 16, 128)
    for v in sends:
        v.wait_send()

    def drain(s, _):
        c = step_copies(s)
        for name in ("xp", "xm", "z"):
            c[name].wait_send()
        when(iy > 0, c["yl"].wait_send)
        when(iy < 3, c["yh"].wait_send)
        neighbours(c, ("rs", "ro", "bs", "bo"), "wait_send", False)
        return 0

    lax.fori_loop(0, STEPS, drain, 0)


def per_device(orbitals, potential, tile_proj, tile_atom, tile_column, tile_count, atom_home, coupling):
    vmem = pl.BlockSpec(memory_space=pltpu.VMEM)
    hbm = pl.BlockSpec(memory_space=pltpu.HBM)
    smem = pl.BlockSpec(memory_space=pltpu.SMEM)
    return pl.pallas_call(
        kernel,
        out_shape=jax.ShapeDtypeStruct((16, 4, 16, 128), F32),
        in_specs=[hbm] * 5 + [smem] + [hbm] * 3,
        out_specs=vmem,
        scratch_shapes=[
            pltpu.VMEM((6, 4, 24, 32, 128), F32),
            pltpu.VMEM((4, 16, 16, 128), F32),
            pltpu.VMEM((4, 16, 16, 128), BF16),
            pltpu.VMEM((4, 16, 16, 128), BF16),
            pltpu.VMEM((1024, 128), F32),
            pltpu.VMEM((4, 4, 128, 256), F32),
            pltpu.VMEM((16, 16, 128), F32),
            pltpu.VMEM((4, 8, 256), I32),
            pltpu.VMEM((4, 128, 256), BF16),
            pltpu.VMEM((4, 16, 256), I32),
            pltpu.VMEM((4, 27, 16, 256), BF16),
            pltpu.VMEM((4, 256, 256), BF16),
            pltpu.VMEM((18, 32, 1024), BF16),
            pltpu.VMEM((9, 32, 256), BF16),
            pltpu.VMEM((4, 9, 2, 16, 128), F32),
            pltpu.VMEM((4, 9, 8, 128), F32),
            pltpu.VMEM((4, 9, 2, 16, 128), F32),
            pltpu.VMEM((4, 9, 8, 128), F32),
            pltpu.VMEM((4, 2, 16, 128), F32),
            pltpu.VMEM((4, 8, 128), F32),
            pltpu.VMEM((4, 9, 2, 16, 128), F32),
            pltpu.VMEM((4, 9, 8, 128), F32),
            pltpu.VMEM((288, 256), BF16),
            pltpu.VMEM((144, 256), BF16),
            pltpu.VMEM((2, 16, 128), F32),
            pltpu.VMEM((4, 8, 1024), F32),
            pltpu.VMEM((4, 8, 1024), F32),
            pltpu.VMEM((256, 128), F32),
            pltpu.VMEM((128, 256), BF16),
            pltpu.VMEM((4, 16, 256), F32),
            pltpu.VMEM((4, 16, 256), F32),
            pltpu.VMEM((4, 16, 256), F32),
            pltpu.VMEM((4, 16, 256), F32),
            pltpu.VMEM((16, 4, 16, 128), F32),
            pltpu.VMEM((16, 4, 16, 128), F32),
            pltpu.VMEM((2, 2, 4, 16, 128), F32),
            pltpu.VMEM((2, 2, 4, 16, 128), F32),
            pltpu.VMEM((1, 256), I32),
            pltpu.VMEM((1, 256), I32),
            pltpu.VMEM((2, 128), I32),
            pltpu.VMEM((4, 64), F32),
            pltpu.VMEM((144, 128), F32),
            pltpu.SemaphoreType.DMA((NSET,)),
            pltpu.SemaphoreType.DMA((NSET,)),
            pltpu.SemaphoreType.DMA((STEPS, NSEM)),
            pltpu.SemaphoreType.DMA((STEPS, NSEM)),
            pltpu.SemaphoreType.DMA((9,)),
        ],
        compiler_params=pltpu.CompilerParams(
            collective_id=0, has_side_effects=True, vmem_limit_bytes=60000 * 1024
        ),
        name="chebyshev",
    )(
        orbitals,
        potential,
        tile_proj.reshape(1024, 128),
        tile_atom.reshape(1, 256),
        tile_column.reshape(1, 256),
        tile_count,
        atom_home.reshape(64, 128),
        coupling.T,
        jnp.asarray(stencil_constants()),
    )


def solution(mesh):
    return jax.shard_map(
        per_device,
        mesh=mesh,
        in_specs=(
            P(None, "gz", "gy", "gx"),
            P("gz", "gy", "gx"),
            P(("gx", "gy", "gz"), None, None),
            P(("gx", "gy", "gz")),
            P(("gx", "gy", "gz")),
            P(("gx", "gy", "gz")),
            P(),
            P(("gx", "gy", "gz"), None),
        ),
        out_specs=P(None, "gz", "gy", "gx"),
        check_vma=False,
    )
```

```python
import jax
import jax.numpy as jnp
import numpy as np
from jax import lax
from jax.experimental import pallas as pl
from jax.experimental.pallas import tpu as pltpu
from jax.sharding import PartitionSpec as P

F32, BF16, I32 = jnp.float32, jnp.bfloat16, jnp.int32
STENCIL = (-205.0 / 72.0, 8.0 / 5.0, -1.0 / 5.0, 8.0 / 315.0, -1.0 / 560.0)
CENTER, HALF = 14.0, 10.0
STEPS = 4
HALVES = 2
DIRS = [(dx, dy) for dx in (-1, 0, 1) for dy in (-1, 0, 1)]
SELF = 4
XP, XM, YL, YH, ZH, RS0, RO0, BS0, BO0, NSEM = 0, 1, 2, 3, 4, 5, 14, 23, 32, 41
V0, PF0, PT0, ME0, CP0, PA0, OU0, FT0, NSET = 0, 6, 12, 15, 18, 28, 31, 37, 43


def stencil_constants():
    table = np.zeros((144, 128), np.float32)
    for x in range(128):
        for k in range(1, 5):
            if x + k < 128:
                table[x, x + k] = -0.5 * STENCIL[k]
            if x - k >= 0:
                table[x, x - k] = -0.5 * STENCIL[k]
    for j in range(4):
        table[128 + j, 124 + j] = 1.0
        table[132 + j, j] = 1.0
        for x in range(128):
            k = x + 4 - j
            if 1 <= k <= 4:
                table[136 + j, x] = -0.5 * STENCIL[k]
            k = 128 + j - x
            if 1 <= k <= 4:
                table[140 + j, x] = -0.5 * STENCIL[k]
    return table


def split(value):
    high = value.astype(BF16)
    return high, (value - high.astype(F32)).astype(BF16)


def dot_nt(a, b):
    return lax.dot_general(a, b, (((1,), (1,)), ((), ())), preferred_element_type=F32)


def dot_nn(a, b):
    return lax.dot_general(a, b, (((1,), (0,)), ((), ())), preferred_element_type=F32)


def dot_tn(a, b):
    return lax.dot_general(a, b, (((0,), (0,)), ((), ())), preferred_element_type=F32)


def kernel(
    orb, pot_in, tp, atom_hbm, column_hbm, count_in, home_hbm, cpl_hbm, table_hbm, out,
    X, Z, VH, VL, PF, PT, POT, META, MKB, NIDX, NMB, WT, LH, LHO, LSA, LSO, RS, RO, CS, CSO, SSA, SSO, SHA, SHO, SC, XS, XR, CB, CONST,
    PART, PART0, PTS, PTR, ZO, ORB, RL, RLO, atom_in, column_in, home_in, cpl_in, table,
    set_s, set_r, sem_s, sem_r, local_sem,
):
    ix, iy, iz = lax.axis_index("gx"), lax.axis_index("gy"), lax.axis_index("gz")
    zh, q = iz // 4, iz % 4
    oz = 1 - zh
    edge_block = 3 * oz
    below, above, across = (q + 3) % 4, (q + 1) % 4, (q + 2) % 4

    def dev(gx, gy, gz):
        return {"gx": gx, "gy": gy, "gz": gz}

    def ring(j):
        return dev(ix, iy, zh * 4 + (q + j) % 4)

    def near(dx, dy, half):
        return dev((ix + dx + 4) % 4, (iy + dy + 4) % 4, half * 4 + q)

    def exists(i):
        dx, dy = DIRS[i]
        return jnp.logical_and(
            jnp.logical_and(ix + dx >= 0, ix + dx <= 3), jnp.logical_and(iy + dy >= 0, iy + dy <= 3)
        )

    def copy(src, dst, s, r, to):
        return pltpu.make_async_remote_copy(
            src_ref=src, dst_ref=dst, send_sem=s, recv_sem=r, device_id=to, device_id_type=pl.DeviceIdType.MESH
        )

    barrier = pltpu.get_barrier_semaphore()
    peers = [near(dx, dy, half) for dx, dy in DIRS for half in (zh, oz)]
    peers = [p for i, p in enumerate(peers) if i != 2 * SELF]
    peers += [ring(j) for j in (1, 2, 3)]
    peers += [dev((ix + 2) % 4, iy, iz), dev(ix, (iy + 2) % 4, iz)]
    for peer in peers:
        pl.semaphore_signal(barrier, inc=1, device_id=peer, device_id_type=pl.DeviceIdType.MESH)
    take_proj = pltpu.make_async_copy(tp, PF, local_sem.at[0])
    take_orb = pltpu.make_async_copy(orb, ORB, local_sem.at[1])
    take_pot = pltpu.make_async_copy(pot_in, POT.at[pl.ds(4 * q, 4)], local_sem.at[2])
    take_own = pltpu.make_async_copy(
        orb.at[pl.ds(4 * q, 4)], X.at[1, :, pl.ds(4 + 4 * q, 4), pl.ds(8, 16), :], local_sem.at[3]
    )
    smalls = [
        pltpu.make_async_copy(src, dst, local_sem.at[4 + i])
        for i, (src, dst) in enumerate(
            (
                (atom_hbm, atom_in),
                (column_hbm, column_in),
                (cpl_hbm, cpl_in),
                (table_hbm, table),
                (home_hbm.at[pl.ds(2 * ((ix * 4 + iy) * 2 + zh), 2)], home_in),
            )
        )
    ]
    for c in smalls + [take_proj, take_orb, take_own, take_pot]:
        c.start()
    for c in smalls:
        c.wait()

    atom = atom_in[...]
    owner = lax.shift_right_logical(atom, 6)
    dx = lax.shift_right_logical(owner, 5) - ix + 1
    dy = jnp.bitwise_and(lax.shift_right_logical(owner, 3), 3) - iy + 1
    zb = jnp.bitwise_and(owner, 7) - 4 * zh
    pair = jnp.where(jnp.logical_and(zb >= 0, zb < 4), lax.shift_right_arithmetic(zb, 1), 2)
    number = (dx * 3 + dy) * 3 + pair
    lane = jnp.bitwise_and(zb, 1) * 64 + jnp.bitwise_and(atom, 63)
    column = jnp.where(lax.broadcasted_iota(I32, (1, 256), 1) < count_in[0], column_in[...], -1)
    META[pl.ds(q, 1)] = jnp.concatenate([number, lane, column] + [column] * 5, axis=0)[None]
    cpl = cpl_in[...]
    mine = 2 * ((ix * 4 + iy) * 8 + iz)
    CB[pl.ds(mine, 2), :] = jnp.concatenate(
        [jnp.concatenate([cpl[0:1], cpl[1:2]], axis=1), jnp.concatenate([cpl[2:3], cpl[3:4]], axis=1)], axis=0
    )

    row64 = lax.broadcasted_iota(I32, (64, 256), 0)
    row128 = lax.broadcasted_iota(I32, (128, 256), 0)

    def masks(b):
        mask = jnp.where(row64 == META[b, 2:3, :], 1.0, 0.0).astype(BF16)
        MKB[b, 0:64] = mask
        MKB[b, 64:128] = mask

    masks(q)

    def clear(i, _):
        X[i, :, pl.ds(20 * zh, 4)] = jnp.zeros((4, 4, 32, 128), F32)

        @pl.when(iy == 0)
        def _():
            X[i, :, 4:20, 0:8] = jnp.zeros((4, 16, 8, 128), F32)

        @pl.when(iy == 3)
        def _():
            X[i, :, 4:20, 24:32] = jnp.zeros((4, 16, 8, 128), F32)

        return 0

    lax.fori_loop(1, 5, clear, 0)

    def clear_sums(i, _):
        for slot in range(9):
            if slot != SELF:

                @pl.when(jnp.logical_not(exists(slot)))
                def _():
                    RS[i, :, slot] = jnp.zeros((2, 2, 8, 128), F32)
                    RO[i, :, slot] = jnp.zeros((2, 4, 128), F32)

        return 0

    lax.fori_loop(0, 4, clear_sums, 0)

    wx_h, wx_l = split(table[0:128, :])
    CONST[0:128, 0:128] = wx_h
    CONST[0:128, 128:256] = wx_l
    e2 = table[128:136, :].astype(BF16)
    edge_row = lax.broadcasted_iota(I32, (8, 128), 0)
    inside = jnp.where(
        edge_row < 4, jnp.where(ix > 0, 1.0, 0.0).astype(F32), jnp.where(ix < 3, 1.0, 0.0).astype(F32)
    )
    edge = table[136:144, :] * inside
    edge_h = edge.astype(BF16).astype(F32)
    edge_1 = jnp.concatenate([edge_h, edge_h], axis=0).astype(BF16)
    edge_2 = jnp.concatenate([edge - edge_h, edge - edge_h], axis=0).astype(BF16)

    take_proj.wait()
    for p in range(4):
        PT[q, p] = PF[pl.ds(p, 256, stride=4), :].T
    pl.semaphore_wait(barrier, len(peers))

    def field_block(index, block):
        return X.at[index, :, pl.ds(4 + 4 * block, 4), pl.ds(8, 16), :]

    sends = []

    def start(c):
        c.start()
        sends.append(c)
        return c

    def set_copy(src, dst, index, to):
        return copy(src, dst, set_s.at[index], set_r.at[index], to)

    def rows(first, count):
        return CB.at[pl.ds(first, count)]

    metas = [start(set_copy(META.at[q], META.at[q], ME0 + j - 1, ring(j))) for j in (1, 3, 2)]
    ring_cpl = [start(set_copy(rows(mine, 2), rows(mine, 2), CP0 + j - 1, ring(j))) for j in (1, 3, 2)]

    def around(source, target, relay, base):
        to_up = start(set_copy(source(across, 0, 2), relay.at[0], base, ring(1)))
        to_down = start(set_copy(source(across, 2, 2), relay.at[1], base + 1, ring(3)))
        near_up = start(set_copy(source(above, 0, 4), target(q, 0, 4), base + 2, ring(1)))
        near_down = start(set_copy(source(below, 0, 4), target(q, 0, 4), base + 3, ring(3)))

        def forward():
            to_up.wait_recv()
            far_up = start(set_copy(relay.at[0], target(below, 0, 2), base + 4, ring(1)))
            to_down.wait_recv()
            far_down = start(set_copy(relay.at[1], target(above, 2, 2), base + 5, ring(3)))
            return near_up, near_down, far_up, far_down

        return forward

    values_on = around(
        lambda block, o, n: orb.at[pl.ds(4 * block + o, n)],
        lambda block, o, n: X.at[1, pl.ds(o, n), pl.ds(4 + 4 * block, 4), pl.ds(8, 16), :],
        RL,
        V0,
    )

    def tile_sums(vh, vl, b, result, at, h):
        for o in range(2):
            r = dot_tn(jnp.concatenate([vh[o], vl[o]], axis=0), MKB[b])
            for p in range(4):
                result[at, h, pl.ds(p * 2 + o, 1), :] = jnp.sum(r * PT[b, p], axis=0, keepdims=True)

    take_orb.wait()

    def own_sums(g, _):
        for h in range(HALVES):
            vh, vl = split(ORB[pl.ds(4 * g + 2 * h, 2)].reshape(2, 64, 128))
            tile_sums(vh, vl, q, PART0, g, h)
        return 0

    lax.fori_loop(0, 4, own_sums, 0)
    values = values_on()
    parts = [start(set_copy(PART0.at[(q + j) % 4], PART.at[q], PA0 + j - 1, ring(j))) for j in (2, 1, 3)]
    half = [pl.ds(0, 2), pl.ds(2, 2)]
    up = [start(set_copy(PT.at[q, half[h]], PT.at[q, half[h]], PF0 + h, ring(1))) for h in (0, 1)]
    down = [start(set_copy(PT.at[q, half[h]], PT.at[q, half[h]], PF0 + 3 - h, ring(3))) for h in (1, 0)]
    pots = [start(set_copy(pot_in, POT.at[pl.ds(4 * q, 4)], PT0 + j - 1, ring(j))) for j in (1, 3, 2)]
    PART[pl.ds(q, 1)] = PART0[pl.ds(q, 1)]

    for c in ring_cpl:
        c.wait_recv()
    group = 2 * ((ix * 4 + iy) * 8 + zh * 4)
    flip = start(set_copy(rows(group, 8), rows(group, 8), CP0 + 3, dev(ix, iy, oz * 4 + q)))

    for c in metas:
        c.wait_recv()
    masks(below)
    masks(above)
    masks(across)
    for b in range(4):
        index = META[b]
        hot = jnp.where(row128 == index[1:2, :], 1.0, 0.0).astype(BF16)
        WT[b, 0:128] = hot
        WT[b, 128:256] = hot
        number = jnp.broadcast_to(index[0:1, :], (16, 256))
        NIDX[b] = number
        for n in range(27):
            NMB[b, n] = jnp.where(number == n, 1.0, 0.0).astype(BF16)

    flip.wait_recv()
    group = 2 * ((ix * 4 + iy) * 8)
    cpl_y = [
        start(set_copy(rows(group, 16), rows(group, 16), CP0 + 3 + j, dev(ix, (iy + j) % 4, iz))) for j in (1, 3, 2)
    ]

    def step_copies(s, h):
        cur = s + 1
        pair_of = pl.ds(2 * h, 2)

        def sc(src, dst, index, to):
            return copy(src, dst, sem_s.at[s, h * NSEM + index], sem_r.at[s, h * NSEM + index], to)

        c = {}
        c["xp"] = sc(XS.at[s, h, pl.ds(0, 4)], XR.at[s, h, pl.ds(0, 4)], XP, dev((ix + 1) % 4, iy, iz))
        c["xm"] = sc(XS.at[s, h, pl.ds(4, 4)], XR.at[s, h, pl.ds(4, 4)], XM, dev((ix + 3) % 4, iy, iz))
        inner = pl.ds(4, 16)

        def y_rows(first):
            return X.at[cur, pair_of, inner, pl.ds(first, 4), :]

        c["yl"] = sc(y_rows(8), y_rows(24), YL, dev(ix, (iy + 3) % 4, iz))
        c["yh"] = sc(y_rows(20), y_rows(4), YH, dev(ix, (iy + 1) % 4, iz))
        c["z"] = sc(
            X.at[cur, pair_of, pl.ds(4 + 12 * oz, 4), pl.ds(8, 16), :],
            X.at[cur, pair_of, pl.ds(20 * zh, 4), pl.ds(8, 16), :],
            ZH,
            dev(ix, iy, oz * 4 + q),
        )
        for i, (dx, dy) in enumerate(DIRS):
            slot = 8 - i
            if i != SELF:
                c["rs", i] = sc(LSA.at[s, h, i], RS.at[s, h, slot], RS0 + slot, near(dx, dy, zh))
                c["bs", i] = sc(CS.at[s, h], SSA.at[s, h, slot], BS0 + slot, near(dx, dy, zh))
            c["ro", i] = sc(LSO.at[s, h, i], RO.at[s, h, slot], RO0 + slot, near(dx, dy, oz))
            c["bo", i] = sc(CSO.at[s, h], SSO.at[s, h, slot], BO0 + slot, near(dx, dy, oz))
        return c

    def when(condition, action):
        @pl.when(condition)
        def _():
            action()

    def neighbours(c, names, action, mirrored):
        for i in range(9):
            def both(i=i):
                for name in names:
                    if (name, i) in c:
                        getattr(c[name, i], action)()

            if i == SELF:
                both()
            else:
                when(exists(8 - i if mirrored else i), both)

    def send_y(c):
        when(iy > 0, c["yl"].start)
        when(iy < 3, c["yh"].start)

    def pack_x(s, h, c):
        vh_all = VH[2 * h : 2 * h + 2].reshape(512, 128)
        vl_all = VL[2 * h : 2 * h + 2].reshape(512, 128)
        XS[s, h] = dot_nt(e2, vh_all) + dot_nt(e2, vl_all)
        xp = dot_nt(jnp.concatenate([vh_all, vh_all], axis=1), CONST[...]) + dot_nt(vl_all, CONST[:, 0:128])
        Z[2 * h : 2 * h + 2] = xp.reshape(2, 16, 16, 128)
        c["xp"].start()
        c["xm"].start()

    def turn(value):
        return pltpu.roll(value, 64, 1)

    def both_parts(b, h):
        ph, pl_ = split(PART[b, h])
        return jnp.concatenate([ph.astype(F32), pl_.astype(F32)], axis=0).astype(BF16)

    def sums_for_other_half(s, h, c):
        parts16 = both_parts(edge_block, h)
        for i in range(9):
            LHO[i] = parts16 * NMB[edge_block, 3 * i + 2]
        sums = dot_nt(LHO[...].reshape(144, 256), WT[edge_block, 0:128])
        for i in range(9):
            one = sums[16 * i : 16 * i + 8] + sums[16 * i + 8 : 16 * i + 16]
            LSO[s, h, i] = one[0:4] + turn(one[4:8])
        neighbours(c, ("ro",), "start", False)

    def sums_for_own_half(s, h, c):
        for b in range(4):
            parts16 = both_parts(b, h)
            for i in range(9):
                for pair in range(2):
                    LH[2 * i + pair, :, b * 256 : (b + 1) * 256] = parts16 * NMB[b, 3 * i + pair]
        sums = None
        for b in range(4):
            lhs = LH[:, :, b * 256 : (b + 1) * 256].reshape(288, 256)
            term = dot_nt(lhs, WT[b, 0:128])
            sums = term if sums is None else sums + term
        sums = sums.reshape(18, 16, 128)
        LSA[s, h] = (sums[:, 0:8] + sums[:, 8:16]).reshape(9, 2, 8, 128)
        neighbours(c, ("rs",), "start", False)

    def stencil(s, h, c, first):
        c["xp"].wait_recv()
        c["xm"].wait_recv()
        xr = XR[s, h]
        xr_h = xr.astype(BF16).astype(F32)
        faces = jnp.concatenate([xr_h, xr - xr_h], axis=0).astype(BF16)
        Z[2 * h : 2 * h + 2] = Z[2 * h : 2 * h + 2] + (dot_tn(faces, edge_1) + dot_tn(faces, edge_2)).reshape(
            2, 16, 16, 128
        )
        c["z"].wait_recv()
        when(iy > 0, c["yh"].wait_recv)
        when(iy < 3, c["yl"].wait_recv)
        cur = s + 1
        scale = (1.0 if first else 2.0) / HALF

        def line(i, _):
            o = i // 16
            z = i % 16
            v0 = X[cur, o, z + 4, 8:24, :]
            acc = Z[o, z] + v0 * (POT[z] + (-1.5 * STENCIL[0] - CENTER))
            for k in range(1, 5):
                around = (X[cur, o, z + 4 - k, 8:24, :] + X[cur, o, z + 4 + k, 8:24, :]) + (
                    X[cur, o, z + 4, 8 - k : 24 - k, :] + X[cur, o, z + 4, 8 + k : 24 + k, :]
                )
                acc = acc + (-0.5 * STENCIL[k]) * around
            acc = scale * acc
            Z[o, z] = acc if first else acc - X[s, o, z + 4, 8:24, :]
            return 0

        lax.fori_loop(32 * h, 32 * h + 32, line, 0, unroll=4)

    theirs = lax.broadcasted_iota(I32, (4, 128), 1) // 64 == oz
    at_0 = jnp.where(zh == 1, 1.0, 0.0).astype(F32)

    def scale_totals(s, h, c, first):
        neighbours(c, ("rs", "ro"), "wait_recv", True)
        total = LSA[s, h, SELF]
        other = None
        for slot in range(9):
            if slot != SELF:
                total = total + RS[s, h, slot]
            other = RO[s, h, slot] if other is None else other + RO[s, h, slot]
        other = jnp.concatenate([jnp.where(theirs, other, 0.0), jnp.where(theirs, turn(other), 0.0)], axis=0)
        scale = (1.0 if first else 2.0) / HALF
        scaled = scale * SC[...] * jnp.stack([total[0] + at_0 * other, total[1] + (1.0 - at_0) * other])
        CS[s, h] = scaled
        edge_pair = at_0 * scaled[0] + (1.0 - at_0) * scaled[1]
        CSO[s, h] = jnp.where(theirs, edge_pair[0:4], turn(edge_pair[4:8]))
        SSA[s, h, SELF] = scaled
        neighbours(c, ("bo", "bs"), "start", False)

    def take(s, h, c):
        neighbours(c, ("bs",), "wait_recv", True)
        sh, sl = split(SSA[s, h].reshape(144, 128))
        SHA[h, :, 0:128] = sh
        SHA[h, :, 128:256] = sl
        neighbours(c, ("bo",), "wait_recv", True)
        rows8 = []
        for slot in range(9):
            packed = SSO[s, h, slot]
            rows8 += [packed, turn(packed)]
        sh, sl = split(jnp.concatenate(rows8, axis=0))
        SHO[h, :, 0:128] = sh
        SHO[h, :, 128:256] = sl

    def per_tile(b, h, with_other):
        r = dot_nn(SHA[h], WT[b])
        number = NIDX[b, 0:8]
        pt = jnp.zeros((8, 256), F32)
        for i in range(9):
            for pair in range(2):
                k = 2 * i + pair
                pt = pt + jnp.where(number == 3 * i + pair, r[k * 8 : (k + 1) * 8], 0.0)
        if with_other:
            r = dot_nn(SHO[h], WT[b])
            for i in range(9):
                pt = pt + jnp.where(number == 3 * i + 2, r[i * 8 : (i + 1) * 8], 0.0)
        return pt

    def project(pt, b):
        mask = MKB[b, 0:64]
        results = []
        for o in range(2):
            r = PT[b, 0] * pt[o : o + 1]
            for p in range(1, 4):
                r = r + PT[b, p] * pt[p * 2 + o : p * 2 + o + 1]
            rh, rl = split(r)
            results.append(dot_nt(mask, rh) + dot_nt(mask, rl))
        return jnp.stack(results).reshape(2, 4, 16, 128)

    def apply(s, b, h, with_other):
        o = slice(2 * h, 2 * h + 2)
        y = Z[o, pl.ds(4 * b, 4)] + project(per_tile(b, h, with_other), b)
        X[s + 2, o, pl.ds(4 + 4 * b, 4), 8:24, :] = y
        yh, yl = split(y)
        VH[o, pl.ds(4 * b, 4)] = yh
        VL[o, pl.ds(4 * b, 4)] = yl

    def block_sums(b, h):
        o = slice(2 * h, 2 * h + 2)
        vh = VH[o, pl.ds(4 * b, 4)].reshape(2, 64, 128)
        vl = VL[o, pl.ds(4 * b, 4)].reshape(2, 64, 128)
        tile_sums(vh, vl, b, PART, b, h)

    c = [step_copies(0, h) for h in range(HALVES)]
    take_own.wait()
    for v in values:
        v.wait_recv()
    for h in range(HALVES):
        c[h]["z"].start()
        send_y(c[h])
    for v in parts:
        v.wait_recv()
    for h in range(HALVES):
        sums_for_other_half(0, h, c[h])
        sums_for_own_half(0, h, c[h])
    for v in cpl_y:
        v.wait_recv()
    group = 2 * (ix * 32)
    cpl_x = [
        start(set_copy(rows(group, 64), rows(group, 64), CP0 + 6 + j, dev((ix + j) % 4, iy, iz))) for j in (1, 3, 2)
    ]
    high, low = split(X[1, :, 4:20, 8:24, :])
    VH[...] = high
    VL[...] = low
    for h in range(HALVES):
        pack_x(0, h, c[h])
    for v in cpl_x:
        v.wait_recv()
    home2 = home_in[...]
    home = jnp.concatenate([home2[0:1], home2[1:2]], axis=1)
    home_row = 2 * lax.shift_right_logical(home, 6)
    rows256 = lax.broadcasted_iota(I32, (256, 256), 0)
    lane_hot = jnp.where(row64 == jnp.bitwise_and(home, 63), 1.0, 0.0).astype(F32)
    cb = CB[...]
    cb_1 = cb.astype(BF16)
    rest = cb - cb_1.astype(F32)
    cb_2 = rest.astype(BF16)
    cb_3 = (rest - cb_2.astype(F32)).astype(BF16)
    for r in range(2):
        pick = jnp.where(rows256 == home_row + r, 1.0, 0.0).astype(BF16)
        found = dot_tn(cb_1, pick) + dot_tn(cb_2, pick) + dot_tn(cb_3, pick)
        for p2 in range(2):
            line = jnp.sum(found[p2 * 64 : (p2 + 1) * 64] * lane_hot, axis=0, keepdims=True)
            p = 2 * r + p2
            for pair in range(2):
                SC[pair, p * 2 : (p + 1) * 2, :] = jnp.broadcast_to(line[:, pair * 128 : (pair + 1) * 128], (2, 128))

    for h in range(HALVES):
        scale_totals(0, h, c[h], True)

    up[0].wait_recv()
    on_up = start(set_copy(PT.at[below, half[0]], PT.at[below, half[0]], PF0 + 4, ring(1)))
    down[0].wait_recv()
    on_down = start(set_copy(PT.at[above, half[1]], PT.at[above, half[1]], PF0 + 5, ring(3)))
    take_pot.wait()
    for v in pots:
        v.wait_recv()
    for h in range(HALVES):
        stencil(0, h, c[h], True)

    def rest_of_step(s, c):
        for h in range(HALVES):
            pack_x(s, h, c[h])
        for h in range(HALVES):
            scale_totals(s, h, c[h], False)
        for h in range(HALVES):
            stencil(s, h, c[h], False)

    for h in range(HALVES):
        take(0, h, c[h])
    for b, arrivals in ((q, ()), (below, (up[1],)), (above, (down[1],))):
        for v in arrivals:
            v.wait_recv()
        for h in range(HALVES):
            apply(0, b, h, True)
            block_sums(b, h)
    on_up.wait_recv()
    on_down.wait_recv()
    c = [step_copies(1, h) for h in range(HALVES)]
    for h in range(HALVES):
        apply(0, across, h, True)
        block_sums(across, h)
        c[h]["z"].start()
        sums_for_other_half(1, h, c[h])
        send_y(c[h])
        sums_for_own_half(1, h, c[h])
    rest_of_step(1, c)

    def step(s, _):
        before = [step_copies(s - 1, h) for h in range(HALVES)]
        c = [step_copies(s, h) for h in range(HALVES)]
        for h in range(HALVES):
            take(s - 1, h, before[h])
            apply(s - 1, edge_block, h, True)
            c[h]["z"].start()
            block_sums(edge_block, h)
            sums_for_other_half(s, h, c[h])

            def one(j, _):
                b = (edge_block + j) % 4
                apply(s - 1, b, h, False)
                block_sums(b, h)
                return 0

            lax.fori_loop(1, 4, one, 0)
            send_y(c[h])
            sums_for_own_half(s, h, c[h])
        rest_of_step(s, c)
        return 0

    lax.fori_loop(2, STEPS, step, 0)

    last = STEPS - 1
    outs_on = around(
        lambda block, o, n: Z.at[pl.ds(o, n), pl.ds(4 * block, 4)],
        lambda block, o, n: ZO.at[pl.ds(4 * block + o, n)],
        RLO,
        OU0,
    )
    finals = {}
    for h in range(HALVES):
        take(last, h, step_copies(last, h))
        for j in (2, 1, 3):
            b = (q + j) % 4
            PTS[pl.ds(b, 1), h] = per_tile(b, h, True)[None]
            finals[j, h] = start(set_copy(PTS.at[b, h], PTR.at[q, h], FT0 + 2 * (j - 1) + h, ring(j)))
    outs = outs_on()
    for h in range(HALVES):
        out[pl.ds(4 * q + 2 * h, 2)] = Z[2 * h : 2 * h + 2, pl.ds(4 * q, 4)] + project(per_tile(q, h, True), q)
    for v in outs:
        v.wait_recv()
    for j in (1, 3, 2):
        for h in range(HALVES):
            finals[j, h].wait_recv()
            g = (q - j + 4) % 4
            mine_of = pl.ds(4 * g + 2 * h, 2)
            out[mine_of] = ZO[mine_of] + project(PTR[g, h], q)
    for v in sends:
        v.wait_send()

    def drain(s, _):
        for h in range(HALVES):
            c = step_copies(s, h)
            for name in ("xp", "xm", "z"):
                c[name].wait_send()
            when(iy > 0, c["yl"].wait_send)
            when(iy < 3, c["yh"].wait_send)
            neighbours(c, ("rs", "ro", "bs", "bo"), "wait_send", False)
        return 0

    lax.fori_loop(0, STEPS, drain, 0)


def per_device(orbitals, potential, tile_proj, tile_atom, tile_column, tile_count, atom_home, coupling):
    vmem = pl.BlockSpec(memory_space=pltpu.VMEM)
    hbm = pl.BlockSpec(memory_space=pltpu.HBM)
    smem = pl.BlockSpec(memory_space=pltpu.SMEM)
    return pl.pallas_call(
        kernel,
        out_shape=jax.ShapeDtypeStruct((16, 4, 16, 128), F32),
        in_specs=[hbm] * 5 + [smem] + [hbm] * 3,
        out_specs=vmem,
        scratch_shapes=[
            pltpu.VMEM((6, 4, 24, 32, 128), F32),
            pltpu.VMEM((4, 16, 16, 128), F32),
            pltpu.VMEM((4, 16, 16, 128), BF16),
            pltpu.VMEM((4, 16, 16, 128), BF16),
            pltpu.VMEM((1024, 128), F32),
            pltpu.VMEM((4, 4, 128, 256), F32),
            pltpu.VMEM((16, 16, 128), F32),
            pltpu.VMEM((4, 8, 256), I32),
            pltpu.VMEM((4, 128, 256), BF16),
            pltpu.VMEM((4, 16, 256), I32),
            pltpu.VMEM((4, 27, 16, 256), BF16),
            pltpu.VMEM((4, 256, 256), BF16),
            pltpu.VMEM((18, 16, 1024), BF16),
            pltpu.VMEM((9, 16, 256), BF16),
            pltpu.VMEM((4, 2, 9, 2, 8, 128), F32),
            pltpu.VMEM((4, 2, 9, 4, 128), F32),
            pltpu.VMEM((4, 2, 9, 2, 8, 128), F32),
            pltpu.VMEM((4, 2, 9, 4, 128), F32),
            pltpu.VMEM((4, 2, 2, 8, 128), F32),
            pltpu.VMEM((4, 2, 4, 128), F32),
            pltpu.VMEM((4, 2, 9, 2, 8, 128), F32),
            pltpu.VMEM((4, 2, 9, 4, 128), F32),
            pltpu.VMEM((2, 144, 256), BF16),
            pltpu.VMEM((2, 72, 256), BF16),
            pltpu.VMEM((2, 8, 128), F32),
            pltpu.VMEM((4, 2, 8, 512), F32),
            pltpu.VMEM((4, 2, 8, 512), F32),
            pltpu.VMEM((256, 128), F32),
            pltpu.VMEM((128, 256), BF16),
            pltpu.VMEM((4, 2, 8, 256), F32),
            pltpu.VMEM((4, 2, 8, 256), F32),
            pltpu.VMEM((4, 2, 8, 256), F32),
            pltpu.VMEM((4, 2, 8, 256), F32),
            pltpu.VMEM((16, 4, 16, 128), F32),
            pltpu.VMEM((16, 4, 16, 128), F32),
            pltpu.VMEM((2, 2, 4, 16, 128), F32),
            pltpu.VMEM((2, 2, 4, 16, 128), F32),
            pltpu.VMEM((1, 256), I32),
            pltpu.VMEM((1, 256), I32),
            pltpu.VMEM((2, 128), I32),
            pltpu.VMEM((4, 64), F32),
            pltpu.VMEM((144, 128), F32),
            pltpu.SemaphoreType.DMA((NSET,)),
            pltpu.SemaphoreType.DMA((NSET,)),
            pltpu.SemaphoreType.DMA((STEPS, HALVES * NSEM)),
            pltpu.SemaphoreType.DMA((STEPS, HALVES * NSEM)),
            pltpu.SemaphoreType.DMA((9,)),
        ],
        compiler_params=pltpu.CompilerParams(
            collective_id=0, has_side_effects=True, vmem_limit_bytes=60000 * 1024
        ),
        name="chebyshev",
    )(
        orbitals,
        potential,
        tile_proj.reshape(1024, 128),
        tile_atom.reshape(1, 256),
        tile_column.reshape(1, 256),
        tile_count,
        atom_home.reshape(64, 128),
        coupling.T,
        jnp.asarray(stencil_constants()),
    )


def solution(mesh):
    return jax.shard_map(
        per_device,
        mesh=mesh,
        in_specs=(
            P(None, "gz", "gy", "gx"),
            P("gz", "gy", "gx"),
            P(("gx", "gy", "gz"), None, None),
            P(("gx", "gy", "gz")),
            P(("gx", "gy", "gz")),
            P(("gx", "gy", "gz")),
            P(),
            P(("gx", "gy", "gz"), None),
        ),
        out_specs=P(None, "gz", "gy", "gx"),
        check_vma=False,
    )
```

```python
import jax
import jax.numpy as jnp
import numpy as np
from jax import lax
from jax.experimental import pallas as pl
from jax.experimental.pallas import tpu as pltpu
from jax.sharding import PartitionSpec as P

F32, BF16, I32 = jnp.float32, jnp.bfloat16, jnp.int32
STENCIL = (-205.0 / 72.0, 8.0 / 5.0, -1.0 / 5.0, 8.0 / 315.0, -1.0 / 560.0)
CENTER, HALF = 14.0, 10.0
STEPS = 4
DIRS = [(dx, dy) for dx in (-1, 0, 1) for dy in (-1, 0, 1)]
SELF = 4
XP, XM, YL, YH, ZH, RS0, RO0, BS0, BO0, NSEM = 0, 1, 2, 3, 4, 5, 14, 23, 32, 41
V0, PF0, PT0, ME0, CP0, PA0, OU0, FT0, NSET = 0, 6, 12, 15, 18, 28, 31, 37, 40


def stencil_constants():
    table = np.zeros((144, 128), np.float32)
    for x in range(128):
        for k in range(1, 5):
            if x + k < 128:
                table[x, x + k] = -0.5 * STENCIL[k]
            if x - k >= 0:
                table[x, x - k] = -0.5 * STENCIL[k]
    for j in range(4):
        table[128 + j, 124 + j] = 1.0
        table[132 + j, j] = 1.0
        for x in range(128):
            k = x + 4 - j
            if 1 <= k <= 4:
                table[136 + j, x] = -0.5 * STENCIL[k]
            k = 128 + j - x
            if 1 <= k <= 4:
                table[140 + j, x] = -0.5 * STENCIL[k]
    return table


def split(value):
    high = value.astype(BF16)
    return high, (value - high.astype(F32)).astype(BF16)


def dot_nt(a, b):
    return lax.dot_general(a, b, (((1,), (1,)), ((), ())), preferred_element_type=F32)


def dot_nn(a, b):
    return lax.dot_general(a, b, (((1,), (0,)), ((), ())), preferred_element_type=F32)


def dot_tn(a, b):
    return lax.dot_general(a, b, (((0,), (0,)), ((), ())), preferred_element_type=F32)


def kernel(
    orb, pot_in, tp, atom_hbm, column_hbm, count_in, home_hbm, cpl_hbm, table_hbm, out,
    X, Z, VH, VL, PF, PT, POT, META, MKB, NIDX, NMB, WT, LH, LHO, LSA, LSO, RS, RO, CS, CSO, SSA, SSO, SHA, SHO, SC, XS, XR, CB, CONST,
    PART, PART0, PTS, PTR, ZO, ORB, RL, RLO, atom_in, column_in, home_in, cpl_in, table,
    set_s, set_r, sem_s, sem_r, local_sem,
):
    ix, iy, iz = lax.axis_index("gx"), lax.axis_index("gy"), lax.axis_index("gz")
    zh, q = iz // 4, iz % 4
    oz = 1 - zh
    edge_block = 3 * oz
    below, above, across = (q + 3) % 4, (q + 1) % 4, (q + 2) % 4

    def dev(gx, gy, gz):
        return {"gx": gx, "gy": gy, "gz": gz}

    def ring(j):
        return dev(ix, iy, zh * 4 + (q + j) % 4)

    def near(dx, dy, half):
        return dev((ix + dx + 4) % 4, (iy + dy + 4) % 4, half * 4 + q)

    def exists(i):
        dx, dy = DIRS[i]
        return jnp.logical_and(
            jnp.logical_and(ix + dx >= 0, ix + dx <= 3), jnp.logical_and(iy + dy >= 0, iy + dy <= 3)
        )

    def copy(src, dst, s, r, to):
        return pltpu.make_async_remote_copy(
            src_ref=src, dst_ref=dst, send_sem=s, recv_sem=r, device_id=to, device_id_type=pl.DeviceIdType.MESH
        )

    barrier = pltpu.get_barrier_semaphore()
    peers = [near(dx, dy, half) for dx, dy in DIRS for half in (zh, oz)]
    peers = [p for i, p in enumerate(peers) if i != 2 * SELF]
    peers += [ring(j) for j in (1, 2, 3)]
    peers += [dev((ix + 2) % 4, iy, iz), dev(ix, (iy + 2) % 4, iz)]
    for peer in peers:
        pl.semaphore_signal(barrier, inc=1, device_id=peer, device_id_type=pl.DeviceIdType.MESH)
    take_proj = pltpu.make_async_copy(tp, PF, local_sem.at[0])
    take_orb = pltpu.make_async_copy(orb, ORB, local_sem.at[1])
    take_pot = pltpu.make_async_copy(pot_in, POT.at[pl.ds(4 * q, 4)], local_sem.at[2])
    take_own = pltpu.make_async_copy(
        orb.at[pl.ds(4 * q, 4)], X.at[1, :, pl.ds(4 + 4 * q, 4), pl.ds(8, 16), :], local_sem.at[3]
    )
    smalls = [
        pltpu.make_async_copy(src, dst, local_sem.at[4 + i])
        for i, (src, dst) in enumerate(
            (
                (atom_hbm, atom_in),
                (column_hbm, column_in),
                (cpl_hbm, cpl_in),
                (table_hbm, table),
                (home_hbm.at[pl.ds(2 * ((ix * 4 + iy) * 2 + zh), 2)], home_in),
            )
        )
    ]
    for c in smalls + [take_proj, take_orb, take_own, take_pot]:
        c.start()
    for c in smalls:
        c.wait()

    atom = atom_in[...]
    owner = lax.shift_right_logical(atom, 6)
    dx = lax.shift_right_logical(owner, 5) - ix + 1
    dy = jnp.bitwise_and(lax.shift_right_logical(owner, 3), 3) - iy + 1
    zb = jnp.bitwise_and(owner, 7) - 4 * zh
    pair = jnp.where(jnp.logical_and(zb >= 0, zb < 4), lax.shift_right_arithmetic(zb, 1), 2)
    number = (dx * 3 + dy) * 3 + pair
    lane = jnp.bitwise_and(zb, 1) * 64 + jnp.bitwise_and(atom, 63)
    column = jnp.where(lax.broadcasted_iota(I32, (1, 256), 1) < count_in[0], column_in[...], -1)
    META[pl.ds(q, 1)] = jnp.concatenate([number, lane, column] + [column] * 5, axis=0)[None]
    cpl = cpl_in[...]
    mine = 2 * ((ix * 4 + iy) * 8 + iz)
    CB[pl.ds(mine, 2), :] = jnp.concatenate(
        [jnp.concatenate([cpl[0:1], cpl[1:2]], axis=1), jnp.concatenate([cpl[2:3], cpl[3:4]], axis=1)], axis=0
    )

    row64 = lax.broadcasted_iota(I32, (64, 256), 0)
    row128 = lax.broadcasted_iota(I32, (128, 256), 0)

    def masks(b):
        mask = jnp.where(row64 == META[b, 2:3, :], 1.0, 0.0).astype(BF16)
        MKB[b, 0:64] = mask
        MKB[b, 64:128] = mask

    masks(q)

    def clear(i, _):
        X[i, :, pl.ds(20 * zh, 4)] = jnp.zeros((4, 4, 32, 128), F32)

        @pl.when(iy == 0)
        def _():
            X[i, :, 4:20, 0:8] = jnp.zeros((4, 16, 8, 128), F32)

        @pl.when(iy == 3)
        def _():
            X[i, :, 4:20, 24:32] = jnp.zeros((4, 16, 8, 128), F32)

        return 0

    lax.fori_loop(1, 5, clear, 0)

    def clear_sums(i, _):
        for slot in range(9):
            if slot != SELF:

                @pl.when(jnp.logical_not(exists(slot)))
                def _():
                    RS[i, slot] = jnp.zeros((2, 16, 128), F32)
                    RO[i, slot] = jnp.zeros((8, 128), F32)

        return 0

    lax.fori_loop(0, 4, clear_sums, 0)

    wx_h, wx_l = split(table[0:128, :])
    CONST[0:128, 0:128] = wx_h
    CONST[0:128, 128:256] = wx_l
    e2 = table[128:136, :].astype(BF16)
    edge_row = lax.broadcasted_iota(I32, (8, 128), 0)
    inside = jnp.where(
        edge_row < 4, jnp.where(ix > 0, 1.0, 0.0).astype(F32), jnp.where(ix < 3, 1.0, 0.0).astype(F32)
    )
    edge = table[136:144, :] * inside
    edge_h = edge.astype(BF16).astype(F32)
    edge_1 = jnp.concatenate([edge_h, edge_h], axis=0).astype(BF16)
    edge_2 = jnp.concatenate([edge - edge_h, edge - edge_h], axis=0).astype(BF16)

    take_proj.wait()
    for p in range(4):
        PT[q, p] = PF[pl.ds(p, 256, stride=4), :].T
    pl.semaphore_wait(barrier, len(peers))

    def field_block(index, block):
        return X.at[index, :, pl.ds(4 + 4 * block, 4), pl.ds(8, 16), :]

    sends = []

    def start(c):
        c.start()
        sends.append(c)
        return c

    def set_copy(src, dst, index, to):
        return copy(src, dst, set_s.at[index], set_r.at[index], to)

    def rows(first, count):
        return CB.at[pl.ds(first, count)]

    metas = [start(set_copy(META.at[q], META.at[q], ME0 + j - 1, ring(j))) for j in (1, 3, 2)]
    ring_cpl = [start(set_copy(rows(mine, 2), rows(mine, 2), CP0 + j - 1, ring(j))) for j in (1, 3, 2)]

    def around(source, target, relay, base):
        to_up = start(set_copy(source(across, 0, 2), relay.at[0], base, ring(1)))
        to_down = start(set_copy(source(across, 2, 2), relay.at[1], base + 1, ring(3)))
        near_up = start(set_copy(source(above, 0, 4), target(q, 0, 4), base + 2, ring(1)))
        near_down = start(set_copy(source(below, 0, 4), target(q, 0, 4), base + 3, ring(3)))

        def forward():
            to_up.wait_recv()
            far_up = start(set_copy(relay.at[0], target(below, 0, 2), base + 4, ring(1)))
            to_down.wait_recv()
            far_down = start(set_copy(relay.at[1], target(above, 2, 2), base + 5, ring(3)))
            return near_up, near_down, far_up, far_down

        return forward

    values_on = around(
        lambda block, o, n: orb.at[pl.ds(4 * block + o, n)],
        lambda block, o, n: X.at[1, pl.ds(o, n), pl.ds(4 + 4 * block, 4), pl.ds(8, 16), :],
        RL,
        V0,
    )

    def tile_sums(vh, vl, b, result, at):
        for o in range(4):
            r = dot_tn(jnp.concatenate([vh[o], vl[o]], axis=0), MKB[b])
            for p in range(4):
                result[at, pl.ds(p * 4 + o, 1), :] = jnp.sum(r * PT[b, p], axis=0, keepdims=True)

    take_orb.wait()

    def own_sums(g, _):
        vh, vl = split(ORB[pl.ds(4 * g, 4)].reshape(4, 64, 128))
        tile_sums(vh, vl, q, PART0, g)
        return 0

    lax.fori_loop(0, 4, own_sums, 0)
    values = values_on()
    parts = [start(set_copy(PART0.at[(q + j) % 4], PART.at[q], PA0 + j - 1, ring(j))) for j in (2, 1, 3)]
    half = [pl.ds(0, 2), pl.ds(2, 2)]
    up = [start(set_copy(PT.at[q, half[h]], PT.at[q, half[h]], PF0 + h, ring(1))) for h in (0, 1)]
    down = [start(set_copy(PT.at[q, half[h]], PT.at[q, half[h]], PF0 + 3 - h, ring(3))) for h in (1, 0)]
    pots = [start(set_copy(pot_in, POT.at[pl.ds(4 * q, 4)], PT0 + j - 1, ring(j))) for j in (1, 3, 2)]
    PART[pl.ds(q, 1)] = PART0[pl.ds(q, 1)]

    for c in ring_cpl:
        c.wait_recv()
    group = 2 * ((ix * 4 + iy) * 8 + zh * 4)
    flip = start(set_copy(rows(group, 8), rows(group, 8), CP0 + 3, dev(ix, iy, oz * 4 + q)))

    for c in metas:
        c.wait_recv()
    masks(below)
    masks(above)
    masks(across)
    for b in range(4):
        index = META[b]
        hot = jnp.where(row128 == index[1:2, :], 1.0, 0.0).astype(BF16)
        WT[b, 0:128] = hot
        WT[b, 128:256] = hot
        number = jnp.broadcast_to(index[0:1, :], (16, 256))
        NIDX[b] = number
        for n in range(27):
            NMB[b, n] = jnp.where(number == n, 1.0, 0.0).astype(BF16)

    flip.wait_recv()
    group = 2 * ((ix * 4 + iy) * 8)
    cpl_y = [
        start(set_copy(rows(group, 16), rows(group, 16), CP0 + 3 + j, dev(ix, (iy + j) % 4, iz))) for j in (1, 3, 2)
    ]

    def step_copies(s):
        cur = s + 1

        def sc(src, dst, index, to):
            return copy(src, dst, sem_s.at[s, index], sem_r.at[s, index], to)

        c = {}
        c["xp"] = sc(XS.at[s, pl.ds(0, 4)], XR.at[s, pl.ds(0, 4)], XP, dev((ix + 1) % 4, iy, iz))
        c["xm"] = sc(XS.at[s, pl.ds(4, 4)], XR.at[s, pl.ds(4, 4)], XM, dev((ix + 3) % 4, iy, iz))
        inner = pl.ds(4, 16)
        c["yl"] = sc(
            X.at[cur, :, inner, pl.ds(8, 4), :], X.at[cur, :, inner, pl.ds(24, 4), :], YL, dev(ix, (iy + 3) % 4, iz)
        )
        c["yh"] = sc(
            X.at[cur, :, inner, pl.ds(20, 4), :], X.at[cur, :, inner, pl.ds(4, 4), :], YH, dev(ix, (iy + 1) % 4, iz)
        )
        c["z"] = sc(
            X.at[cur, :, pl.ds(4 + 12 * oz, 4), pl.ds(8, 16), :],
            X.at[cur, :, pl.ds(20 * zh, 4), pl.ds(8, 16), :],
            ZH,
            dev(ix, iy, oz * 4 + q),
        )
        for i, (dx, dy) in enumerate(DIRS):
            slot = 8 - i
            if i != SELF:
                c["rs", i] = sc(LSA.at[s, i], RS.at[s, slot], RS0 + slot, near(dx, dy, zh))
                c["bs", i] = sc(CS.at[s], SSA.at[s, slot], BS0 + slot, near(dx, dy, zh))
            c["ro", i] = sc(LSO.at[s, i], RO.at[s, slot], RO0 + slot, near(dx, dy, oz))
            c["bo", i] = sc(CSO.at[s], SSO.at[s, slot], BO0 + slot, near(dx, dy, oz))
        return c

    def when(condition, action):
        @pl.when(condition)
        def _():
            action()

    def neighbours(c, names, action, mirrored):
        for i in range(9):
            def both(i=i):
                for name in names:
                    if (name, i) in c:
                        getattr(c[name, i], action)()

            if i == SELF:
                both()
            else:
                when(exists(8 - i if mirrored else i), both)

    def send_y(c):
        when(iy > 0, c["yl"].start)
        when(iy < 3, c["yh"].start)

    def pack_x(s, c):
        vh_all = VH[...].reshape(1024, 128)
        vl_all = VL[...].reshape(1024, 128)
        XS[s] = dot_nt(e2, vh_all) + dot_nt(e2, vl_all)
        xp = dot_nt(jnp.concatenate([vh_all, vh_all], axis=1), CONST[...]) + dot_nt(vl_all, CONST[:, 0:128])
        Z[...] = xp.reshape(4, 16, 16, 128)
        c["xp"].start()
        c["xm"].start()

    def turn(value):
        return pltpu.roll(value.reshape(-1, 128), 64, 1).reshape(value.shape)

    def sums_for_other_half(s, c):
        ph, pl_ = split(PART[edge_block])
        for i in range(9):
            m = NMB[edge_block, 3 * i + 2]
            LHO[i, 0:16] = ph * m
            LHO[i, 16:32] = pl_ * m
        sums = dot_nt(LHO[...].reshape(288, 256), WT[edge_block, 0:128]).reshape(9, 32, 128)
        sums = sums[:, 0:16] + sums[:, 16:32]
        LSO[s] = sums[:, 0:8] + turn(sums[:, 8:16])
        neighbours(c, ("ro",), "start", False)

    def sums_for_own_half(s, c):
        for b in range(4):
            ph, pl_ = split(PART[b])
            for i in range(9):
                for pair in range(2):
                    m = NMB[b, 3 * i + pair]
                    LH[2 * i + pair, 0:16, b * 256 : (b + 1) * 256] = ph * m
                    LH[2 * i + pair, 16:32, b * 256 : (b + 1) * 256] = pl_ * m
        sums = None
        for b in range(4):
            lhs = LH[:, :, b * 256 : (b + 1) * 256].reshape(576, 256)
            term = dot_nt(lhs, WT[b, 0:128])
            sums = term if sums is None else sums + term
        sums = sums.reshape(18, 32, 128)
        LSA[s] = (sums[:, 0:16] + sums[:, 16:32]).reshape(9, 2, 16, 128)
        neighbours(c, ("rs",), "start", False)

    def stencil(s, c, first):
        c["xp"].wait_recv()
        c["xm"].wait_recv()
        xr = XR[s]
        xr_h = xr.astype(BF16).astype(F32)
        faces = jnp.concatenate([xr_h, xr - xr_h], axis=0).astype(BF16)
        Z[...] = Z[...] + (dot_tn(faces, edge_1) + dot_tn(faces, edge_2)).reshape(4, 16, 16, 128)
        c["z"].wait_recv()
        when(iy > 0, c["yh"].wait_recv)
        when(iy < 3, c["yl"].wait_recv)
        cur = s + 1
        scale = (1.0 if first else 2.0) / HALF

        def line(i, _):
            o = i // 16
            z = i % 16
            v0 = X[cur, o, z + 4, 8:24, :]
            acc = Z[o, z] + v0 * (POT[z] + (-1.5 * STENCIL[0] - CENTER))
            for k in range(1, 5):
                around = (X[cur, o, z + 4 - k, 8:24, :] + X[cur, o, z + 4 + k, 8:24, :]) + (
                    X[cur, o, z + 4, 8 - k : 24 - k, :] + X[cur, o, z + 4, 8 + k : 24 + k, :]
                )
                acc = acc + (-0.5 * STENCIL[k]) * around
            acc = scale * acc
            Z[o, z] = acc if first else acc - X[s, o, z + 4, 8:24, :]
            return 0

        lax.fori_loop(0, 64, line, 0, unroll=4)

    def scale_totals(s, c, first):
        neighbours(c, ("rs", "ro"), "wait_recv", True)
        total = LSA[s, SELF]
        other = None
        for slot in range(9):
            if slot != SELF:
                total = total + RS[s, slot]
            other = RO[s, slot] if other is None else other + RO[s, slot]
        theirs = lax.broadcasted_iota(I32, (8, 128), 1) // 64 == oz
        other = jnp.concatenate([jnp.where(theirs, other, 0.0), jnp.where(theirs, turn(other), 0.0)], axis=0)
        at_0 = jnp.where(zh == 1, 1.0, 0.0).astype(F32)
        scale = (1.0 if first else 2.0) / HALF
        scaled = scale * SC[...] * jnp.stack([total[0] + at_0 * other, total[1] + (1.0 - at_0) * other])
        CS[s] = scaled
        edge_pair = at_0 * scaled[0] + (1.0 - at_0) * scaled[1]
        CSO[s] = jnp.where(theirs, edge_pair[0:8], turn(edge_pair[8:16]))
        SSA[s, SELF] = scaled
        neighbours(c, ("bo", "bs"), "start", False)

    def take_same(s, c):
        neighbours(c, ("bs",), "wait_recv", True)
        sh, sl = split(SSA[s].reshape(288, 128))
        SHA[:, 0:128] = sh
        SHA[:, 128:256] = sl

    def take_other(s, c):
        neighbours(c, ("bo",), "wait_recv", True)
        packed = SSO[s]
        sh, sl = split(jnp.concatenate([packed, turn(packed)], axis=1).reshape(144, 128))
        SHO[:, 0:128] = sh
        SHO[:, 128:256] = sl

    def per_tile(b, with_other):
        r = dot_nn(SHA[...], WT[b])
        number = NIDX[b]
        pt = jnp.zeros((16, 256), F32)
        for i in range(9):
            for pair in range(2):
                k = 2 * i + pair
                pt = pt + jnp.where(number == 3 * i + pair, r[k * 16 : (k + 1) * 16], 0.0)
        if with_other:
            r = dot_nn(SHO[...], WT[b])
            for i in range(9):
                pt = pt + jnp.where(number == 3 * i + 2, r[i * 16 : (i + 1) * 16], 0.0)
        return pt

    def project(pt, b):
        mask = MKB[b, 0:64]
        results = []
        for o in range(4):
            r = PT[b, 0] * pt[o : o + 1]
            for p in range(1, 4):
                r = r + PT[b, p] * pt[p * 4 + o : p * 4 + o + 1]
            rh, rl = split(r)
            results.append(dot_nt(mask, rh) + dot_nt(mask, rl))
        return jnp.stack(results)

    def apply(s, b, with_other):
        y = Z[:, pl.ds(4 * b, 4)] + project(per_tile(b, with_other), b).reshape(4, 4, 16, 128)
        X[s + 2, :, pl.ds(4 + 4 * b, 4), 8:24, :] = y
        yh, yl = split(y)
        VH[:, pl.ds(4 * b, 4)] = yh
        VL[:, pl.ds(4 * b, 4)] = yl

    c = step_copies(0)
    take_own.wait()
    for v in values:
        v.wait_recv()
    c["z"].start()
    send_y(c)
    for v in parts:
        v.wait_recv()
    sums_for_other_half(0, c)
    sums_for_own_half(0, c)
    for v in cpl_y:
        v.wait_recv()
    group = 2 * (ix * 32)
    cpl_x = [
        start(set_copy(rows(group, 64), rows(group, 64), CP0 + 6 + j, dev((ix + j) % 4, iy, iz))) for j in (1, 3, 2)
    ]
    high, low = split(X[1, :, 4:20, 8:24, :])
    VH[...] = high
    VL[...] = low
    pack_x(0, c)
    for v in cpl_x:
        v.wait_recv()
    home2 = home_in[...]
    home = jnp.concatenate([home2[0:1], home2[1:2]], axis=1)
    home_row = 2 * lax.shift_right_logical(home, 6)
    rows256 = lax.broadcasted_iota(I32, (256, 256), 0)
    lane_hot = jnp.where(row64 == jnp.bitwise_and(home, 63), 1.0, 0.0).astype(F32)
    cb = CB[...]
    cb_1 = cb.astype(BF16)
    rest = cb - cb_1.astype(F32)
    cb_2 = rest.astype(BF16)
    cb_3 = (rest - cb_2.astype(F32)).astype(BF16)
    for r in range(2):
        pick = jnp.where(rows256 == home_row + r, 1.0, 0.0).astype(BF16)
        found = dot_tn(cb_1, pick) + dot_tn(cb_2, pick) + dot_tn(cb_3, pick)
        for p2 in range(2):
            line = jnp.sum(found[p2 * 64 : (p2 + 1) * 64] * lane_hot, axis=0, keepdims=True)
            p = 2 * r + p2
            for pair in range(2):
                SC[pair, p * 4 : (p + 1) * 4, :] = jnp.broadcast_to(line[:, pair * 128 : (pair + 1) * 128], (4, 128))

    scale_totals(0, c, True)

    up[0].wait_recv()
    on_up = start(set_copy(PT.at[below, half[0]], PT.at[below, half[0]], PF0 + 4, ring(1)))
    down[0].wait_recv()
    on_down = start(set_copy(PT.at[above, half[1]], PT.at[above, half[1]], PF0 + 5, ring(3)))
    take_pot.wait()
    for v in pots:
        v.wait_recv()
    stencil(0, c, True)
    def block_sums(b):
        vh = VH[:, pl.ds(4 * b, 4)].reshape(4, 64, 128)
        vl = VL[:, pl.ds(4 * b, 4)].reshape(4, 64, 128)
        tile_sums(vh, vl, b, PART, b)

    def rest_of_step(s, c):
        sums_for_own_half(s, c)
        send_y(c)
        pack_x(s, c)
        scale_totals(s, c, False)
        stencil(s, c, False)

    take_same(0, c)
    take_other(0, c)
    c = step_copies(1)
    for b, arrivals in ((q, ()), (below, (up[1],)), (above, (down[1],)), (across, (on_up, on_down))):
        for v in arrivals:
            v.wait_recv()
        apply(0, b, True)
        block_sums(b)
    c["z"].start()
    sums_for_other_half(1, c)
    rest_of_step(1, c)

    def step(s, _):
        before = step_copies(s - 1)
        c = step_copies(s)
        take_same(s - 1, before)
        take_other(s - 1, before)
        apply(s - 1, edge_block, True)
        c["z"].start()
        block_sums(edge_block)
        sums_for_other_half(s, c)

        def one(j, _):
            b = (edge_block + j) % 4
            apply(s - 1, b, False)
            block_sums(b)
            return 0

        lax.fori_loop(1, 4, one, 0)
        rest_of_step(s, c)
        return 0

    lax.fori_loop(2, STEPS, step, 0)

    last = STEPS - 1
    c = step_copies(last)
    outs_on = around(
        lambda block, o, n: Z.at[pl.ds(o, n), pl.ds(4 * block, 4)],
        lambda block, o, n: ZO.at[pl.ds(4 * block + o, n)],
        RLO,
        OU0,
    )
    take_same(last, c)
    take_other(last, c)
    finals = []
    for j in (2, 1, 3):
        b = (q + j) % 4
        PTS[pl.ds(b, 1)] = per_tile(b, True)[None]
        finals.append(start(set_copy(PTS.at[b], PTR.at[q], FT0 + j - 1, ring(j))))
    outs = outs_on()
    result = Z[:, pl.ds(4 * q, 4)] + project(per_tile(q, True), q).reshape(4, 4, 16, 128)
    out[pl.ds(4 * q, 4)] = result
    for v in outs:
        v.wait_recv()
    for index, j in ((1, 1), (2, 3), (0, 2)):
        finals[index].wait_recv()
        g = (q - j + 4) % 4
        out[pl.ds(4 * g, 4)] = ZO[pl.ds(4 * g, 4)] + project(PTR[g], q).reshape(4, 4, 16, 128)
    for v in sends:
        v.wait_send()

    def drain(s, _):
        c = step_copies(s)
        for name in ("xp", "xm", "z"):
            c[name].wait_send()
        when(iy > 0, c["yl"].wait_send)
        when(iy < 3, c["yh"].wait_send)
        neighbours(c, ("rs", "ro", "bs", "bo"), "wait_send", False)
        return 0

    lax.fori_loop(0, STEPS, drain, 0)


def per_device(orbitals, potential, tile_proj, tile_atom, tile_column, tile_count, atom_home, coupling):
    vmem = pl.BlockSpec(memory_space=pltpu.VMEM)
    hbm = pl.BlockSpec(memory_space=pltpu.HBM)
    smem = pl.BlockSpec(memory_space=pltpu.SMEM)

    def in_hbm(x):
        return pltpu.with_memory_space_constraint(x, pltpu.HBM)

    return pl.pallas_call(
        kernel,
        out_shape=jax.ShapeDtypeStruct((16, 4, 16, 128), F32),
        in_specs=[hbm] * 5 + [smem] + [hbm] * 3,
        out_specs=vmem,
        scratch_shapes=[
            pltpu.VMEM((6, 4, 24, 32, 128), F32),
            pltpu.VMEM((4, 16, 16, 128), F32),
            pltpu.VMEM((4, 16, 16, 128), BF16),
            pltpu.VMEM((4, 16, 16, 128), BF16),
            pltpu.VMEM((1024, 128), F32),
            pltpu.VMEM((4, 4, 128, 256), F32),
            pltpu.VMEM((16, 16, 128), F32),
            pltpu.VMEM((4, 8, 256), I32),
            pltpu.VMEM((4, 128, 256), BF16),
            pltpu.VMEM((4, 16, 256), I32),
            pltpu.VMEM((4, 27, 16, 256), BF16),
            pltpu.VMEM((4, 256, 256), BF16),
            pltpu.VMEM((18, 32, 1024), BF16),
            pltpu.VMEM((9, 32, 256), BF16),
            pltpu.VMEM((4, 9, 2, 16, 128), F32),
            pltpu.VMEM((4, 9, 8, 128), F32),
            pltpu.VMEM((4, 9, 2, 16, 128), F32),
            pltpu.VMEM((4, 9, 8, 128), F32),
            pltpu.VMEM((4, 2, 16, 128), F32),
            pltpu.VMEM((4, 8, 128), F32),
            pltpu.VMEM((4, 9, 2, 16, 128), F32),
            pltpu.VMEM((4, 9, 8, 128), F32),
            pltpu.VMEM((288, 256), BF16),
            pltpu.VMEM((144, 256), BF16),
            pltpu.VMEM((2, 16, 128), F32),
            pltpu.VMEM((4, 8, 1024), F32),
            pltpu.VMEM((4, 8, 1024), F32),
            pltpu.VMEM((256, 128), F32),
            pltpu.VMEM((128, 256), BF16),
            pltpu.VMEM((4, 16, 256), F32),
            pltpu.VMEM((4, 16, 256), F32),
            pltpu.VMEM((4, 16, 256), F32),
            pltpu.VMEM((4, 16, 256), F32),
            pltpu.VMEM((16, 4, 16, 128), F32),
            pltpu.VMEM((16, 4, 16, 128), F32),
            pltpu.VMEM((2, 2, 4, 16, 128), F32),
            pltpu.VMEM((2, 2, 4, 16, 128), F32),
            pltpu.VMEM((1, 256), I32),
            pltpu.VMEM((1, 256), I32),
            pltpu.VMEM((2, 128), I32),
            pltpu.VMEM((4, 64), F32),
            pltpu.VMEM((144, 128), F32),
            pltpu.SemaphoreType.DMA((NSET,)),
            pltpu.SemaphoreType.DMA((NSET,)),
            pltpu.SemaphoreType.DMA((STEPS, NSEM)),
            pltpu.SemaphoreType.DMA((STEPS, NSEM)),
            pltpu.SemaphoreType.DMA((9,)),
        ],
        compiler_params=pltpu.CompilerParams(
            collective_id=0, has_side_effects=True, vmem_limit_bytes=40000 * 1024
        ),
        name="chebyshev",
    )(
        in_hbm(orbitals),
        in_hbm(potential),
        in_hbm(tile_proj.reshape(1024, 128)),
        in_hbm(tile_atom.reshape(1, 256)),
        in_hbm(tile_column.reshape(1, 256)),
        tile_count,
        in_hbm(atom_home.reshape(64, 128)),
        in_hbm(coupling.T),
        in_hbm(jnp.asarray(stencil_constants())),
    )


def solution(mesh):
    return jax.shard_map(
        per_device,
        mesh=mesh,
        in_specs=(
            P(None, "gz", "gy", "gx"),
            P("gz", "gy", "gx"),
            P(("gx", "gy", "gz"), None, None),
            P(("gx", "gy", "gz")),
            P(("gx", "gy", "gz")),
            P(("gx", "gy", "gz")),
            P(),
            P(("gx", "gy", "gz"), None),
        ),
        out_specs=P(None, "gz", "gy", "gx"),
        check_vma=False,
    )
```

```python
import jax
import jax.numpy as jnp
import numpy as np
from jax import lax
from jax.experimental import pallas as pl
from jax.experimental.pallas import tpu as pltpu
from jax.sharding import PartitionSpec as P

F32, BF16, I32 = jnp.float32, jnp.bfloat16, jnp.int32
STENCIL = (-205.0 / 72.0, 8.0 / 5.0, -1.0 / 5.0, 8.0 / 315.0, -1.0 / 560.0)
CENTER, HALF = 14.0, 10.0
STEPS = 4
DIRS = [(dx, dy) for dx in (-1, 0, 1) for dy in (-1, 0, 1)]
SELF = 4
XP, XM, YL, YH, ZH, RS0, RO0, BS0, BO0, NSEM = 0, 1, 2, 3, 4, 5, 14, 23, 32, 41
V0, PF0, PT0, ME0, CP0, PA0, OU0, FT0, NSET = 0, 6, 12, 15, 18, 28, 31, 37, 40


def stencil_constants():
    table = np.zeros((144, 128), np.float32)
    for x in range(128):
        for k in range(1, 5):
            if x + k < 128:
                table[x, x + k] = -0.5 * STENCIL[k]
            if x - k >= 0:
                table[x, x - k] = -0.5 * STENCIL[k]
    for j in range(4):
        table[128 + j, 124 + j] = 1.0
        table[132 + j, j] = 1.0
        for x in range(128):
            k = x + 4 - j
            if 1 <= k <= 4:
                table[136 + j, x] = -0.5 * STENCIL[k]
            k = 128 + j - x
            if 1 <= k <= 4:
                table[140 + j, x] = -0.5 * STENCIL[k]
    return table


def split(value):
    high = value.astype(BF16)
    return high, (value - high.astype(F32)).astype(BF16)


def dot_nt(a, b):
    return lax.dot_general(a, b, (((1,), (1,)), ((), ())), preferred_element_type=F32)


def dot_nn(a, b):
    return lax.dot_general(a, b, (((1,), (0,)), ((), ())), preferred_element_type=F32)


def dot_tn(a, b):
    return lax.dot_general(a, b, (((0,), (0,)), ((), ())), preferred_element_type=F32)


def kernel(
    orb, pot_in, tp, atom_hbm, column_hbm, count_in, home_hbm, cpl_hbm, table_hbm, out,
    X, Z, VH, VL, PF, PT, POT, META, MKB, NIDX, NMB, WT, LH, LHO, LSA, LSO, RS, RO, CS, CSO, SSA, SSO, SHA, SHO, SC, XS, XR, CB, CONST,
    PART, PART0, PTS, PTR, ZO, ORB, RL, RLO, atom_in, column_in, home_in, cpl_in, table,
    set_s, set_r, sem_s, sem_r, local_sem,
):
    ix, iy, iz = lax.axis_index("gx"), lax.axis_index("gy"), lax.axis_index("gz")
    zh, q = iz // 4, iz % 4
    oz = 1 - zh
    edge_block = 3 * oz
    below, above, across = (q + 3) % 4, (q + 1) % 4, (q + 2) % 4

    def dev(gx, gy, gz):
        return {"gx": gx, "gy": gy, "gz": gz}

    def ring(j):
        return dev(ix, iy, zh * 4 + (q + j) % 4)

    def near(dx, dy, half):
        return dev((ix + dx + 4) % 4, (iy + dy + 4) % 4, half * 4 + q)

    def exists(i):
        dx, dy = DIRS[i]
        return jnp.logical_and(
            jnp.logical_and(ix + dx >= 0, ix + dx <= 3), jnp.logical_and(iy + dy >= 0, iy + dy <= 3)
        )

    def copy(src, dst, s, r, to):
        return pltpu.make_async_remote_copy(
            src_ref=src, dst_ref=dst, send_sem=s, recv_sem=r, device_id=to, device_id_type=pl.DeviceIdType.MESH
        )

    barrier = pltpu.get_barrier_semaphore()
    peers = [near(dx, dy, half) for dx, dy in DIRS for half in (zh, oz)]
    peers = [p for i, p in enumerate(peers) if i != 2 * SELF]
    peers += [ring(j) for j in (1, 2, 3)]
    peers += [dev((ix + 2) % 4, iy, iz), dev(ix, (iy + 2) % 4, iz)]
    for peer in peers:
        pl.semaphore_signal(barrier, inc=1, device_id=peer, device_id_type=pl.DeviceIdType.MESH)
    take_proj = pltpu.make_async_copy(tp, PF, local_sem.at[0])
    take_orb = pltpu.make_async_copy(orb, ORB, local_sem.at[1])
    take_pot = pltpu.make_async_copy(pot_in, POT.at[pl.ds(4 * q, 4)], local_sem.at[2])
    take_own = pltpu.make_async_copy(
        orb.at[pl.ds(4 * q, 4)], X.at[1, :, pl.ds(4 + 4 * q, 4), pl.ds(8, 16), :], local_sem.at[3]
    )
    smalls = [
        pltpu.make_async_copy(src, dst, local_sem.at[4 + i])
        for i, (src, dst) in enumerate(
            (
                (atom_hbm, atom_in),
                (column_hbm, column_in),
                (cpl_hbm, cpl_in),
                (table_hbm, table),
                (home_hbm.at[pl.ds(2 * ((ix * 4 + iy) * 2 + zh), 2)], home_in),
            )
        )
    ]
    for c in smalls + [take_proj, take_orb, take_own, take_pot]:
        c.start()
    for c in smalls:
        c.wait()

    atom = atom_in[...]
    owner = lax.shift_right_logical(atom, 6)
    dx = lax.shift_right_logical(owner, 5) - ix + 1
    dy = jnp.bitwise_and(lax.shift_right_logical(owner, 3), 3) - iy + 1
    zb = jnp.bitwise_and(owner, 7) - 4 * zh
    pair = jnp.where(jnp.logical_and(zb >= 0, zb < 4), lax.shift_right_arithmetic(zb, 1), 2)
    number = (dx * 3 + dy) * 3 + pair
    lane = jnp.bitwise_and(zb, 1) * 64 + jnp.bitwise_and(atom, 63)
    column = jnp.where(lax.broadcasted_iota(I32, (1, 256), 1) < count_in[0], column_in[...], -1)
    META[pl.ds(q, 1)] = jnp.concatenate([number, lane, column] + [column] * 5, axis=0)[None]
    cpl = cpl_in[...]
    mine = 2 * ((ix * 4 + iy) * 8 + iz)
    CB[pl.ds(mine, 2), :] = jnp.concatenate(
        [jnp.concatenate([cpl[0:1], cpl[1:2]], axis=1), jnp.concatenate([cpl[2:3], cpl[3:4]], axis=1)], axis=0
    )

    row64 = lax.broadcasted_iota(I32, (64, 256), 0)
    row128 = lax.broadcasted_iota(I32, (128, 256), 0)

    def masks(b):
        mask = jnp.where(row64 == META[b, 2:3, :], 1.0, 0.0).astype(BF16)
        MKB[b, 0:64] = mask
        MKB[b, 64:128] = mask

    masks(q)

    def clear(i, _):
        X[i, :, pl.ds(20 * zh, 4)] = jnp.zeros((4, 4, 32, 128), F32)

        @pl.when(iy == 0)
        def _():
            X[i, :, 4:20, 0:8] = jnp.zeros((4, 16, 8, 128), F32)

        @pl.when(iy == 3)
        def _():
            X[i, :, 4:20, 24:32] = jnp.zeros((4, 16, 8, 128), F32)

        return 0

    lax.fori_loop(1, 5, clear, 0)

    def clear_sums(i, _):
        for slot in range(9):
            if slot != SELF:

                @pl.when(jnp.logical_not(exists(slot)))
                def _():
                    RS[i, slot] = jnp.zeros((2, 16, 128), F32)
                    RO[i, slot] = jnp.zeros((8, 128), F32)

        return 0

    lax.fori_loop(0, 4, clear_sums, 0)

    wx_h, wx_l = split(table[0:128, :])
    CONST[0:128, 0:128] = wx_h
    CONST[0:128, 128:256] = wx_l
    e2 = table[128:136, :].astype(BF16)
    edge_row = lax.broadcasted_iota(I32, (8, 128), 0)
    inside = jnp.where(
        edge_row < 4, jnp.where(ix > 0, 1.0, 0.0).astype(F32), jnp.where(ix < 3, 1.0, 0.0).astype(F32)
    )
    edge = table[136:144, :] * inside
    edge_h = edge.astype(BF16).astype(F32)
    edge_1 = jnp.concatenate([edge_h, edge_h], axis=0).astype(BF16)
    edge_2 = jnp.concatenate([edge - edge_h, edge - edge_h], axis=0).astype(BF16)

    take_proj.wait()
    for p in range(4):
        PT[q, p] = PF[pl.ds(p, 256, stride=4), :].T
    pl.semaphore_wait(barrier, len(peers))

    def field_block(index, block):
        return X.at[index, :, pl.ds(4 + 4 * block, 4), pl.ds(8, 16), :]

    sends = []

    def start(c):
        c.start()
        sends.append(c)
        return c

    def set_copy(src, dst, index, to):
        return copy(src, dst, set_s.at[index], set_r.at[index], to)

    def rows(first, count):
        return CB.at[pl.ds(first, count)]

    metas = [start(set_copy(META.at[q], META.at[q], ME0 + j - 1, ring(j))) for j in (1, 3, 2)]
    ring_cpl = [start(set_copy(rows(mine, 2), rows(mine, 2), CP0 + j - 1, ring(j))) for j in (1, 3, 2)]

    def around(source, target, relay, base):
        to_up = start(set_copy(source(across, 0, 2), relay.at[0], base, ring(1)))
        to_down = start(set_copy(source(across, 2, 2), relay.at[1], base + 1, ring(3)))
        near_up = start(set_copy(source(above, 0, 4), target(q, 0, 4), base + 2, ring(1)))
        near_down = start(set_copy(source(below, 0, 4), target(q, 0, 4), base + 3, ring(3)))

        def forward():
            to_up.wait_recv()
            far_up = start(set_copy(relay.at[0], target(below, 0, 2), base + 4, ring(1)))
            to_down.wait_recv()
            far_down = start(set_copy(relay.at[1], target(above, 2, 2), base + 5, ring(3)))
            return near_up, near_down, far_up, far_down

        return forward

    values_on = around(
        lambda block, o, n: orb.at[pl.ds(4 * block + o, n)],
        lambda block, o, n: X.at[1, pl.ds(o, n), pl.ds(4 + 4 * block, 4), pl.ds(8, 16), :],
        RL,
        V0,
    )

    def tile_sums(vh, vl, b, result, at):
        for o in range(4):
            r = dot_tn(jnp.concatenate([vh[o], vl[o]], axis=0), MKB[b])
            for p in range(4):
                result[at, pl.ds(p * 4 + o, 1), :] = jnp.sum(r * PT[b, p], axis=0, keepdims=True)

    take_orb.wait()

    def own_sums(g, _):
        vh, vl = split(ORB[pl.ds(4 * g, 4)].reshape(4, 64, 128))
        tile_sums(vh, vl, q, PART0, g)
        return 0

    lax.fori_loop(0, 4, own_sums, 0)
    values = values_on()
    parts = [start(set_copy(PART0.at[(q + j) % 4], PART.at[q], PA0 + j - 1, ring(j))) for j in (2, 1, 3)]
    half = [pl.ds(0, 2), pl.ds(2, 2)]
    up = [start(set_copy(PT.at[q, half[h]], PT.at[q, half[h]], PF0 + h, ring(1))) for h in (0, 1)]
    down = [start(set_copy(PT.at[q, half[h]], PT.at[q, half[h]], PF0 + 3 - h, ring(3))) for h in (1, 0)]
    pots = [start(set_copy(pot_in, POT.at[pl.ds(4 * q, 4)], PT0 + j - 1, ring(j))) for j in (1, 3, 2)]
    PART[pl.ds(q, 1)] = PART0[pl.ds(q, 1)]

    for c in ring_cpl:
        c.wait_recv()
    group = 2 * ((ix * 4 + iy) * 8 + zh * 4)
    flip = start(set_copy(rows(group, 8), rows(group, 8), CP0 + 3, dev(ix, iy, oz * 4 + q)))

    for c in metas:
        c.wait_recv()
    masks(below)
    masks(above)
    masks(across)
    for b in range(4):
        index = META[b]
        hot = jnp.where(row128 == index[1:2, :], 1.0, 0.0).astype(BF16)
        WT[b, 0:128] = hot
        WT[b, 128:256] = hot
        number = jnp.broadcast_to(index[0:1, :], (16, 256))
        NIDX[b] = number
        for n in range(27):
            NMB[b, n] = jnp.where(number == n, 1.0, 0.0).astype(BF16)

    flip.wait_recv()
    group = 2 * ((ix * 4 + iy) * 8)
    cpl_y = [
        start(set_copy(rows(group, 16), rows(group, 16), CP0 + 3 + j, dev(ix, (iy + j) % 4, iz))) for j in (1, 3, 2)
    ]

    def step_copies(s):
        cur = s + 1

        def sc(src, dst, index, to):
            return copy(src, dst, sem_s.at[s, index], sem_r.at[s, index], to)

        c = {}
        c["xp"] = sc(XS.at[s, pl.ds(0, 4)], XR.at[s, pl.ds(0, 4)], XP, dev((ix + 1) % 4, iy, iz))
        c["xm"] = sc(XS.at[s, pl.ds(4, 4)], XR.at[s, pl.ds(4, 4)], XM, dev((ix + 3) % 4, iy, iz))
        inner = pl.ds(4, 16)
        c["yl"] = sc(
            X.at[cur, :, inner, pl.ds(8, 4), :], X.at[cur, :, inner, pl.ds(24, 4), :], YL, dev(ix, (iy + 3) % 4, iz)
        )
        c["yh"] = sc(
            X.at[cur, :, inner, pl.ds(20, 4), :], X.at[cur, :, inner, pl.ds(4, 4), :], YH, dev(ix, (iy + 1) % 4, iz)
        )
        c["z"] = sc(
            X.at[cur, :, pl.ds(4 + 12 * oz, 4), pl.ds(8, 16), :],
            X.at[cur, :, pl.ds(20 * zh, 4), pl.ds(8, 16), :],
            ZH,
            dev(ix, iy, oz * 4 + q),
        )
        for i, (dx, dy) in enumerate(DIRS):
            slot = 8 - i
            if i != SELF:
                c["rs", i] = sc(LSA.at[s, i], RS.at[s, slot], RS0 + slot, near(dx, dy, zh))
                c["bs", i] = sc(CS.at[s], SSA.at[s, slot], BS0 + slot, near(dx, dy, zh))
            c["ro", i] = sc(LSO.at[s, i], RO.at[s, slot], RO0 + slot, near(dx, dy, oz))
            c["bo", i] = sc(CSO.at[s], SSO.at[s, slot], BO0 + slot, near(dx, dy, oz))
        return c

    def when(condition, action):
        @pl.when(condition)
        def _():
            action()

    def neighbours(c, names, action, mirrored):
        for i in range(9):
            def both(i=i):
                for name in names:
                    if (name, i) in c:
                        getattr(c[name, i], action)()

            if i == SELF:
                both()
            else:
                when(exists(8 - i if mirrored else i), both)

    def send_y(c):
        when(iy > 0, c["yl"].start)
        when(iy < 3, c["yh"].start)

    def pack_x(s, c):
        vh_all = VH[...].reshape(1024, 128)
        vl_all = VL[...].reshape(1024, 128)
        XS[s] = dot_nt(e2, vh_all) + dot_nt(e2, vl_all)
        xp = dot_nt(jnp.concatenate([vh_all, vh_all], axis=1), CONST[...]) + dot_nt(vl_all, CONST[:, 0:128])
        Z[...] = xp.reshape(4, 16, 16, 128)
        c["xp"].start()
        c["xm"].start()

    def turn(value):
        return pltpu.roll(value.reshape(-1, 128), 64, 1).reshape(value.shape)

    def sums_for_other_half(s, c):
        ph, pl_ = split(PART[edge_block])
        for i in range(9):
            m = NMB[edge_block, 3 * i + 2]
            LHO[i, 0:16] = ph * m
            LHO[i, 16:32] = pl_ * m
        sums = dot_nt(LHO[...].reshape(288, 256), WT[edge_block, 0:128]).reshape(9, 32, 128)
        sums = sums[:, 0:16] + sums[:, 16:32]
        LSO[s] = sums[:, 0:8] + turn(sums[:, 8:16])
        neighbours(c, ("ro",), "start", False)

    def sums_for_own_half(s, c):
        for b in range(4):
            ph, pl_ = split(PART[b])
            for i in range(9):
                for pair in range(2):
                    m = NMB[b, 3 * i + pair]
                    LH[2 * i + pair, 0:16, b * 256 : (b + 1) * 256] = ph * m
                    LH[2 * i + pair, 16:32, b * 256 : (b + 1) * 256] = pl_ * m
        sums = None
        for b in range(4):
            lhs = LH[:, :, b * 256 : (b + 1) * 256].reshape(576, 256)
            term = dot_nt(lhs, WT[b, 0:128])
            sums = term if sums is None else sums + term
        sums = sums.reshape(18, 32, 128)
        LSA[s] = (sums[:, 0:16] + sums[:, 16:32]).reshape(9, 2, 16, 128)
        neighbours(c, ("rs",), "start", False)

    def stencil(s, c, first):
        c["xp"].wait_recv()
        c["xm"].wait_recv()
        xr = XR[s]
        xr_h = xr.astype(BF16).astype(F32)
        faces = jnp.concatenate([xr_h, xr - xr_h], axis=0).astype(BF16)
        Z[...] = Z[...] + (dot_tn(faces, edge_1) + dot_tn(faces, edge_2)).reshape(4, 16, 16, 128)
        c["z"].wait_recv()
        when(iy > 0, c["yh"].wait_recv)
        when(iy < 3, c["yl"].wait_recv)
        cur = s + 1
        scale = (1.0 if first else 2.0) / HALF

        def line(i, _):
            o = i // 16
            z = i % 16
            v0 = X[cur, o, z + 4, 8:24, :]
            acc = Z[o, z] + v0 * (POT[z] + (-1.5 * STENCIL[0] - CENTER))
            for k in range(1, 5):
                around = (X[cur, o, z + 4 - k, 8:24, :] + X[cur, o, z + 4 + k, 8:24, :]) + (
                    X[cur, o, z + 4, 8 - k : 24 - k, :] + X[cur, o, z + 4, 8 + k : 24 + k, :]
                )
                acc = acc + (-0.5 * STENCIL[k]) * around
            acc = scale * acc
            Z[o, z] = acc if first else acc - X[s, o, z + 4, 8:24, :]
            return 0

        lax.fori_loop(0, 64, line, 0, unroll=4)

    def scale_totals(s, c, first):
        neighbours(c, ("rs", "ro"), "wait_recv", True)
        total = LSA[s, SELF]
        other = None
        for slot in range(9):
            if slot != SELF:
                total = total + RS[s, slot]
            other = RO[s, slot] if other is None else other + RO[s, slot]
        theirs = lax.broadcasted_iota(I32, (8, 128), 1) // 64 == oz
        other = jnp.concatenate([jnp.where(theirs, other, 0.0), jnp.where(theirs, turn(other), 0.0)], axis=0)
        at_0 = jnp.where(zh == 1, 1.0, 0.0).astype(F32)
        scale = (1.0 if first else 2.0) / HALF
        scaled = scale * SC[...] * jnp.stack([total[0] + at_0 * other, total[1] + (1.0 - at_0) * other])
        CS[s] = scaled
        edge_pair = at_0 * scaled[0] + (1.0 - at_0) * scaled[1]
        CSO[s] = jnp.where(theirs, edge_pair[0:8], turn(edge_pair[8:16]))
        SSA[s, SELF] = scaled
        neighbours(c, ("bo", "bs"), "start", False)

    def take_same(s, c):
        neighbours(c, ("bs",), "wait_recv", True)
        sh, sl = split(SSA[s].reshape(288, 128))
        SHA[:, 0:128] = sh
        SHA[:, 128:256] = sl

    def take_other(s, c):
        neighbours(c, ("bo",), "wait_recv", True)
        packed = SSO[s]
        sh, sl = split(jnp.concatenate([packed, turn(packed)], axis=1).reshape(144, 128))
        SHO[:, 0:128] = sh
        SHO[:, 128:256] = sl

    def per_tile(b, with_other):
        r = dot_nn(SHA[...], WT[b])
        number = NIDX[b]
        pt = jnp.zeros((16, 256), F32)
        for i in range(9):
            for pair in range(2):
                k = 2 * i + pair
                pt = pt + jnp.where(number == 3 * i + pair, r[k * 16 : (k + 1) * 16], 0.0)
        if with_other:
            r = dot_nn(SHO[...], WT[b])
            for i in range(9):
                pt = pt + jnp.where(number == 3 * i + 2, r[i * 16 : (i + 1) * 16], 0.0)
        return pt

    def project(pt, b):
        mask = MKB[b, 0:64]
        results = []
        for o in range(4):
            r = PT[b, 0] * pt[o : o + 1]
            for p in range(1, 4):
                r = r + PT[b, p] * pt[p * 4 + o : p * 4 + o + 1]
            rh, rl = split(r)
            results.append(dot_nt(mask, rh) + dot_nt(mask, rl))
        return jnp.stack(results)

    def apply(s, b, with_other):
        y = Z[:, pl.ds(4 * b, 4)] + project(per_tile(b, with_other), b).reshape(4, 4, 16, 128)
        X[s + 2, :, pl.ds(4 + 4 * b, 4), 8:24, :] = y
        yh, yl = split(y)
        VH[:, pl.ds(4 * b, 4)] = yh
        VL[:, pl.ds(4 * b, 4)] = yl

    c = step_copies(0)
    take_own.wait()
    for v in values:
        v.wait_recv()
    c["z"].start()
    send_y(c)
    for v in parts:
        v.wait_recv()
    sums_for_other_half(0, c)
    sums_for_own_half(0, c)
    for v in cpl_y:
        v.wait_recv()
    group = 2 * (ix * 32)
    cpl_x = [
        start(set_copy(rows(group, 64), rows(group, 64), CP0 + 6 + j, dev((ix + j) % 4, iy, iz))) for j in (1, 3, 2)
    ]
    high, low = split(X[1, :, 4:20, 8:24, :])
    VH[...] = high
    VL[...] = low
    pack_x(0, c)
    for v in cpl_x:
        v.wait_recv()
    home2 = home_in[...]
    home = jnp.concatenate([home2[0:1], home2[1:2]], axis=1)
    home_row = 2 * lax.shift_right_logical(home, 6)
    rows256 = lax.broadcasted_iota(I32, (256, 256), 0)
    lane_hot = jnp.where(row64 == jnp.bitwise_and(home, 63), 1.0, 0.0).astype(F32)
    cb = CB[...]
    cb_1 = cb.astype(BF16)
    rest = cb - cb_1.astype(F32)
    cb_2 = rest.astype(BF16)
    cb_3 = (rest - cb_2.astype(F32)).astype(BF16)
    for r in range(2):
        pick = jnp.where(rows256 == home_row + r, 1.0, 0.0).astype(BF16)
        found = dot_tn(cb_1, pick) + dot_tn(cb_2, pick) + dot_tn(cb_3, pick)
        for p2 in range(2):
            line = jnp.sum(found[p2 * 64 : (p2 + 1) * 64] * lane_hot, axis=0, keepdims=True)
            p = 2 * r + p2
            for pair in range(2):
                SC[pair, p * 4 : (p + 1) * 4, :] = jnp.broadcast_to(line[:, pair * 128 : (pair + 1) * 128], (4, 128))

    scale_totals(0, c, True)

    up[0].wait_recv()
    on_up = start(set_copy(PT.at[below, half[0]], PT.at[below, half[0]], PF0 + 4, ring(1)))
    down[0].wait_recv()
    on_down = start(set_copy(PT.at[above, half[1]], PT.at[above, half[1]], PF0 + 5, ring(3)))
    take_pot.wait()
    for v in pots:
        v.wait_recv()
    stencil(0, c, True)
    def block_sums(b):
        vh = VH[:, pl.ds(4 * b, 4)].reshape(4, 64, 128)
        vl = VL[:, pl.ds(4 * b, 4)].reshape(4, 64, 128)
        tile_sums(vh, vl, b, PART, b)

    def rest_of_step(s, c):
        sums_for_own_half(s, c)
        c["z"].start()
        send_y(c)
        pack_x(s, c)
        scale_totals(s, c, False)
        stencil(s, c, False)

    take_same(0, c)
    take_other(0, c)
    c = step_copies(1)
    for b, arrivals in ((q, ()), (below, (up[1],)), (above, (down[1],)), (across, (on_up, on_down))):
        for v in arrivals:
            v.wait_recv()
        apply(0, b, True)
        block_sums(b)
    sums_for_other_half(1, c)
    rest_of_step(1, c)

    def step(s, _):
        before = step_copies(s - 1)
        c = step_copies(s)
        take_same(s - 1, before)
        take_other(s - 1, before)
        apply(s - 1, edge_block, True)
        block_sums(edge_block)
        sums_for_other_half(s, c)

        def one(j, _):
            b = (edge_block + j) % 4
            apply(s - 1, b, False)
            block_sums(b)
            return 0

        lax.fori_loop(1, 4, one, 0)
        rest_of_step(s, c)
        return 0

    lax.fori_loop(2, STEPS, step, 0)

    last = STEPS - 1
    c = step_copies(last)
    outs_on = around(
        lambda block, o, n: Z.at[pl.ds(o, n), pl.ds(4 * block, 4)],
        lambda block, o, n: ZO.at[pl.ds(4 * block + o, n)],
        RLO,
        OU0,
    )
    outs = outs_on()
    take_same(last, c)
    take_other(last, c)
    finals = []
    for j in (2, 1, 3):
        b = (q + j) % 4
        PTS[pl.ds(b, 1)] = per_tile(b, True)[None]
        finals.append(start(set_copy(PTS.at[b], PTR.at[q], FT0 + j - 1, ring(j))))
    result = Z[:, pl.ds(4 * q, 4)] + project(per_tile(q, True), q).reshape(4, 4, 16, 128)
    out[pl.ds(4 * q, 4)] = result
    for v in outs:
        v.wait_recv()
    for index, j in ((1, 1), (2, 3), (0, 2)):
        finals[index].wait_recv()
        g = (q - j + 4) % 4
        out[pl.ds(4 * g, 4)] = ZO[pl.ds(4 * g, 4)] + project(PTR[g], q).reshape(4, 4, 16, 128)
    for v in sends:
        v.wait_send()

    def drain(s, _):
        c = step_copies(s)
        for name in ("xp", "xm", "z"):
            c[name].wait_send()
        when(iy > 0, c["yl"].wait_send)
        when(iy < 3, c["yh"].wait_send)
        neighbours(c, ("rs", "ro", "bs", "bo"), "wait_send", False)
        return 0

    lax.fori_loop(0, STEPS, drain, 0)


def per_device(orbitals, potential, tile_proj, tile_atom, tile_column, tile_count, atom_home, coupling):
    vmem = pl.BlockSpec(memory_space=pltpu.VMEM)
    hbm = pl.BlockSpec(memory_space=pltpu.HBM)
    smem = pl.BlockSpec(memory_space=pltpu.SMEM)

    def in_hbm(x):
        return pltpu.with_memory_space_constraint(x, pltpu.HBM)

    return pl.pallas_call(
        kernel,
        out_shape=jax.ShapeDtypeStruct((16, 4, 16, 128), F32),
        in_specs=[hbm] * 5 + [smem] + [hbm] * 3,
        out_specs=vmem,
        scratch_shapes=[
            pltpu.VMEM((6, 4, 24, 32, 128), F32),
            pltpu.VMEM((4, 16, 16, 128), F32),
            pltpu.VMEM((4, 16, 16, 128), BF16),
            pltpu.VMEM((4, 16, 16, 128), BF16),
            pltpu.VMEM((1024, 128), F32),
            pltpu.VMEM((4, 4, 128, 256), F32),
            pltpu.VMEM((16, 16, 128), F32),
            pltpu.VMEM((4, 8, 256), I32),
            pltpu.VMEM((4, 128, 256), BF16),
            pltpu.VMEM((4, 16, 256), I32),
            pltpu.VMEM((4, 27, 16, 256), BF16),
            pltpu.VMEM((4, 256, 256), BF16),
            pltpu.VMEM((18, 32, 1024), BF16),
            pltpu.VMEM((9, 32, 256), BF16),
            pltpu.VMEM((4, 9, 2, 16, 128), F32),
            pltpu.VMEM((4, 9, 8, 128), F32),
            pltpu.VMEM((4, 9, 2, 16, 128), F32),
            pltpu.VMEM((4, 9, 8, 128), F32),
            pltpu.VMEM((4, 2, 16, 128), F32),
            pltpu.VMEM((4, 8, 128), F32),
            pltpu.VMEM((4, 9, 2, 16, 128), F32),
            pltpu.VMEM((4, 9, 8, 128), F32),
            pltpu.VMEM((288, 256), BF16),
            pltpu.VMEM((144, 256), BF16),
            pltpu.VMEM((2, 16, 128), F32),
            pltpu.VMEM((4, 8, 1024), F32),
            pltpu.VMEM((4, 8, 1024), F32),
            pltpu.VMEM((256, 128), F32),
            pltpu.VMEM((128, 256), BF16),
            pltpu.VMEM((4, 16, 256), F32),
            pltpu.VMEM((4, 16, 256), F32),
            pltpu.VMEM((4, 16, 256), F32),
            pltpu.VMEM((4, 16, 256), F32),
            pltpu.VMEM((16, 4, 16, 128), F32),
            pltpu.VMEM((16, 4, 16, 128), F32),
            pltpu.VMEM((2, 2, 4, 16, 128), F32),
            pltpu.VMEM((2, 2, 4, 16, 128), F32),
            pltpu.VMEM((1, 256), I32),
            pltpu.VMEM((1, 256), I32),
            pltpu.VMEM((2, 128), I32),
            pltpu.VMEM((4, 64), F32),
            pltpu.VMEM((144, 128), F32),
            pltpu.SemaphoreType.DMA((NSET,)),
            pltpu.SemaphoreType.DMA((NSET,)),
            pltpu.SemaphoreType.DMA((STEPS, NSEM)),
            pltpu.SemaphoreType.DMA((STEPS, NSEM)),
            pltpu.SemaphoreType.DMA((9,)),
        ],
        compiler_params=pltpu.CompilerParams(
            collective_id=0, has_side_effects=True, vmem_limit_bytes=40000 * 1024
        ),
        name="chebyshev",
    )(
        in_hbm(orbitals),
        in_hbm(potential),
        in_hbm(tile_proj.reshape(1024, 128)),
        in_hbm(tile_atom.reshape(1, 256)),
        in_hbm(tile_column.reshape(1, 256)),
        tile_count,
        in_hbm(atom_home.reshape(64, 128)),
        in_hbm(coupling.T),
        in_hbm(jnp.asarray(stencil_constants())),
    )


def solution(mesh):
    return jax.shard_map(
        per_device,
        mesh=mesh,
        in_specs=(
            P(None, "gz", "gy", "gx"),
            P("gz", "gy", "gx"),
            P(("gx", "gy", "gz"), None, None),
            P(("gx", "gy", "gz")),
            P(("gx", "gy", "gz")),
            P(("gx", "gy", "gz")),
            P(),
            P(("gx", "gy", "gz"), None),
        ),
        out_specs=P(None, "gz", "gy", "gx"),
        check_vma=False,
    )
```

```python
import jax
import jax.numpy as jnp
import numpy as np
from jax import lax
from jax.experimental import pallas as pl
from jax.experimental.pallas import tpu as pltpu
from jax.sharding import PartitionSpec as P

F32, BF16, I32 = jnp.float32, jnp.bfloat16, jnp.int32
STENCIL = (-205.0 / 72.0, 8.0 / 5.0, -1.0 / 5.0, 8.0 / 315.0, -1.0 / 560.0)
CENTER, HALF = 14.0, 10.0
STEPS = 4
DIRS = [(dx, dy) for dx in (-1, 0, 1) for dy in (-1, 0, 1)]
SELF = 4
XP, XM, YL, YH, ZH, RS0, RO0, BS0, BO0, NSEM = 0, 1, 2, 3, 4, 5, 14, 23, 32, 41
V0, PF0, PT0, ME0, CP0, PA0, OU0, FT0, NSET = 0, 6, 12, 15, 18, 28, 31, 37, 40


def stencil_constants():
    table = np.zeros((144, 128), np.float32)
    for x in range(128):
        for k in range(1, 5):
            if x + k < 128:
                table[x, x + k] = -0.5 * STENCIL[k]
            if x - k >= 0:
                table[x, x - k] = -0.5 * STENCIL[k]
    for j in range(4):
        table[128 + j, 124 + j] = 1.0
        table[132 + j, j] = 1.0
        for x in range(128):
            k = x + 4 - j
            if 1 <= k <= 4:
                table[136 + j, x] = -0.5 * STENCIL[k]
            k = 128 + j - x
            if 1 <= k <= 4:
                table[140 + j, x] = -0.5 * STENCIL[k]
    return table


def split(value):
    high = value.astype(BF16)
    return high, (value - high.astype(F32)).astype(BF16)


def dot_nt(a, b):
    return lax.dot_general(a, b, (((1,), (1,)), ((), ())), preferred_element_type=F32)


def dot_nn(a, b):
    return lax.dot_general(a, b, (((1,), (0,)), ((), ())), preferred_element_type=F32)


def dot_tn(a, b):
    return lax.dot_general(a, b, (((0,), (0,)), ((), ())), preferred_element_type=F32)


def kernel(
    orb, pot_in, tp, atom_hbm, column_hbm, count_in, home_hbm, cpl_hbm, table_hbm, out,
    X, Z, VH, VL, PF, PT, POT, META, MKB, NIDX, NMB, WT, LH, LHO, LSA, LSO, RS, RO, CS, CSO, SSA, SSO, SHA, SHO, SC, XS, XR, CB, CONST,
    PART, PART0, PTS, PTR, ZO, ORB, RL, RLO, atom_in, column_in, home_in, cpl_in, table,
    set_s, set_r, sem_s, sem_r, local_sem,
):
    ix, iy, iz = lax.axis_index("gx"), lax.axis_index("gy"), lax.axis_index("gz")
    zh, q = iz // 4, iz % 4
    oz = 1 - zh
    edge_block = 3 * oz
    below, above, across = (q + 3) % 4, (q + 1) % 4, (q + 2) % 4

    def dev(gx, gy, gz):
        return {"gx": gx, "gy": gy, "gz": gz}

    def ring(j):
        return dev(ix, iy, zh * 4 + (q + j) % 4)

    def near(dx, dy, half):
        return dev((ix + dx + 4) % 4, (iy + dy + 4) % 4, half * 4 + q)

    def exists(i):
        dx, dy = DIRS[i]
        return jnp.logical_and(
            jnp.logical_and(ix + dx >= 0, ix + dx <= 3), jnp.logical_and(iy + dy >= 0, iy + dy <= 3)
        )

    def copy(src, dst, s, r, to):
        return pltpu.make_async_remote_copy(
            src_ref=src, dst_ref=dst, send_sem=s, recv_sem=r, device_id=to, device_id_type=pl.DeviceIdType.MESH
        )

    barrier = pltpu.get_barrier_semaphore()
    peers = [near(dx, dy, half) for dx, dy in DIRS for half in (zh, oz)]
    peers = [p for i, p in enumerate(peers) if i != 2 * SELF]
    peers += [ring(j) for j in (1, 2, 3)]
    peers += [dev((ix + 2) % 4, iy, iz), dev(ix, (iy + 2) % 4, iz)]
    for peer in peers:
        pl.semaphore_signal(barrier, inc=1, device_id=peer, device_id_type=pl.DeviceIdType.MESH)
    take_proj = pltpu.make_async_copy(tp, PF, local_sem.at[0])
    take_orb = pltpu.make_async_copy(orb, ORB, local_sem.at[1])
    take_pot = pltpu.make_async_copy(pot_in, POT.at[pl.ds(4 * q, 4)], local_sem.at[2])
    take_own = pltpu.make_async_copy(
        orb.at[pl.ds(4 * q, 4)], X.at[1, :, pl.ds(4 + 4 * q, 4), pl.ds(8, 16), :], local_sem.at[3]
    )
    smalls = [
        pltpu.make_async_copy(src, dst, local_sem.at[4 + i])
        for i, (src, dst) in enumerate(
            (
                (atom_hbm, atom_in),
                (column_hbm, column_in),
                (cpl_hbm, cpl_in),
                (table_hbm, table),
                (home_hbm.at[pl.ds(2 * ((ix * 4 + iy) * 2 + zh), 2)], home_in),
            )
        )
    ]
    for c in smalls + [take_proj, take_orb, take_own, take_pot]:
        c.start()
    for c in smalls:
        c.wait()

    atom = atom_in[...]
    owner = lax.shift_right_logical(atom, 6)
    dx = lax.shift_right_logical(owner, 5) - ix + 1
    dy = jnp.bitwise_and(lax.shift_right_logical(owner, 3), 3) - iy + 1
    zb = jnp.bitwise_and(owner, 7) - 4 * zh
    pair = jnp.where(jnp.logical_and(zb >= 0, zb < 4), lax.shift_right_arithmetic(zb, 1), 2)
    number = (dx * 3 + dy) * 3 + pair
    lane = jnp.bitwise_and(zb, 1) * 64 + jnp.bitwise_and(atom, 63)
    column = jnp.where(lax.broadcasted_iota(I32, (1, 256), 1) < count_in[0], column_in[...], -1)
    META[pl.ds(q, 1)] = jnp.concatenate([number, lane, column] + [column] * 5, axis=0)[None]
    cpl = cpl_in[...]
    mine = 2 * ((ix * 4 + iy) * 8 + iz)
    CB[pl.ds(mine, 2), :] = jnp.concatenate(
        [jnp.concatenate([cpl[0:1], cpl[1:2]], axis=1), jnp.concatenate([cpl[2:3], cpl[3:4]], axis=1)], axis=0
    )

    row64 = lax.broadcasted_iota(I32, (64, 256), 0)
    row128 = lax.broadcasted_iota(I32, (128, 256), 0)

    def masks(b):
        mask = jnp.where(row64 == META[b, 2:3, :], 1.0, 0.0).astype(BF16)
        MKB[b, 0:64] = mask
        MKB[b, 64:128] = mask

    masks(q)

    def clear(i, _):
        X[i, :, pl.ds(20 * zh, 4)] = jnp.zeros((4, 4, 32, 128), F32)

        @pl.when(iy == 0)
        def _():
            X[i, :, 4:20, 0:8] = jnp.zeros((4, 16, 8, 128), F32)

        @pl.when(iy == 3)
        def _():
            X[i, :, 4:20, 24:32] = jnp.zeros((4, 16, 8, 128), F32)

        return 0

    lax.fori_loop(1, 5, clear, 0)

    def clear_sums(i, _):
        for slot in range(9):
            if slot != SELF:

                @pl.when(jnp.logical_not(exists(slot)))
                def _():
                    RS[i, slot] = jnp.zeros((2, 16, 128), F32)
                    RO[i, slot] = jnp.zeros((8, 128), F32)

        return 0

    lax.fori_loop(0, 4, clear_sums, 0)

    wx_h, wx_l = split(table[0:128, :])
    CONST[0:128, 0:128] = wx_h
    CONST[0:128, 128:256] = wx_l
    e2 = table[128:136, :].astype(BF16)
    edge_row = lax.broadcasted_iota(I32, (8, 128), 0)
    inside = jnp.where(
        edge_row < 4, jnp.where(ix > 0, 1.0, 0.0).astype(F32), jnp.where(ix < 3, 1.0, 0.0).astype(F32)
    )
    edge = table[136:144, :] * inside
    edge_h = edge.astype(BF16).astype(F32)
    edge_1 = jnp.concatenate([edge_h, edge_h], axis=0).astype(BF16)
    edge_2 = jnp.concatenate([edge - edge_h, edge - edge_h], axis=0).astype(BF16)

    take_proj.wait()
    for p in range(4):
        PT[q, p] = PF[pl.ds(p, 256, stride=4), :].T
    pl.semaphore_wait(barrier, len(peers))

    def field_block(index, block):
        return X.at[index, :, pl.ds(4 + 4 * block, 4), pl.ds(8, 16), :]

    sends = []

    def start(c):
        c.start()
        sends.append(c)
        return c

    def set_copy(src, dst, index, to):
        return copy(src, dst, set_s.at[index], set_r.at[index], to)

    def rows(first, count):
        return CB.at[pl.ds(first, count)]

    metas = [start(set_copy(META.at[q], META.at[q], ME0 + j - 1, ring(j))) for j in (1, 3, 2)]
    ring_cpl = [start(set_copy(rows(mine, 2), rows(mine, 2), CP0 + j - 1, ring(j))) for j in (1, 3, 2)]

    def around(source, target, relay, base):
        to_up = start(set_copy(source(across, 0, 2), relay.at[0], base, ring(1)))
        to_down = start(set_copy(source(across, 2, 2), relay.at[1], base + 1, ring(3)))
        near_up = start(set_copy(source(above, 0, 4), target(q, 0, 4), base + 2, ring(1)))
        near_down = start(set_copy(source(below, 0, 4), target(q, 0, 4), base + 3, ring(3)))

        def forward():
            to_up.wait_recv()
            far_up = start(set_copy(relay.at[0], target(below, 0, 2), base + 4, ring(1)))
            to_down.wait_recv()
            far_down = start(set_copy(relay.at[1], target(above, 2, 2), base + 5, ring(3)))
            return near_up, near_down, far_up, far_down

        return forward

    values_on = around(
        lambda block, o, n: orb.at[pl.ds(4 * block + o, n)],
        lambda block, o, n: X.at[1, pl.ds(o, n), pl.ds(4 + 4 * block, 4), pl.ds(8, 16), :],
        RL,
        V0,
    )

    def tile_sums(vh, vl, b, result, at):
        for o in range(4):
            r = dot_tn(jnp.concatenate([vh[o], vl[o]], axis=0), MKB[b])
            for p in range(4):
                result[at, pl.ds(p * 4 + o, 1), :] = jnp.sum(r * PT[b, p], axis=0, keepdims=True)

    take_orb.wait()

    def own_sums(g, _):
        vh, vl = split(ORB[pl.ds(4 * g, 4)].reshape(4, 64, 128))
        tile_sums(vh, vl, q, PART0, g)
        return 0

    lax.fori_loop(0, 4, own_sums, 0)
    values = values_on()
    parts = [start(set_copy(PART0.at[(q + j) % 4], PART.at[q], PA0 + j - 1, ring(j))) for j in (2, 1, 3)]
    half = [pl.ds(0, 2), pl.ds(2, 2)]
    up = [start(set_copy(PT.at[q, half[h]], PT.at[q, half[h]], PF0 + h, ring(1))) for h in (0, 1)]
    down = [start(set_copy(PT.at[q, half[h]], PT.at[q, half[h]], PF0 + 3 - h, ring(3))) for h in (1, 0)]
    pots = [start(set_copy(pot_in, POT.at[pl.ds(4 * q, 4)], PT0 + j - 1, ring(j))) for j in (1, 3, 2)]
    PART[pl.ds(q, 1)] = PART0[pl.ds(q, 1)]

    for c in ring_cpl:
        c.wait_recv()
    group = 2 * ((ix * 4 + iy) * 8 + zh * 4)
    flip = start(set_copy(rows(group, 8), rows(group, 8), CP0 + 3, dev(ix, iy, oz * 4 + q)))

    for c in metas:
        c.wait_recv()
    masks(below)
    masks(above)
    masks(across)
    for b in range(4):
        index = META[b]
        hot = jnp.where(row128 == index[1:2, :], 1.0, 0.0).astype(BF16)
        WT[b, 0:128] = hot
        WT[b, 128:256] = hot
        number = jnp.broadcast_to(index[0:1, :], (16, 256))
        NIDX[b] = number
        for n in range(27):
            NMB[b, n] = jnp.where(number == n, 1.0, 0.0).astype(BF16)

    flip.wait_recv()
    group = 2 * ((ix * 4 + iy) * 8)
    cpl_y = [
        start(set_copy(rows(group, 16), rows(group, 16), CP0 + 3 + j, dev(ix, (iy + j) % 4, iz))) for j in (1, 3, 2)
    ]

    def step_copies(s):
        cur = s + 1

        def sc(src, dst, index, to):
            return copy(src, dst, sem_s.at[s, index], sem_r.at[s, index], to)

        c = {}
        c["xp"] = sc(XS.at[s, pl.ds(0, 4)], XR.at[s, pl.ds(0, 4)], XP, dev((ix + 1) % 4, iy, iz))
        c["xm"] = sc(XS.at[s, pl.ds(4, 4)], XR.at[s, pl.ds(4, 4)], XM, dev((ix + 3) % 4, iy, iz))
        inner = pl.ds(4, 16)
        c["yl"] = sc(
            X.at[cur, :, inner, pl.ds(8, 4), :], X.at[cur, :, inner, pl.ds(24, 4), :], YL, dev(ix, (iy + 3) % 4, iz)
        )
        c["yh"] = sc(
            X.at[cur, :, inner, pl.ds(20, 4), :], X.at[cur, :, inner, pl.ds(4, 4), :], YH, dev(ix, (iy + 1) % 4, iz)
        )
        c["z"] = sc(
            X.at[cur, :, pl.ds(4 + 12 * oz, 4), pl.ds(8, 16), :],
            X.at[cur, :, pl.ds(20 * zh, 4), pl.ds(8, 16), :],
            ZH,
            dev(ix, iy, oz * 4 + q),
        )
        for i, (dx, dy) in enumerate(DIRS):
            slot = 8 - i
            if i != SELF:
                c["rs", i] = sc(LSA.at[s, i], RS.at[s, slot], RS0 + slot, near(dx, dy, zh))
                c["bs", i] = sc(CS.at[s], SSA.at[s, slot], BS0 + slot, near(dx, dy, zh))
            c["ro", i] = sc(LSO.at[s, i], RO.at[s, slot], RO0 + slot, near(dx, dy, oz))
            c["bo", i] = sc(CSO.at[s], SSO.at[s, slot], BO0 + slot, near(dx, dy, oz))
        return c

    def when(condition, action):
        @pl.when(condition)
        def _():
            action()

    def neighbours(c, names, action, mirrored):
        for i in range(9):
            def both(i=i):
                for name in names:
                    if (name, i) in c:
                        getattr(c[name, i], action)()

            if i == SELF:
                both()
            else:
                when(exists(8 - i if mirrored else i), both)

    def send_y(c):
        when(iy > 0, c["yl"].start)
        when(iy < 3, c["yh"].start)

    def pack_x(s, c):
        vh_all = VH[...].reshape(1024, 128)
        vl_all = VL[...].reshape(1024, 128)
        XS[s] = dot_nt(e2, vh_all) + dot_nt(e2, vl_all)
        xp = dot_nt(jnp.concatenate([vh_all, vh_all], axis=1), CONST[...]) + dot_nt(vl_all, CONST[:, 0:128])
        Z[...] = xp.reshape(4, 16, 16, 128)
        c["xp"].start()
        c["xm"].start()

    def turn(value):
        return pltpu.roll(value.reshape(-1, 128), 64, 1).reshape(value.shape)

    def sums_for_other_half(s, c):
        ph, pl_ = split(PART[edge_block])
        for i in range(9):
            m = NMB[edge_block, 3 * i + 2]
            LHO[i, 0:16] = ph * m
            LHO[i, 16:32] = pl_ * m
        sums = dot_nt(LHO[...].reshape(288, 256), WT[edge_block, 0:128]).reshape(9, 32, 128)
        sums = sums[:, 0:16] + sums[:, 16:32]
        LSO[s] = sums[:, 0:8] + turn(sums[:, 8:16])
        neighbours(c, ("ro",), "start", False)

    def sums_for_own_half(s, c):
        for b in range(4):
            ph, pl_ = split(PART[b])
            for i in range(9):
                for pair in range(2):
                    m = NMB[b, 3 * i + pair]
                    LH[2 * i + pair, 0:16, b * 256 : (b + 1) * 256] = ph * m
                    LH[2 * i + pair, 16:32, b * 256 : (b + 1) * 256] = pl_ * m
        sums = None
        for b in range(4):
            lhs = LH[:, :, b * 256 : (b + 1) * 256].reshape(576, 256)
            term = dot_nt(lhs, WT[b, 0:128])
            sums = term if sums is None else sums + term
        sums = sums.reshape(18, 32, 128)
        LSA[s] = (sums[:, 0:16] + sums[:, 16:32]).reshape(9, 2, 16, 128)
        neighbours(c, ("rs",), "start", False)

    def stencil(s, c, first):
        c["xp"].wait_recv()
        c["xm"].wait_recv()
        xr = XR[s]
        xr_h = xr.astype(BF16).astype(F32)
        faces = jnp.concatenate([xr_h, xr - xr_h], axis=0).astype(BF16)
        Z[...] = Z[...] + (dot_tn(faces, edge_1) + dot_tn(faces, edge_2)).reshape(4, 16, 16, 128)
        c["z"].wait_recv()
        when(iy > 0, c["yh"].wait_recv)
        when(iy < 3, c["yl"].wait_recv)
        cur = s + 1
        scale = (1.0 if first else 2.0) / HALF

        def line(i, _):
            o = i // 16
            z = i % 16
            v0 = X[cur, o, z + 4, 8:24, :]
            acc = Z[o, z] + v0 * (POT[z] + (-1.5 * STENCIL[0] - CENTER))
            for k in range(1, 5):
                around = (X[cur, o, z + 4 - k, 8:24, :] + X[cur, o, z + 4 + k, 8:24, :]) + (
                    X[cur, o, z + 4, 8 - k : 24 - k, :] + X[cur, o, z + 4, 8 + k : 24 + k, :]
                )
                acc = acc + (-0.5 * STENCIL[k]) * around
            acc = scale * acc
            Z[o, z] = acc if first else acc - X[s, o, z + 4, 8:24, :]
            return 0

        lax.fori_loop(0, 64, line, 0, unroll=4)

    def scale_totals(s, c, first):
        neighbours(c, ("rs", "ro"), "wait_recv", True)
        total = LSA[s, SELF]
        other = None
        for slot in range(9):
            if slot != SELF:
                total = total + RS[s, slot]
            other = RO[s, slot] if other is None else other + RO[s, slot]
        theirs = lax.broadcasted_iota(I32, (8, 128), 1) // 64 == oz
        other = jnp.concatenate([jnp.where(theirs, other, 0.0), jnp.where(theirs, turn(other), 0.0)], axis=0)
        at_0 = jnp.where(zh == 1, 1.0, 0.0).astype(F32)
        scale = (1.0 if first else 2.0) / HALF
        scaled = scale * SC[...] * jnp.stack([total[0] + at_0 * other, total[1] + (1.0 - at_0) * other])
        CS[s] = scaled
        edge_pair = at_0 * scaled[0] + (1.0 - at_0) * scaled[1]
        CSO[s] = jnp.where(theirs, edge_pair[0:8], turn(edge_pair[8:16]))
        SSA[s, SELF] = scaled
        neighbours(c, ("bo", "bs"), "start", False)

    def take_same(s, c):
        neighbours(c, ("bs",), "wait_recv", True)
        sh, sl = split(SSA[s].reshape(288, 128))
        SHA[:, 0:128] = sh
        SHA[:, 128:256] = sl

    def take_other(s, c):
        neighbours(c, ("bo",), "wait_recv", True)
        packed = SSO[s]
        sh, sl = split(jnp.concatenate([packed, turn(packed)], axis=1).reshape(144, 128))
        SHO[:, 0:128] = sh
        SHO[:, 128:256] = sl

    def per_tile(b, with_other):
        r = dot_nn(SHA[...], WT[b])
        number = NIDX[b]
        pt = jnp.zeros((16, 256), F32)
        for i in range(9):
            for pair in range(2):
                k = 2 * i + pair
                pt = pt + jnp.where(number == 3 * i + pair, r[k * 16 : (k + 1) * 16], 0.0)
        if with_other:
            r = dot_nn(SHO[...], WT[b])
            for i in range(9):
                pt = pt + jnp.where(number == 3 * i + 2, r[i * 16 : (i + 1) * 16], 0.0)
        return pt

    def project(pt, b):
        mask = MKB[b, 0:64]
        results = []
        for o in range(4):
            r = PT[b, 0] * pt[o : o + 1]
            for p in range(1, 4):
                r = r + PT[b, p] * pt[p * 4 + o : p * 4 + o + 1]
            rh, rl = split(r)
            results.append(dot_nt(mask, rh) + dot_nt(mask, rl))
        return jnp.stack(results)

    def apply(s, b, with_other):
        y = Z[:, pl.ds(4 * b, 4)] + project(per_tile(b, with_other), b).reshape(4, 4, 16, 128)
        X[s + 2, :, pl.ds(4 + 4 * b, 4), 8:24, :] = y
        yh, yl = split(y)
        VH[:, pl.ds(4 * b, 4)] = yh
        VL[:, pl.ds(4 * b, 4)] = yl

    c = step_copies(0)
    take_own.wait()
    for v in values:
        v.wait_recv()
    c["z"].start()
    send_y(c)
    for v in parts:
        v.wait_recv()
    sums_for_other_half(0, c)
    sums_for_own_half(0, c)
    for v in cpl_y:
        v.wait_recv()
    group = 2 * (ix * 32)
    cpl_x = [
        start(set_copy(rows(group, 64), rows(group, 64), CP0 + 6 + j, dev((ix + j) % 4, iy, iz))) for j in (1, 3, 2)
    ]
    high, low = split(X[1, :, 4:20, 8:24, :])
    VH[...] = high
    VL[...] = low
    pack_x(0, c)
    for v in cpl_x:
        v.wait_recv()
    home2 = home_in[...]
    home = jnp.concatenate([home2[0:1], home2[1:2]], axis=1)
    home_row = 2 * lax.shift_right_logical(home, 6)
    rows256 = lax.broadcasted_iota(I32, (256, 256), 0)
    lane_hot = jnp.where(row64 == jnp.bitwise_and(home, 63), 1.0, 0.0).astype(F32)
    cb = CB[...]
    cb_1 = cb.astype(BF16)
    rest = cb - cb_1.astype(F32)
    cb_2 = rest.astype(BF16)
    cb_3 = (rest - cb_2.astype(F32)).astype(BF16)
    for r in range(2):
        pick = jnp.where(rows256 == home_row + r, 1.0, 0.0).astype(BF16)
        found = dot_tn(cb_1, pick) + dot_tn(cb_2, pick) + dot_tn(cb_3, pick)
        for p2 in range(2):
            line = jnp.sum(found[p2 * 64 : (p2 + 1) * 64] * lane_hot, axis=0, keepdims=True)
            p = 2 * r + p2
            for pair in range(2):
                SC[pair, p * 4 : (p + 1) * 4, :] = jnp.broadcast_to(line[:, pair * 128 : (pair + 1) * 128], (4, 128))

    scale_totals(0, c, True)

    up[0].wait_recv()
    on_up = start(set_copy(PT.at[below, half[0]], PT.at[below, half[0]], PF0 + 4, ring(1)))
    down[0].wait_recv()
    on_down = start(set_copy(PT.at[above, half[1]], PT.at[above, half[1]], PF0 + 5, ring(3)))
    take_pot.wait()
    for v in pots:
        v.wait_recv()
    stencil(0, c, True)
    def block_sums(b):
        vh = VH[:, pl.ds(4 * b, 4)].reshape(4, 64, 128)
        vl = VL[:, pl.ds(4 * b, 4)].reshape(4, 64, 128)
        tile_sums(vh, vl, b, PART, b)

    def rest_of_step(s, c):
        sums_for_own_half(s, c)
        send_y(c)
        pack_x(s, c)
        scale_totals(s, c, False)
        stencil(s, c, False)

    take_same(0, c)
    take_other(0, c)
    c = step_copies(1)
    for b, arrivals in ((q, ()), (below, (up[1],)), (above, (down[1],)), (across, (on_up, on_down))):
        for v in arrivals:
            v.wait_recv()
        apply(0, b, True)
        block_sums(b)
    c["z"].start()
    sums_for_other_half(1, c)
    rest_of_step(1, c)

    def step(s, _):
        before = step_copies(s - 1)
        c = step_copies(s)
        take_same(s - 1, before)
        take_other(s - 1, before)
        apply(s - 1, edge_block, True)
        c["z"].start()
        block_sums(edge_block)
        sums_for_other_half(s, c)

        def one(j, _):
            b = (edge_block + j) % 4
            apply(s - 1, b, False)
            block_sums(b)
            return 0

        lax.fori_loop(1, 4, one, 0)
        rest_of_step(s, c)
        return 0

    lax.fori_loop(2, STEPS, step, 0)

    last = STEPS - 1
    c = step_copies(last)
    outs_on = around(
        lambda block, o, n: Z.at[pl.ds(o, n), pl.ds(4 * block, 4)],
        lambda block, o, n: ZO.at[pl.ds(4 * block + o, n)],
        RLO,
        OU0,
    )
    outs = outs_on()
    take_same(last, c)
    take_other(last, c)
    finals = []
    for j in (2, 1, 3):
        b = (q + j) % 4
        PTS[pl.ds(b, 1)] = per_tile(b, True)[None]
        finals.append(start(set_copy(PTS.at[b], PTR.at[q], FT0 + j - 1, ring(j))))
    result = Z[:, pl.ds(4 * q, 4)] + project(per_tile(q, True), q).reshape(4, 4, 16, 128)
    out[pl.ds(4 * q, 4)] = result
    for v in outs:
        v.wait_recv()
    for index, j in ((1, 1), (2, 3), (0, 2)):
        finals[index].wait_recv()
        g = (q - j + 4) % 4
        out[pl.ds(4 * g, 4)] = ZO[pl.ds(4 * g, 4)] + project(PTR[g], q).reshape(4, 4, 16, 128)
    for v in sends:
        v.wait_send()

    def drain(s, _):
        c = step_copies(s)
        for name in ("xp", "xm", "z"):
            c[name].wait_send()
        when(iy > 0, c["yl"].wait_send)
        when(iy < 3, c["yh"].wait_send)
        neighbours(c, ("rs", "ro", "bs", "bo"), "wait_send", False)
        return 0

    lax.fori_loop(0, STEPS, drain, 0)


def per_device(orbitals, potential, tile_proj, tile_atom, tile_column, tile_count, atom_home, coupling):
    vmem = pl.BlockSpec(memory_space=pltpu.VMEM)
    hbm = pl.BlockSpec(memory_space=pltpu.HBM)
    smem = pl.BlockSpec(memory_space=pltpu.SMEM)

    def in_hbm(x):
        return pltpu.with_memory_space_constraint(x, pltpu.HBM)

    return pl.pallas_call(
        kernel,
        out_shape=jax.ShapeDtypeStruct((16, 4, 16, 128), F32),
        in_specs=[hbm] * 5 + [smem] + [hbm] * 3,
        out_specs=vmem,
        scratch_shapes=[
            pltpu.VMEM((6, 4, 24, 32, 128), F32),
            pltpu.VMEM((4, 16, 16, 128), F32),
            pltpu.VMEM((4, 16, 16, 128), BF16),
            pltpu.VMEM((4, 16, 16, 128), BF16),
            pltpu.VMEM((1024, 128), F32),
            pltpu.VMEM((4, 4, 128, 256), F32),
            pltpu.VMEM((16, 16, 128), F32),
            pltpu.VMEM((4, 8, 256), I32),
            pltpu.VMEM((4, 128, 256), BF16),
            pltpu.VMEM((4, 16, 256), I32),
            pltpu.VMEM((4, 27, 16, 256), BF16),
            pltpu.VMEM((4, 256, 256), BF16),
            pltpu.VMEM((18, 32, 1024), BF16),
            pltpu.VMEM((9, 32, 256), BF16),
            pltpu.VMEM((4, 9, 2, 16, 128), F32),
            pltpu.VMEM((4, 9, 8, 128), F32),
            pltpu.VMEM((4, 9, 2, 16, 128), F32),
            pltpu.VMEM((4, 9, 8, 128), F32),
            pltpu.VMEM((4, 2, 16, 128), F32),
            pltpu.VMEM((4, 8, 128), F32),
            pltpu.VMEM((4, 9, 2, 16, 128), F32),
            pltpu.VMEM((4, 9, 8, 128), F32),
            pltpu.VMEM((288, 256), BF16),
            pltpu.VMEM((144, 256), BF16),
            pltpu.VMEM((2, 16, 128), F32),
            pltpu.VMEM((4, 8, 1024), F32),
            pltpu.VMEM((4, 8, 1024), F32),
            pltpu.VMEM((256, 128), F32),
            pltpu.VMEM((128, 256), BF16),
            pltpu.VMEM((4, 16, 256), F32),
            pltpu.VMEM((4, 16, 256), F32),
            pltpu.VMEM((4, 16, 256), F32),
            pltpu.VMEM((4, 16, 256), F32),
            pltpu.VMEM((16, 4, 16, 128), F32),
            pltpu.VMEM((16, 4, 16, 128), F32),
            pltpu.VMEM((2, 2, 4, 16, 128), F32),
            pltpu.VMEM((2, 2, 4, 16, 128), F32),
            pltpu.VMEM((1, 256), I32),
            pltpu.VMEM((1, 256), I32),
            pltpu.VMEM((2, 128), I32),
            pltpu.VMEM((4, 64), F32),
            pltpu.VMEM((144, 128), F32),
            pltpu.SemaphoreType.DMA((NSET,)),
            pltpu.SemaphoreType.DMA((NSET,)),
            pltpu.SemaphoreType.DMA((STEPS, NSEM)),
            pltpu.SemaphoreType.DMA((STEPS, NSEM)),
            pltpu.SemaphoreType.DMA((9,)),
        ],
        compiler_params=pltpu.CompilerParams(
            collective_id=0, has_side_effects=True, vmem_limit_bytes=40000 * 1024
        ),
        name="chebyshev",
    )(
        in_hbm(orbitals),
        in_hbm(potential),
        in_hbm(tile_proj.reshape(1024, 128)),
        in_hbm(tile_atom.reshape(1, 256)),
        in_hbm(tile_column.reshape(1, 256)),
        tile_count,
        in_hbm(atom_home.reshape(64, 128)),
        in_hbm(coupling.T),
        in_hbm(jnp.asarray(stencil_constants())),
    )


def solution(mesh):
    return jax.shard_map(
        per_device,
        mesh=mesh,
        in_specs=(
            P(None, "gz", "gy", "gx"),
            P("gz", "gy", "gx"),
            P(("gx", "gy", "gz"), None, None),
            P(("gx", "gy", "gz")),
            P(("gx", "gy", "gz")),
            P(("gx", "gy", "gz")),
            P(),
            P(("gx", "gy", "gz"), None),
        ),
        out_specs=P(None, "gz", "gy", "gx"),
        check_vma=False,
    )
```
